32 devices in a mesh: dp: 8 (over z, x), tensor: 4 (over y, core).
Axes of the slice: x: 2, y: 2, z: 4, core: 2. Of those that a mesh axis runs over, the one named last changes fastest.
Arguments:
- inputs: bfloat16 [16, 1024, 768], P('dp', 'tensor'), may hold values from -6 to 6
- time_embed: bfloat16 [16, 768], P('dp'), may hold values from -6 to 6
- first_gain: bfloat16 [768], P('dp'), may hold values from 0.25 to 1.75
- first_shift: bfloat16 [768], P('dp'), may hold values from -3 to 3
- query_weight: bfloat16 [768, 768], P('dp', 'tensor'), may hold values from -0.21875 to 0.21875
- query_bias: bfloat16 [768], P(('tensor', 'dp')), may hold values from -3 to 3
- key_weight: bfloat16 [768, 768], P('dp', 'tensor'), may hold values from -0.21875 to 0.21875
- value_weight: bfloat16 [768, 768], P('dp', 'tensor'), may hold values from -0.21875 to 0.21875
- value_bias: bfloat16 [768], P(('tensor', 'dp')), may hold values from -3 to 3
- output_weight: bfloat16 [768, 768], P('tensor', 'dp'), may hold values from -4 to 4
- output_bias: bfloat16 [768], P('dp'), may hold values from -3 to 3
- second_gain: bfloat16 [768], P('dp'), may hold values from 0.25 to 1.75
- second_shift: bfloat16 [768], P('dp'), may hold values from -3 to 3
- hidden_weight: bfloat16 [768, 3072], P('dp', 'tensor'), may hold values from -0.21875 to 0.21875
- hidden_bias: bfloat16 [3072], P(('tensor', 'dp')), may hold values from -3 to 3
- down_weight: bfloat16 [3072, 768], P('tensor', 'dp'), may hold values from -0.625 to 0.625
- down_bias: bfloat16 [768], P('dp'), may hold values from -3 to 3
- cotangent: bfloat16 [16, 1024, 768], P('dp', 'tensor'), may hold values from -18 to 18
Outputs:
- block_output: bfloat16 [16, 1024, 768], P('dp', 'tensor')
- input_gradient: bfloat16 [16, 1024, 768], P('dp', 'tensor')
- embed_gradient: float32 [16, 768], P('dp')
- first_gain_gradient: float32 [768], P('dp')
- first_shift_gradient: float32 [768], P('dp')
- query_weight_gradient: float32 [768, 768], P('dp', 'tensor')
- query_bias_gradient: float32 [768], P(('tensor', 'dp'))
- key_weight_gradient: float32 [768, 768], P('dp', 'tensor')
- value_weight_gradient: float32 [768, 768], P('dp', 'tensor')
- value_bias_gradient: float32 [768], P(('tensor', 'dp'))
- output_weight_gradient: float32 [768, 768], P('tensor', 'dp')
- output_bias_gradient: float32 [768], P('dp')
- second_gain_gradient: float32 [768], P('dp')
- second_shift_gradient: float32 [768], P('dp')
- hidden_weight_gradient: float32 [768, 3072], P('dp', 'tensor')
- hidden_bias_gradient: float32 [3072], P(('tensor', 'dp'))
- down_weight_gradient: float32 [3072, 768], P('tensor', 'dp')
- down_bias_gradient: float32 [768], P('dp')
The draws below stay inside these ranges and needn't reach their ends.
All inputs are finite; a program needn't handle non-finite values.
Results may differ from the reference program's by a relative error of at most 0.015.
Values may be sent and summed in bfloat16 or wider, within the bound.
No kernel may reach another device: no remote copies, remote signals or barrier semaphores. Data moves between devices by JAX's collectives and lax.ppermute only.
A program may use at most 128 MiB of HBM per device.

```python
import jax
import jax.numpy as jnp
from jax import lax

D = 768
HEADS = 12
HD = 64
FF = 3072
SEQ = 1024
SEQS = 16


def draw_cotangent(key, part):
    base_key = jax.random.fold_in(key, 11)
    ramp = 3.0 ** (jnp.arange(SEQS, dtype=jnp.float32) / max(SEQS - 1, 1))
    values = jnp.clip(jax.random.normal(base_key, (SEQS, SEQ, D), jnp.float32), -6.0, 6.0)
    values = values * ramp[:, None, None]
    return values.astype(jnp.bfloat16)


def steps_of(stream_key, extent, cuts, least, top_value):
    def one(axis_at, shards_of):
        draws = jax.random.uniform(jax.random.fold_in(jax.random.fold_in(stream_key, 6), axis_at), (shards_of,), jnp.float32, least / len(cuts), top_value / len(cuts))
        return jnp.repeat(jnp.exp(draws), extent[axis_at] // shards_of).reshape((-1,) + (1,) * (len(extent) - axis_at - 1))

    loudness = one(*cuts[0])
    for cut in cuts[1:]:
        loudness = loudness * one(*cut)
    return loudness


def bell_draw(own_key, dims, scale, reach, shards=(), kind=jnp.bfloat16):
    values = scale * jax.random.normal(own_key, dims, jnp.float32)
    if shards:
        values = values * steps_of(own_key, dims, shards, -0.22, 0.18)
    return jnp.clip(values, -reach, reach).astype(kind)


def setup_inputs(seed: int = 0) -> dict:
    key_list = jax.random.split(jax.random.key(seed), 19)
    inputs = bell_draw(key_list[0], (SEQS, SEQ, D), 1.0, 6.0, ((0, 8), (1, 4)))
    time_embed = bell_draw(key_list[1], (SEQS, D), 1.0, 6.0, ((0, 8),))
    first_gain = jnp.clip(1.0 + 0.15 * jax.random.normal(key_list[2], (D,), jnp.float32), 0.25, 1.75).astype(jnp.bfloat16)
    first_shift = bell_draw(key_list[3], (D,), 0.5, 3.0, ((0, 8),))
    query_weight = bell_draw(key_list[4], (D, D), D ** -0.5, 0.21875, ((0, 8), (1, 4)))
    query_bias = bell_draw(key_list[5], (D,), 0.5, 3.0, ((0, 32),))
    key_weight = bell_draw(key_list[6], (D, D), D ** -0.5, 0.21875, ((0, 8), (1, 4)))
    value_weight = bell_draw(key_list[7], (D, D), D ** -0.5, 0.21875, ((0, 8), (1, 4)))
    value_bias = bell_draw(key_list[8], (D,), 0.5, 3.0, ((0, 32),))
    output_weight = bell_draw(key_list[9], (D, D), 2 ** -0.5, 4.0, ((0, 4), (1, 8)))
    output_bias = bell_draw(key_list[10], (D,), 0.5, 3.0, ((0, 8),))
    second_gain = jnp.clip(1.0 + 0.15 * jax.random.normal(key_list[11], (D,), jnp.float32), 0.25, 1.75).astype(jnp.bfloat16)
    second_shift = bell_draw(key_list[12], (D,), 0.5, 3.0, ((0, 8),))
    hidden_weight = bell_draw(key_list[13], (D, FF), D ** -0.5, 0.21875, ((0, 8), (1, 4)))
    hidden_bias = bell_draw(key_list[14], (FF,), 0.5, 3.0, ((0, 32),))
    down_weight = bell_draw(key_list[15], (FF, D), (FF // 32) ** -0.5, 0.625, ((0, 4), (1, 8)))
    down_bias = bell_draw(key_list[16], (D,), 0.5, 3.0, ((0, 8),))
    cotangent = draw_cotangent(jax.random.fold_in(key_list[18], 71), 0)
    return dict(inputs=inputs, time_embed=time_embed, first_gain=first_gain, first_shift=first_shift, query_weight=query_weight, query_bias=query_bias, key_weight=key_weight, value_weight=value_weight, value_bias=value_bias, output_weight=output_weight, output_bias=output_bias, second_gain=second_gain, second_shift=second_shift, hidden_weight=hidden_weight, hidden_bias=hidden_bias, down_weight=down_weight, down_bias=down_bias, cotangent=cotangent)


@jax.custom_vjp
def low(v):
    return lax.optimization_barrier(v.astype(jnp.bfloat16)).astype(jnp.float32)

@jax.custom_vjp
def low_back(v):
    return v

def low_keep(v):
    return (low(v), None)

def low_pass(kept, grad):
    return (grad,)

def back_keep(v):
    return (v, None)

def back_low(kept, grad):
    return (low(grad),)
low.defvjp(low_keep, low_pass)
low_back.defvjp(back_keep, back_low)
EPSILON = 1e-05
SCALE = 0.125
HIGHEST = lax.Precision.HIGHEST

def layer_norm(values, gain, shift):
    center = values - lax.optimization_barrier(jnp.mean(values, axis=-1, keepdims=True))
    spread = lax.optimization_barrier(jnp.mean(center * center, axis=-1, keepdims=True))
    return center * lax.rsqrt(spread + EPSILON) * gain + shift

def project(values, matrix):
    return jnp.einsum('gnd,de->gne', values, matrix, precision=HIGHEST)

def attend(packed):
    queries, key_rows, value_rows = packed
    scores = low_back(SCALE * jnp.einsum('qhd,khd->hqk', queries, key_rows, precision=HIGHEST))
    expon = jnp.exp(scores - lax.optimization_barrier(jnp.max(scores, axis=-1, keepdims=True)))
    probs = low(expon / lax.optimization_barrier(jnp.sum(expon, axis=-1, keepdims=True)))
    return jnp.einsum('hqk,khd->qhd', probs, value_rows, precision=HIGHEST)

def forward(block_in, embed_in, params):
    first_gain, first_shift, query_weight, query_bias, key_weight, value_weight, value_bias, output_weight, output_bias, second_gain, second_shift, hidden_weight, hidden_bias, down_weight, down_bias = params
    start = block_in + embed_in[:, None, :]
    normed = low(layer_norm(start, first_gain, first_shift))
    queries = low(low_back(project(normed, query_weight) + query_bias))
    key_rows = low(low_back(project(normed, key_weight)))
    value_rows = low(low_back(project(normed, value_weight) + value_bias))
    group_size, length, width = block_in.shape
    split_shape = (group_size, length, HEADS, HD)
    mixed = lax.map(jax.checkpoint(attend), (queries.reshape(split_shape), key_rows.reshape(split_shape), value_rows.reshape(split_shape)))
    mixed = low(low_back(mixed.reshape(group_size, length, width)))
    middle = start + low_back(project(mixed, output_weight)) + output_bias
    normed_second = low(layer_norm(middle, second_gain, second_shift))
    preact = low_back(project(normed_second, hidden_weight) + hidden_bias)
    activated = low(jax.nn.gelu(preact, approximate=False))
    return middle + low_back(project(activated, down_weight)) + down_bias

def reference(inputs, time_embed, first_gain, first_shift, query_weight, query_bias, key_weight, value_weight, value_bias, output_weight, output_bias, second_gain, second_shift, hidden_weight, hidden_bias, down_weight, down_bias, cotangent):
    params = tuple((entry.astype(jnp.float32) for entry in (first_gain, first_shift, query_weight, query_bias, key_weight, value_weight, value_bias, output_weight, output_bias, second_gain, second_shift, hidden_weight, hidden_bias, down_weight, down_bias)))
    group_size = 4 if SEQS % 4 == 0 else 1
    group_count = SEQS // group_size
    block_all = inputs.astype(jnp.float32).reshape(group_count, group_size, SEQ, D)
    embed_all = time_embed.astype(jnp.float32).reshape(group_count, group_size, D)
    cot_all = cotangent.astype(jnp.float32).reshape(group_count, group_size, SEQ, D)

    def step(totals, packed):
        block_in, embed_in, cot_in = packed
        result, pull = jax.vjp(forward, block_in, embed_in, params)
        block_grad, embed_grad, param_grad = pull(cot_in)
        totals = jax.tree.map(jnp.add, totals, param_grad)
        return (totals, (result.astype(jnp.bfloat16), block_grad.astype(jnp.bfloat16), embed_grad))
    zeros = jax.tree.map(jnp.zeros_like, params)
    totals, (outputs, block_grads, embed_grads) = lax.scan(step, zeros, (block_all, embed_all, cot_all))
    return (outputs.reshape(SEQS, SEQ, D), block_grads.reshape(SEQS, SEQ, D), embed_grads.reshape(SEQS, D), totals[0], totals[1], totals[2], totals[3], totals[4], totals[5], totals[6], totals[7], totals[8], totals[9], totals[10], totals[11], totals[12], totals[13], totals[14])
```

```python
import functools

import jax
import jax.numpy as jnp
from jax import lax
from jax.experimental import pallas as pl
from jax.experimental.pallas import tpu as pltpu
from jax.sharding import Mesh
from jax.sharding import PartitionSpec as P

HD = 64
EPSILON = 1e-05
SCALE = 0.125
BF = jnp.bfloat16
F32 = jnp.float32
ZS, XS = 4, 2
KINDS = 8

NN = (((1,), (0,)), ((), ()))
NT = (((1,), (1,)), ((), ()))


def dot(left, right, dims=NN):
    return lax.dot_general(left, right, dims, preferred_element_type=F32)


def call(body, grid, ins, outs, scratch=(), flops=0, moved=0, trans=0, vmem=56):
    return pl.pallas_call(
        body,
        grid=grid,
        in_specs=[s for s in ins],
        out_specs=[s for _, s in outs],
        out_shape=[o for o, _ in outs],
        scratch_shapes=list(scratch),
        compiler_params=pltpu.CompilerParams(vmem_limit_bytes=vmem << 20),
        cost_estimate=pl.CostEstimate(flops=int(flops), bytes_accessed=int(moved), transcendentals=int(trans)),
    )


def whole(shape, n=1):
    zeros = (0,) * len(shape)
    return pl.BlockSpec(shape, lambda *_: zeros, pipeline_mode=pl.Buffered(1))


def kept(shape):
    zeros = (0,) * len(shape)
    return pl.BlockSpec(shape, lambda *_: zeros)


def scalar():
    return pl.BlockSpec(memory_space=pltpu.SMEM)


def sds(shape, dtype):
    return jax.ShapeDtypeStruct(shape, dtype)


def assemble(store, own, oth, x, rows, first=0):
    for z in range(ZS):
        store(pl.multiple_of((2 * z + x) * rows, 32), own[z, first : first + rows, :])
        store(pl.multiple_of((2 * z + 1 - x) * rows, 32), oth[z, first : first + rows, :])


def normalize(values):
    center = values - jnp.mean(values, axis=-1, keepdims=True)
    spread = jnp.mean(center * center, axis=-1, keepdims=True)
    rate = lax.rsqrt(spread + EPSILON)
    return center * rate, rate


def project_body(x_ref, start_ref, te_ref, vec_ref, bias_ref, own_ref, oth_ref, w_ref, qkv_ref, *norm_refs, rows, first):
    @pl.when(pl.program_id(0) == 0)
    def _():
        def store(at, value):
            w_ref[pl.ds(at, rows), :] = value

        assemble(store, own_ref, oth_ref, x_ref[0], rows)

    if first:
        normed_ref, normed_t_ref = norm_refs
        xhat, _ = normalize(start_ref[...].astype(F32) + te_ref[...].astype(F32))
        normed = (xhat * vec_ref[0:1, :] + vec_ref[1:2, :]).astype(BF)
        normed_ref[...] = normed
        normed_t_ref[...] = normed.T
    else:
        normed = start_ref[...]
    made = dot(normed, w_ref[:, :640])[:, :576] + bias_ref[...]
    made = made.astype(BF)
    for j in range(9):
        piece = made[:, 64 * j : 64 * j + 64]
        qkv_ref[j] = piece * BF(SCALE) if j < 3 else piece


def attend_body(q_ref, k_ref, v_ref, e_ref, inv_ref, mixed_ref, wide_ref):
    scores = dot(k_ref[0], q_ref[0], NT)
    expon = jnp.exp(scores - jnp.max(scores, axis=0, keepdims=True))
    inverse = 1.0 / jnp.sum(expon, axis=0, keepdims=True)
    low = expon.astype(BF)
    e_ref[0] = low
    inv_ref[0] = inverse
    wide = dot(v_ref[0].T, low) * inverse
    mixed_ref[0] = wide.astype(BF)
    wide_ref[0] = wide


def attend_back_body(q_ref, k_ref, v_ref, e_ref, inv_ref, mixed_ref, gm_ref, dq_ref, dk_ref, dv_ref, k_acc, v_acc):
    step, last = pl.program_id(1), pl.num_programs(1) - 1
    inverse = inv_ref[0]
    low = (gm_ref[0].astype(F32) * inverse).astype(BF)
    inner = jnp.sum(low.astype(F32) * mixed_ref[0], axis=0, keepdims=True)
    expon = e_ref[0]
    grads = dot(v_ref[0], low)
    grad_scores = (expon.astype(F32) * (grads - inner)).astype(BF)
    dv = dot(expon, low, NT)
    dk = dot(grad_scores, q_ref[0])

    @pl.when(step == 0)
    def _():
        v_acc[...] = dv
        k_acc[...] = dk

    @pl.when(step > 0)
    def _():
        v_acc[...] += dv
        k_acc[...] += dk

    dq_ref[0] = (dot(k_ref[0].T, grad_scores) * SCALE).T.astype(BF)

    @pl.when(step == last)
    def _():
        dk_ref[0] = k_acc[...].astype(BF)
        dv_ref[0] = v_acc[...].astype(BF)


def outproj_body(m0_ref, m1_ref, w0_ref, w1_ref, out_ref, wo_ref):
    @pl.when(pl.program_id(0) == 0)
    def _():
        wo_ref[...] = jnp.concatenate([w0_ref[:, 576:], w1_ref[:, 576:]], axis=1)

    mixed = jnp.concatenate([m0_ref[...], m1_ref[...]], axis=0).T
    out_ref[...] = dot(mixed, wo_ref[...], NT).astype(BF)


def mlp_body(
    x_ref, start_ref, te_ref, a0_ref, a1_ref, cot_ref, vec_ref, hb_ref,
    h_oo, h_ox, h_yo, h_yx, d_oo, d_ox, d_yo, d_yx,
    mid_ref, ff_ref, gs_ref, hbg_ref, gh_oo, gh_ox, gh_yo, gh_yx, gd_oo, gd_ox, gd_yo, gd_yx,
    wh, wd, acc_h, acc_d, *, rows,
):
    step, last = pl.program_id(0), pl.num_programs(0) - 1
    x = x_ref[0]

    @pl.when(step == 0)
    def _():
        for y, (own, oth) in enumerate(((h_oo, h_ox), (h_yo, h_yx))):
            assemble(functools.partial(put, wh, y, rows), own, oth, x, rows)
        for y, (own, oth) in enumerate(((d_oo, d_ox), (d_yo, d_yx))):
            assemble(functools.partial(put, wd, y, rows), own, oth, x, rows)
        acc_h[...] = jnp.zeros_like(acc_h)
        acc_d[...] = jnp.zeros_like(acc_d)
        hbg_ref[...] = jnp.zeros_like(hbg_ref)

    middle = (
        start_ref[...].astype(F32)
        + te_ref[...].astype(F32)
        + (a0_ref[...].astype(F32) + a1_ref[...].astype(F32))
        + vec_ref[2:3, :]
    )
    mid_ref[...] = middle
    xhat, _ = normalize(middle)
    normed = (xhat * vec_ref[3:4, :] + vec_ref[4:5, :]).astype(BF)
    normed_t = normed.T
    cot = cot_ref[...]
    cot_t = cot.T
    ff = gs = None
    for y in range(2):
        pre = dot(normed, wh[y]) + hb_ref[y : y + 1, :]
        below = 0.5 + 0.5 * lax.erf(pre * 0.7071067811865476)
        act = (pre * below).astype(BF)
        slope = below + pre * (jnp.exp(-0.5 * pre * pre) * 0.3989422804014327)
        grad = (dot(cot, wd[y]) * slope).astype(BF)
        ff_y = dot(act, wd[y], NT)
        gs_y = dot(grad, wh[y], NT)
        ff = ff_y if ff is None else ff + ff_y
        gs = gs_y if gs is None else gs + gs_y
        acc_h[y] += dot(normed_t, grad)
        acc_d[y] += dot(cot_t, act)
        hbg_ref[y : y + 1, :] += jnp.sum(grad.astype(F32), axis=0, keepdims=True)
    ff_ref[...] = ff.astype(BF)
    gs_ref[...] = gs.astype(BF)

    @pl.when(step == last)
    def _():
        for acc, sets in ((acc_h, ((gh_oo, gh_ox), (gh_yo, gh_yx))), (acc_d, ((gd_oo, gd_ox), (gd_yo, gd_yx)))):
            for y, (own, oth) in enumerate(sets):
                for z in range(ZS):
                    at = pl.multiple_of((2 * z + x) * rows, 32)
                    own[z] = acc[y, pl.ds(at, rows), :].astype(BF)
                    at = pl.multiple_of((2 * z + 1 - x) * rows, 32)
                    oth[z] = acc[y, pl.ds(at, rows), :].astype(BF)


def put(ref, y, rows, at, value):
    ref[y, pl.ds(at, rows), :] = value


def second_back_body(mid_ref, g0_ref, g1_ref, cot_ref, vec_ref, w0_ref, w1_ref, m0_ref, m1_ref, gm_ref, x0_ref, x1_ref, wo0_ref, wo1_ref, sum_ref, wo_ref, acc):
    step, last = pl.program_id(0), pl.num_programs(0) - 1

    @pl.when(step == 0)
    def _():
        wo_ref[...] = jnp.concatenate([w0_ref[:, 576:], w1_ref[:, 576:]], axis=1)
        acc[...] = jnp.zeros_like(acc)
        sum_ref[...] = jnp.zeros_like(sum_ref)

    xhat, rate = normalize(mid_ref[...])
    second = g0_ref[...].astype(F32) + g1_ref[...].astype(F32)
    cot = cot_ref[...].astype(F32)
    scaled = second * vec_ref[3:4, :]
    inner = jnp.mean(scaled * xhat, axis=-1, keepdims=True)
    grad = cot + rate * (scaled - jnp.mean(scaled, axis=-1, keepdims=True) - xhat * inner)
    gm_ref[...] = grad
    sum_ref[0:1, :] += jnp.sum(second * xhat, axis=0, keepdims=True)
    sum_ref[1:2, :] += jnp.sum(second, axis=0, keepdims=True)
    sum_ref[2:3, :] += jnp.sum(grad, axis=0, keepdims=True)
    sum_ref[3:4, :] += jnp.sum(cot, axis=0, keepdims=True)
    low = grad.astype(BF)
    back = dot(low, wo_ref[...]).astype(BF).T
    x0_ref[...] = back[:192]
    x1_ref[...] = back[192:]
    mixed = jnp.concatenate([m0_ref[...], m1_ref[...]], axis=0)
    acc[...] += dot(low.T, mixed, NT)

    @pl.when(step == last)
    def _():
        wo0_ref[...] = acc[:, :192].astype(BF)
        wo1_ref[...] = acc[:, 192:].astype(BF)


def project_back_body(x_ref, q_ref, k_ref, v_ref, nt_ref, w_ref, wo_ref, *refs, rows, more):
    refs = list(refs)
    prev_ref = refs.pop(0) if more else None
    own_ref, oth_ref, first_ref, sum_ref, acc = refs
    step, last = pl.program_id(0), pl.num_programs(0) - 1
    x = x_ref[0]
    grads = jnp.concatenate([r[h] for r in (q_ref, k_ref, v_ref) for h in range(3)], axis=1)
    made = dot(nt_ref[...], grads)
    total = jnp.sum(grads.astype(F32), axis=0, keepdims=True)

    @pl.when(step == 0)
    def _():
        acc[...] = made
        sum_ref[...] = total

    @pl.when(step > 0)
    def _():
        acc[...] += made
        sum_ref[...] += total

    back = dot(grads, w_ref[:, :576], NT)
    if more:
        back = back + prev_ref[...]
    first_ref[...] = back.astype(first_ref.dtype)

    @pl.when(step == last)
    def _():
        for z in range(ZS):
            for ref, side in ((own_ref, x), (oth_ref, 1 - x)):
                at = pl.multiple_of((2 * z + side) * rows, 32)
                ref[z] = jnp.concatenate(
                    [acc[pl.ds(at, rows), :].astype(BF), wo_ref[pl.ds(at, rows), :]], axis=1
                )


def first_back_body(start_ref, te_ref, vec_ref, g0_ref, g1_ref, gm_ref, out_ref, sum_ref):
    @pl.when(pl.program_id(0) == 0)
    def _():
        sum_ref[...] = jnp.zeros_like(sum_ref)

    xhat, rate = normalize(start_ref[...].astype(F32) + te_ref[...].astype(F32))
    first = g0_ref[...].astype(F32) + g1_ref[...].astype(F32)
    scaled = first * vec_ref[0:1, :]
    inner = jnp.mean(scaled * xhat, axis=-1, keepdims=True)
    grad = gm_ref[...] + rate * (scaled - jnp.mean(scaled, axis=-1, keepdims=True) - xhat * inner)
    out_ref[...] = grad.astype(BF)
    sum_ref[0:1, :] += jnp.sum(first * xhat, axis=0, keepdims=True)
    sum_ref[1:2, :] += jnp.sum(first, axis=0, keepdims=True)
    sum_ref[2:3, :] += jnp.sum(grad, axis=0, keepdims=True)


def output_body(mid_ref, f0_ref, f1_ref, vec_ref, out_ref):
    out_ref[...] = (
        mid_ref[...] + (f0_ref[...].astype(F32) + f1_ref[...].astype(F32)) + vec_ref[5:6, :]
    ).astype(BF)


def swap(size):
    return [(i, size - 1 - i) for i in range(size)]


def to_y(values):
    return lax.ppermute(values, "y", swap(2))


def to_x(values):
    return lax.ppermute(values, "b", swap(2))


def to_core(values):
    return lax.ppermute(values, "c", swap(2))


def spread_z(values):
    return lax.all_to_all(values, "a", 0, 0, tiled=True)


def after(value, *others):
    return lax.optimization_barrier((value, *others))[0]


def body(
    fast,
    inputs,
    time_embed,
    first_gain,
    first_shift,
    query_weight,
    query_bias,
    key_weight,
    value_weight,
    value_bias,
    output_weight,
    output_bias,
    second_gain,
    second_shift,
    hidden_weight,
    hidden_bias,
    down_weight,
    down_bias,
    cotangent,
):
    _, block, width = inputs.shape
    shard = query_weight.shape[0]
    rows = width // (ZS * XS)
    seq = 4 * block
    tile = block
    tiles = seq // tile
    hidden = hidden_weight.shape[1]
    yi = lax.axis_index("y")
    xi = lax.axis_index("b") if fast else jnp.int32(0)
    x_arr = xi.astype(jnp.int32)[None]

    def tokens(values):
        mine = lax.dynamic_index_in_dim(values, yi, 0, keepdims=False)
        sent = lax.dynamic_index_in_dim(values, 1 - yi, 0, keepdims=False)
        pair = jnp.concatenate([mine, to_y(sent)], axis=0)
        return jnp.concatenate([pair, to_core(pair)], axis=0)

    start = tokens(inputs)
    te = lax.dynamic_index_in_dim(time_embed, yi, 0, keepdims=True)

    small = jnp.stack(
        [first_gain, first_shift, output_bias, second_gain, second_shift, down_bias, hidden_bias,
         jnp.pad(jnp.concatenate([query_bias, value_bias]), (0, shard - 2 * query_bias.shape[0]))]
    )
    small = jnp.pad(small, ((0, 0), (0, width - shard)))
    attn_pack = jnp.concatenate(
        [jnp.concatenate([query_weight, key_weight, value_weight, output_weight.T], axis=1), small], axis=0
    )
    h_pack, d_pack = hidden_weight, down_weight.T

    def vectors(own, oth):
        both = jnp.stack([own, oth], axis=1)
        both = jnp.where(xi == 0, both, both[:, ::-1])
        return both.reshape(ZS * XS, KINDS, -1)

    if fast:
        def copies(values):
            return jnp.broadcast_to(values[None], (ZS, *values.shape))

        attn_oo = spread_z(copies(attn_pack))
        h_pack, d_pack = lax.optimization_barrier((h_pack, d_pack, attn_oo))[:2]
        attn_ox = to_x(attn_oo)
        attn_yo = to_y(attn_oo)
        attn_yx = to_y(attn_ox)
        mlp_z = spread_z(copies(jnp.concatenate([h_pack, d_pack], axis=0)))
        h_oo, d_oo = mlp_z[:, :rows], mlp_z[:, rows:]
        h_ox = to_x(h_oo)
        h_yo = to_y(h_oo)
        h_yx = to_y(h_ox)
        d_yo = to_y(d_oo)
        d_ox = to_x(d_oo)
        d_yx = to_x(d_yo)
        vec_o = vectors(attn_oo[:, rows:, :rows], attn_ox[:, rows:, :rows])
        vec_y = vectors(attn_yo[:, rows:, :rows], attn_yx[:, rows:, :rows])
        bias_of = vec_o.shape[-1] // 4
    else:
        def natural(values):
            full = lax.all_gather(values, ("a", "b"), axis=0, tiled=True)
            full = full.reshape(ZS, XS, rows, width)
            return full[:, 0], full[:, 1]

        gathered = lax.all_gather(attn_pack, ("a", "b"), axis=0, tiled=False)
        matrix = gathered[:, :shard].reshape(ZS, XS, rows, width)
        attn_oo, attn_ox = matrix[:, 0], matrix[:, 1]
        attn_yo, attn_yx = to_y(attn_oo), to_y(attn_ox)
        h_oo, h_ox = natural(h_pack)
        d_oo, d_ox = natural(d_pack)
        h_yo, h_yx, d_yo, d_yx = to_y(h_oo), to_y(h_ox), to_y(d_oo), to_y(d_ox)
        vec_o = gathered[:, shard:, :shard]
        vec_y = to_y(vec_o)
        bias_of = shard // 4

    def flat(values):
        return values.astype(F32).transpose(1, 0, 2).reshape(KINDS, -1)

    def qkv_bias(values):
        part = values[:, 7, : 2 * bias_of].astype(F32)
        q_part, v_part = part[:, :bias_of].reshape(1, -1), part[:, bias_of:].reshape(1, -1)
        return jnp.concatenate([q_part, jnp.zeros_like(q_part), v_part], axis=1)

    vec = flat(vec_o)
    bias_o, bias_y = qkv_bias(vec_o), qkv_bias(vec_y)
    hb = jnp.concatenate([vec[6:7], flat(vec_y)[6:7]], axis=0)

    cot = tokens(cotangent)

    by_tile = pl.BlockSpec((tile, width), lambda i: (i, 0))
    by_mate = pl.BlockSpec((tile, width), lambda i: ((i + tiles // 2) % tiles, 0))
    row = kept((1, width))
    vecs = kept((KINDS, width))
    square = whole((width, width))
    part_rows = attn_oo.shape[1]
    heads9 = pl.BlockSpec((9, tile, HD), lambda i: (0, i, 0))

    def project(first, source, bias, own, oth):
        outs = [
            (sds((width, width), BF), kept((width, width))),
            (sds((9, seq, HD), BF), heads9),
        ]
        if first:
            outs += [
                (sds((seq, width), BF), by_tile),
                (sds((width, seq), BF), pl.BlockSpec((width, tile), lambda i: (0, i))),
            ]
        return call(
            functools.partial(project_body, rows=rows, first=first),
            (tiles,),
            [scalar(), by_tile, row, vecs, kept((1, 576)), whole((ZS, part_rows, width)), whole((ZS, part_rows, width))],
            outs,
            flops=2 * seq * width * 576,
            moved=8e6,
        )(x_arr, source, te, vec, bias, own, oth)

    chunks = tiles
    q_spec = pl.BlockSpec((1, tile, HD), lambda h, i: (h, i, 0))
    k_spec = pl.BlockSpec((1, seq, HD), lambda h, i: (3 + h, 0, 0))
    v_spec = pl.BlockSpec((1, seq, HD), lambda h, i: (6 + h, 0, 0))
    e_spec = pl.BlockSpec((1, seq, tile), lambda h, i: (h, 0, i))
    inv_spec = pl.BlockSpec((1, 1, tile), lambda h, i: (h, 0, i))
    t_spec = pl.BlockSpec((1, HD, tile), lambda h, i: (h, 0, i))

    def attend(qkv):
        return call(
            attend_body,
            (3, chunks),
            [q_spec, k_spec, v_spec],
            [
                (sds((3, seq, seq), BF), e_spec),
                (sds((3, 1, seq), F32), inv_spec),
                (sds((3, HD, seq), BF), t_spec),
                (sds((3, HD, seq), F32), t_spec),
            ],
            flops=3 * 16 * seq * seq * HD,
            moved=8e6,
            trans=3 * seq * seq,
        )(qkv, qkv, qkv)

    def attend_back(qkv, expon, inverse, mixed, grad_mixed):
        full = pl.BlockSpec((1, seq, HD), lambda h, i: (h, 0, 0))
        return call(
            attend_back_body,
            (3, chunks),
            [q_spec, k_spec, v_spec, e_spec, inv_spec, t_spec, t_spec],
            [(sds((3, seq, HD), BF), q_spec), (sds((3, seq, HD), BF), full), (sds((3, seq, HD), BF), full)],
            scratch=[pltpu.VMEM((seq, HD), F32), pltpu.VMEM((seq, HD), F32)],
            flops=3 * 40 * seq * seq * HD,
            moved=9e6,
        )(qkv, qkv, qkv, expon, inverse, mixed, grad_mixed)

    w_o, qkv_o, normed, normed_t = project(True, start, bias_o, attn_oo, attn_ox)
    exp_o, inv_o, mixed_o, wide_o = attend(qkv_o)
    w_y, qkv_y = project(False, normed, bias_y, attn_yo, attn_yx)
    exp_y, inv_y, mixed_y, wide_y = attend(qkv_y)

    half_t = pl.BlockSpec((3 * HD, tile), lambda i: (0, i))
    flat_o, flat_y = mixed_o.reshape(3 * HD, seq), mixed_y.reshape(3 * HD, seq)
    (attended,) = call(
        outproj_body,
        (tiles,),
        [half_t, half_t, square, square],
        [(sds((seq, width), BF), by_tile)],
        scratch=[pltpu.VMEM((width, 6 * HD), BF)],
        flops=2 * seq * width * 384,
        moved=6e6,
    )(flat_o, flat_y, w_o, w_y)
    attended_mate = to_core(attended)

    part = (ZS, rows, hidden)
    middle, ff, gs, hb_sum, gh_oo, gh_ox, gh_yo, gh_yx, gd_oo, gd_ox, gd_yo, gd_yx = call(
        functools.partial(mlp_body, rows=rows),
        (tiles,),
        [scalar(), by_tile, row, by_tile, by_mate, by_tile, vecs, kept((2, hidden))] + [whole(part)] * 8,
        [
            (sds((seq, width), F32), by_tile),
            (sds((seq, width), BF), by_tile),
            (sds((seq, width), BF), by_tile),
            (sds((2, hidden), F32), kept((2, hidden))),
        ]
        + [(sds(part, BF), kept(part))] * 8,
        scratch=[
            pltpu.VMEM((2, width, hidden), BF),
            pltpu.VMEM((2, width, hidden), BF),
            pltpu.VMEM((2, width, hidden), F32),
            pltpu.VMEM((2, width, hidden), F32),
        ],
        flops=12 * seq * width * hidden * 2,
        moved=24e6,
        trans=seq * hidden * 4,
    )(x_arr, start, te, attended, attended_mate, cot, vec, hb, h_oo, h_ox, h_yo, h_yx, d_oo, d_ox, d_yo, d_yx)
    gs_mate = to_core(gs)

    grad_middle, gx_o, gx_y, wo_o, wo_y, second_sums = call(
        second_back_body,
        (tiles,),
        [by_tile, by_tile, by_mate, by_tile, vecs, square, square, half_t, half_t],
        [
            (sds((seq, width), F32), by_tile),
            (sds((3 * HD, seq), BF), half_t),
            (sds((3 * HD, seq), BF), half_t),
            (sds((width, 3 * HD), BF), kept((width, 3 * HD))),
            (sds((width, 3 * HD), BF), kept((width, 3 * HD))),
            (sds((KINDS, width), F32), kept((KINDS, width))),
        ],
        scratch=[pltpu.VMEM((width, 6 * HD), BF), pltpu.VMEM((width, 6 * HD), F32)],
        flops=4 * seq * width * 384,
        moved=16e6,
    )(middle, gs, gs_mate, cot, vec, w_o, w_y, flat_o, flat_y)

    heads = pl.BlockSpec((3, tile, HD), lambda i: (0, i, 0))
    attn_part = (ZS, rows, width)

    def project_back(grads, weights, wo, prev):
        more = prev is not None
        return call(
            functools.partial(project_back_body, rows=rows, more=more),
            (tiles,),
            [scalar(), heads, heads, heads, pl.BlockSpec((width, tile), lambda i: (0, i)), square, whole((width, 3 * HD))]
            + ([by_tile] if more else []),
            [
                (sds(attn_part, BF), kept(attn_part)),
                (sds(attn_part, BF), kept(attn_part)),
                (sds((seq, width), BF if more else F32), by_tile),
                (sds((1, 576), F32), kept((1, 576))),
            ],
            scratch=[pltpu.VMEM((width, 576), F32)],
            flops=4 * seq * width * 576,
            moved=10e6,
        )(x_arr, *grads, normed_t, weights, wo, *((prev,) if more else ()))

    grads_y = attend_back(qkv_y, exp_y, inv_y, wide_y, gx_y.reshape(3, HD, seq))
    ga_yo, ga_yx, first_part, qkv_sum_y = project_back(grads_y, w_y, wo_y, None)
    grads_o = attend_back(qkv_o, exp_o, inv_o, wide_o, gx_o.reshape(3, HD, seq))
    ga_oo, ga_ox, first, qkv_sum_o = project_back(grads_o, w_o, wo_o, first_part)
    first_mate = to_core(first)

    input_grad, first_sums = call(
        first_back_body,
        (tiles,),
        [by_tile, row, vecs, by_tile, by_mate, by_tile],
        [(sds((seq, width), BF), by_tile), (sds((KINDS, width), F32), kept((KINDS, width)))],
        flops=1e6,
        moved=12e6,
    )(start, te, vec, first, first_mate, grad_middle)

    half = tiles // 2
    ff_mate = to_core(ff[seq // 2 :])
    (out_tokens,) = call(
        output_body,
        (half,),
        [by_tile, by_tile, by_tile, vecs],
        [(sds((seq // 2, width), BF), by_tile)],
        flops=1e6,
        moved=5e6,
    )(middle, ff, ff_mate, vec)

    def placed(values):
        mine, sent = values[:block], values[block : 2 * block]
        got = to_y(sent)
        return jnp.where(yi == 0, jnp.stack([mine, got]), jnp.stack([got, mine]))

    block_output = placed(out_tokens)
    input_gradient = placed(input_grad)

    def total(values):
        return jnp.sum(values.astype(F32), axis=0)

    def scatter_xy(oo, ox, yo, yx):
        got_o, got_y = to_x(ox), to_x(yx)
        own, oth = oo + got_o, yo + got_y
        return own + to_y(oth)

    def scatter_yx(oo, ox, yo, yx):
        got_y, got_x = to_y(yo), to_y(yx)
        own, oth = oo + got_y, ox + got_x
        return own + to_x(oth)

    def scatter_slow(oo, ox, yo, yx):
        own, oth = oo + to_y(yo), ox + to_y(yx)
        full = jnp.stack([own, oth], axis=1).reshape(width, -1).astype(F32)
        return lax.psum_scatter(full, ("a", "b"), scatter_dimension=0, tiled=True)

    if fast:
        gh = total(spread_z(scatter_xy(gh_oo, gh_ox, gh_yo, gh_yx)))
        gd = total(spread_z(scatter_yx(gd_oo, gd_ox, gd_yo, gd_yx)))
        ga = total(spread_z(scatter_yx(ga_oo, ga_ox, ga_yo, ga_yx)))
    else:
        gh = scatter_slow(gh_oo, gh_ox, gh_yo, gh_yx)
        gd = scatter_slow(gd_oo, gd_ox, gd_yo, gd_yx)
        ga = scatter_slow(ga_oo, ga_ox, ga_yo, ga_yx)

    owners = width // shard

    def pieces(hb_row, qkv_row, shared):
        kinds = [v.reshape(owners, 1, shard) for v in shared + [hb_row]]
        q_part, v_part = qkv_row[:192].reshape(owners, -1), qkv_row[384:].reshape(owners, -1)
        bias = jnp.concatenate([q_part, v_part], axis=1)
        bias = jnp.pad(bias, ((0, 0), (0, shard - bias.shape[1])))
        return jnp.concatenate(kinds + [bias[:, None]], axis=1)

    shared = [first_sums[0], first_sums[1], second_sums[2], second_sums[0], second_sums[1], second_sums[3]]
    small_o = pieces(hb_sum[0], qkv_sum_o[0], shared)
    small_y = pieces(hb_sum[1], qkv_sum_y[0], shared)
    embed = first_sums[2]
    sent = jnp.concatenate([small_y, embed.reshape(owners, 1, shard)], axis=1)
    got = to_y(sent)
    embed_got = got[:, KINDS].reshape(width)
    embed_gradient = jnp.where(yi == 0, jnp.stack([embed, embed_got]), jnp.stack([embed_got, embed]))
    small_sum = small_o + got[:, :KINDS]
    if fast:
        by_x = small_sum.reshape(ZS, XS, KINDS, shard)
        mine = lax.dynamic_index_in_dim(by_x, xi, 1, keepdims=False)
        other = lax.dynamic_index_in_dim(by_x, 1 - xi, 1, keepdims=False)
        sums = total(spread_z(mine + to_x(other)))
    else:
        sums = lax.psum_scatter(small_sum, ("a", "b"), scatter_dimension=0, tiled=True)[0]
    n_bias = query_bias.shape[0]
    n_head = query_weight.shape[1]
    return (
        block_output,
        input_gradient,
        embed_gradient,
        sums[0],
        sums[1],
        ga[:, :n_head],
        sums[7, :n_bias],
        ga[:, n_head : 2 * n_head],
        ga[:, 2 * n_head : 3 * n_head],
        sums[7, n_bias : 2 * n_bias],
        ga[:, 3 * n_head :].T,
        sums[2],
        sums[3],
        sums[4],
        gh,
        sums[6],
        gd.T,
        sums[5],
    )


def solution(mesh):
    dp, tensor = mesh.shape["dp"], mesh.shape["tensor"]
    fine = Mesh(mesh.devices.reshape(dp // 2, 2, tensor // 2, 2), ("a", "b", "y", "c"))
    by_dp, by_tensor = ("a", "b"), ("y", "c")
    both = by_tensor + by_dp
    column, matrix, turned = P(by_dp), P(by_dp, by_tensor), P(by_tensor, by_dp)
    seqs = P(by_dp, by_tensor, None)
    return jax.shard_map(
        functools.partial(body, dp == ZS * XS),
        mesh=fine,
        in_specs=(
            seqs, P(by_dp, None), column, column, matrix, P(both), matrix, matrix, P(both), turned,
            column, column, column, matrix, P(both), turned, column, seqs,
        ),
        out_specs=(
            seqs, seqs, P(by_dp, None), column, column, matrix, P(both), matrix, matrix, P(both), turned,
            column, column, column, matrix, P(both), turned, column,
        ),
        check_vma=False,
    )
```

```python
import functools

import jax
import jax.numpy as jnp
from jax import lax
from jax.experimental import pallas as pl
from jax.experimental.pallas import tpu as pltpu
from jax.sharding import Mesh
from jax.sharding import PartitionSpec as P

HD = 64
EPSILON = 1e-05
SCALE = 0.125
BF = jnp.bfloat16
F32 = jnp.float32
ZS, XS = 4, 2
KINDS = 8

NN = (((1,), (0,)), ((), ()))
NT = (((1,), (1,)), ((), ()))


def dot(left, right, dims=NN):
    return lax.dot_general(left, right, dims, preferred_element_type=F32)


def call(body, grid, ins, outs, scratch=(), flops=0, moved=0, trans=0, vmem=56):
    return pl.pallas_call(
        body,
        grid=grid,
        in_specs=[s for s in ins],
        out_specs=[s for _, s in outs],
        out_shape=[o for o, _ in outs],
        scratch_shapes=list(scratch),
        compiler_params=pltpu.CompilerParams(vmem_limit_bytes=vmem << 20),
        cost_estimate=pl.CostEstimate(flops=int(flops), bytes_accessed=int(moved), transcendentals=int(trans)),
    )


def whole(shape, n=1):
    zeros = (0,) * len(shape)
    return pl.BlockSpec(shape, lambda *_: zeros, pipeline_mode=pl.Buffered(1))


def kept(shape):
    zeros = (0,) * len(shape)
    return pl.BlockSpec(shape, lambda *_: zeros)


def scalar():
    return pl.BlockSpec(memory_space=pltpu.SMEM)


def sds(shape, dtype):
    return jax.ShapeDtypeStruct(shape, dtype)


def assemble(store, own, oth, x, rows, first=0):
    for z in range(ZS):
        store(pl.multiple_of((2 * z + x) * rows, 32), own[z, first : first + rows, :])
        store(pl.multiple_of((2 * z + 1 - x) * rows, 32), oth[z, first : first + rows, :])


def normalize(values):
    center = values - jnp.mean(values, axis=-1, keepdims=True)
    spread = jnp.mean(center * center, axis=-1, keepdims=True)
    rate = lax.rsqrt(spread + EPSILON)
    return center * rate, rate


def pack_attn_body(q_ref, k_ref, v_ref, o_ref, fg, fs, ob, sg, ss, db, hb, qb, vb, out_ref):
    shard = q_ref.shape[0]
    low = jnp.concatenate([q_ref[...], k_ref[...], v_ref[...], o_ref[...].T], axis=1)
    n = qb.shape[1]
    bias = jnp.concatenate([qb[...], vb[...], jnp.zeros((1, shard - 2 * n), BF)], axis=1)
    small = jnp.concatenate([r[...].astype(F32) for r in (fg, fs, ob, sg, ss, db, hb)] + [bias.astype(F32)], axis=0)
    small = jnp.concatenate([small, jnp.zeros((KINDS, low.shape[1] - shard), F32)], axis=1).astype(BF)
    for z in range(out_ref.shape[0]):
        out_ref[z, :shard, :] = low
        out_ref[z, shard:, :] = small


def pack_mlp_body(h_ref, d_ref, out_ref):
    shard = h_ref.shape[0]
    high, low = h_ref[...], d_ref[...].T
    for z in range(out_ref.shape[0]):
        out_ref[z, :shard, :] = high
        out_ref[z, shard:, :] = low


def pick(mine_ref, mate_ref):
    half = pl.num_programs(0) // 2
    return jnp.where(pl.program_id(0) < half, mine_ref[...], mate_ref[...])


def project_body(x_ref, *refs, rows, first):
    refs = list(refs)
    if first:
        mine_ref, mate_ref, te_ref, own_ref, oth_ref, w_ref, vec_ref, qkv_ref, normed_ref, normed_t_ref, bias_ref = refs
    else:
        source_ref, own_ref, oth_ref, w_ref, vec_ref, qkv_ref, bias_ref = refs

    @pl.when(pl.program_id(0) == 0)
    def _():
        def store(at, value):
            w_ref[pl.ds(at, rows), :] = value

        assemble(store, own_ref, oth_ref, x_ref[0], rows)
        own = [own_ref[z, rows:, :rows].astype(F32) for z in range(ZS)]
        oth = [oth_ref[z, rows:, :rows].astype(F32) for z in range(ZS)]
        even = jnp.concatenate([v for pair in zip(own, oth) for v in pair], axis=1)
        odd = jnp.concatenate([v for pair in zip(oth, own) for v in pair], axis=1)
        vec = jnp.where(x_ref[0] == 0, even, odd)
        vec_ref[...] = vec
        n = rows // 4
        last = vec[7:8, :]
        parts = [last[:, rows * k : rows * k + n] for k in range(ZS * XS)]
        parts += [jnp.zeros((1, 3 * HD), F32)]
        parts += [last[:, rows * k + n : rows * k + 2 * n] for k in range(ZS * XS)]
        bias_ref[0:1, :] = jnp.concatenate(parts, axis=1)

    if first:
        xhat, _ = normalize(pick(mine_ref, mate_ref).astype(F32) + te_ref[...].astype(F32))
        normed = (xhat * vec_ref[0:1, :] + vec_ref[1:2, :]).astype(BF)
        normed_ref[...] = normed
        normed_t_ref[...] = normed.T
    else:
        normed = source_ref[...]
    made = dot(normed, w_ref[:, :640])[:, :576] + bias_ref[0:1, :]
    made = made.astype(BF)
    for j in range(9):
        piece = made[:, 64 * j : 64 * j + 64]
        qkv_ref[j] = piece * BF(SCALE) if j < 3 else piece


def attend_body(q_ref, k_ref, v_ref, e_ref, inv_ref, mixed_ref, wide_ref):
    scores = dot(k_ref[0], q_ref[0], NT)
    expon = jnp.exp(scores - jnp.max(scores, axis=0, keepdims=True))
    inverse = 1.0 / jnp.sum(expon, axis=0, keepdims=True)
    low = expon.astype(BF)
    e_ref[0] = low
    inv_ref[0] = inverse
    wide = dot(v_ref[0].T, low) * inverse
    mixed_ref[0] = wide.astype(BF)
    wide_ref[0] = wide


def attend_back_body(q_ref, k_ref, v_ref, e_ref, inv_ref, mixed_ref, gm_ref, dq_ref, dk_ref, dv_ref, k_acc, v_acc):
    step, last = pl.program_id(1), pl.num_programs(1) - 1
    inverse = inv_ref[0]
    low = (gm_ref[0].astype(F32) * inverse).astype(BF)
    inner = jnp.sum(low.astype(F32) * mixed_ref[0], axis=0, keepdims=True)
    expon = e_ref[0]
    grads = dot(v_ref[0], low)
    grad_scores = (expon.astype(F32) * (grads - inner)).astype(BF)
    dv = dot(expon, low, NT)
    dk = dot(grad_scores, q_ref[0])

    @pl.when(step == 0)
    def _():
        v_acc[...] = dv
        k_acc[...] = dk

    @pl.when(step > 0)
    def _():
        v_acc[...] += dv
        k_acc[...] += dk

    dq_ref[0] = (dot(k_ref[0].T, grad_scores) * SCALE).T.astype(BF)

    @pl.when(step == last)
    def _():
        dk_ref[0] = k_acc[...].astype(BF)
        dv_ref[0] = v_acc[...].astype(BF)


def outproj_body(m0_ref, m1_ref, w0_ref, w1_ref, out_ref, wo_ref):
    @pl.when(pl.program_id(0) == 0)
    def _():
        wo_ref[...] = jnp.concatenate([w0_ref[:, 576:], w1_ref[:, 576:]], axis=1)

    mixed = jnp.concatenate([m0_ref[...], m1_ref[...]], axis=0).T
    out_ref[...] = dot(mixed, wo_ref[...], NT).astype(BF)


def mlp_body(
    x_ref, s0_ref, s1_ref, te_ref, a0_ref, a1_ref, c0_ref, c1_ref, vec_ref, vec_y_ref,
    w_oo, w_ox, w_yo, h_yx, d_yx,
    mid_ref, ff0_ref, ff1_ref, gs_ref, hbg_ref, gh_oo, gh_ox, gh_yo, gh_yx, gd_oo, gd_ox, gd_yo, gd_yx,
    wh, wd, acc_h, acc_d, *, rows,
):
    step, last = pl.program_id(0), pl.num_programs(0) - 1
    x = x_ref[0]

    @pl.when(step == 0)
    def _():
        for z in range(ZS):
            own = pl.multiple_of((2 * z + x) * rows, 32)
            oth = pl.multiple_of((2 * z + 1 - x) * rows, 32)
            for y, first, second in ((0, w_oo, w_ox), (1, w_yo, None)):
                wh[y, pl.ds(own, rows), :] = first[z, :rows, :]
                wd[y, pl.ds(own, rows), :] = first[z, rows:, :]
                wh[y, pl.ds(oth, rows), :] = h_yx[z] if second is None else second[z, :rows, :]
                wd[y, pl.ds(oth, rows), :] = d_yx[z] if second is None else second[z, rows:, :]
        acc_h[...] = jnp.zeros_like(acc_h)
        acc_d[...] = jnp.zeros_like(acc_d)
        hbg_ref[...] = jnp.zeros_like(hbg_ref)

    middle = (
        pick(s0_ref, s1_ref).astype(F32)
        + te_ref[...].astype(F32)
        + (a0_ref[...].astype(F32) + a1_ref[...].astype(F32))
        + vec_ref[2:3, :]
    )
    mid_ref[...] = middle
    xhat, _ = normalize(middle)
    normed = (xhat * vec_ref[3:4, :] + vec_ref[4:5, :]).astype(BF)
    normed_t = normed.T
    cot = pick(c0_ref, c1_ref)
    cot_t = cot.T
    ff = gs = None
    for y in range(2):
        pre = dot(normed, wh[y]) + (vec_y_ref if y else vec_ref)[6:7, :]
        below = 0.5 + 0.5 * lax.erf(pre * 0.7071067811865476)
        act = (pre * below).astype(BF)
        slope = below + pre * (jnp.exp(-0.5 * pre * pre) * 0.3989422804014327)
        grad = (dot(cot, wd[y]) * slope).astype(BF)
        ff_y = dot(act, wd[y], NT)
        gs_y = dot(grad, wh[y], NT)
        ff = ff_y if ff is None else ff + ff_y
        gs = gs_y if gs is None else gs + gs_y
        acc_h[y] += dot(normed_t, grad)
        acc_d[y] += dot(cot_t, act)
        hbg_ref[y : y + 1, :] += jnp.sum(grad.astype(F32), axis=0, keepdims=True)

    @pl.when(step < pl.num_programs(0) // 2)
    def _():
        ff0_ref[...] = ff.astype(BF)

    @pl.when(step >= pl.num_programs(0) // 2)
    def _():
        ff1_ref[...] = ff.astype(BF)

    gs_ref[...] = gs.astype(BF)

    @pl.when(step == last)
    def _():
        for acc, sets in ((acc_h, ((gh_oo, gh_ox), (gh_yo, gh_yx))), (acc_d, ((gd_oo, gd_ox), (gd_yo, gd_yx)))):
            for y, (own, oth) in enumerate(sets):
                for z in range(ZS):
                    at = pl.multiple_of((2 * z + x) * rows, 32)
                    own[z] = acc[y, pl.ds(at, rows), :].astype(BF)
                    at = pl.multiple_of((2 * z + 1 - x) * rows, 32)
                    oth[z] = acc[y, pl.ds(at, rows), :].astype(BF)


def second_back_body(mid_ref, g0_ref, g1_ref, c0_ref, c1_ref, vec_ref, w0_ref, w1_ref, m0_ref, m1_ref, gm_ref, x0_ref, x1_ref, wo0_ref, wo1_ref, sum_ref, wo_ref, acc):
    step, last = pl.program_id(0), pl.num_programs(0) - 1

    @pl.when(step == 0)
    def _():
        wo_ref[...] = jnp.concatenate([w0_ref[:, 576:], w1_ref[:, 576:]], axis=1)
        acc[...] = jnp.zeros_like(acc)
        sum_ref[...] = jnp.zeros_like(sum_ref)

    xhat, rate = normalize(mid_ref[...])
    second = g0_ref[...].astype(F32) + g1_ref[...].astype(F32)
    cot = pick(c0_ref, c1_ref).astype(F32)
    scaled = second * vec_ref[3:4, :]
    inner = jnp.mean(scaled * xhat, axis=-1, keepdims=True)
    grad = cot + rate * (scaled - jnp.mean(scaled, axis=-1, keepdims=True) - xhat * inner)
    gm_ref[...] = grad
    sum_ref[0:1, :] += jnp.sum(second * xhat, axis=0, keepdims=True)
    sum_ref[1:2, :] += jnp.sum(second, axis=0, keepdims=True)
    sum_ref[2:3, :] += jnp.sum(grad, axis=0, keepdims=True)
    sum_ref[3:4, :] += jnp.sum(cot, axis=0, keepdims=True)
    low = grad.astype(BF)
    back = dot(low, wo_ref[...]).astype(BF).T
    x0_ref[...] = back[:192]
    x1_ref[...] = back[192:]
    mixed = jnp.concatenate([m0_ref[...], m1_ref[...]], axis=0)
    acc[...] += dot(low.T, mixed, NT)

    @pl.when(step == last)
    def _():
        wo0_ref[...] = acc[:, :192].astype(BF)
        wo1_ref[...] = acc[:, 192:].astype(BF)


def project_back_body(x_ref, q_ref, k_ref, v_ref, nt_ref, w_ref, wo_ref, *refs, rows, more):
    refs = list(refs)
    prev_ref = refs.pop(0) if more else None
    own_ref, oth_ref, first_ref, sum_ref, acc = refs
    step, last = pl.program_id(0), pl.num_programs(0) - 1
    x = x_ref[0]
    grads = jnp.concatenate([r[h] for r in (q_ref, k_ref, v_ref) for h in range(3)], axis=1)
    made = dot(nt_ref[...], grads)
    total = jnp.sum(grads.astype(F32), axis=0, keepdims=True)

    @pl.when(step == 0)
    def _():
        acc[...] = made
        sum_ref[...] = total

    @pl.when(step > 0)
    def _():
        acc[...] += made
        sum_ref[...] += total

    back = dot(grads, w_ref[:, :576], NT)
    if more:
        back = back + prev_ref[...]
    first_ref[...] = back.astype(first_ref.dtype)

    @pl.when(step == last)
    def _():
        for z in range(ZS):
            for ref, side in ((own_ref, x), (oth_ref, 1 - x)):
                at = pl.multiple_of((2 * z + side) * rows, 32)
                ref[z] = jnp.concatenate(
                    [acc[pl.ds(at, rows), :].astype(BF), wo_ref[pl.ds(at, rows), :]], axis=1
                )


def first_back_body(s0_ref, s1_ref, te_ref, vec_ref, g0_ref, g1_ref, gm_ref, out_ref, sum_ref):
    @pl.when(pl.program_id(0) == 0)
    def _():
        sum_ref[...] = jnp.zeros_like(sum_ref)

    xhat, rate = normalize(pick(s0_ref, s1_ref).astype(F32) + te_ref[...].astype(F32))
    first = g0_ref[...].astype(F32) + g1_ref[...].astype(F32)
    scaled = first * vec_ref[0:1, :]
    inner = jnp.mean(scaled * xhat, axis=-1, keepdims=True)
    grad = gm_ref[...] + rate * (scaled - jnp.mean(scaled, axis=-1, keepdims=True) - xhat * inner)
    out_ref[...] = grad.astype(BF)
    sum_ref[0:1, :] += jnp.sum(first * xhat, axis=0, keepdims=True)
    sum_ref[1:2, :] += jnp.sum(first, axis=0, keepdims=True)
    sum_ref[2:3, :] += jnp.sum(grad, axis=0, keepdims=True)


def output_body(mid_ref, f0_ref, f1_ref, vec_ref, out_ref):
    out_ref[...] = (
        mid_ref[...] + (f0_ref[...].astype(F32) + f1_ref[...].astype(F32)) + vec_ref[5:6, :]
    ).astype(BF)


def swap(size):
    return [(i, size - 1 - i) for i in range(size)]


def to_y(values):
    return lax.ppermute(values, "y", swap(2))


def to_x(values):
    return lax.ppermute(values, "b", swap(2))


def to_core(values):
    return lax.ppermute(values, "c", swap(2))


def spread_z(values):
    return lax.all_to_all(values, "a", 0, 0, tiled=True)


def after(value, *others):
    return lax.optimization_barrier((value, *others))[0]


def body(
    fast,
    inputs,
    time_embed,
    first_gain,
    first_shift,
    query_weight,
    query_bias,
    key_weight,
    value_weight,
    value_bias,
    output_weight,
    output_bias,
    second_gain,
    second_shift,
    hidden_weight,
    hidden_bias,
    down_weight,
    down_bias,
    cotangent,
):
    _, block, width = inputs.shape
    shard = query_weight.shape[0]
    rows = width // (ZS * XS)
    seq = 4 * block
    tile = block
    tiles = seq // tile
    hidden = hidden_weight.shape[1]
    yi = lax.axis_index("y")
    xi = lax.axis_index("b") if fast else jnp.int32(0)
    x_arr = xi.astype(jnp.int32)[None]

    both = jnp.concatenate([inputs, cotangent], axis=1)
    stays = lax.dynamic_index_in_dim(both, yi, 0, keepdims=False).reshape(2, 1, block, width)
    comes = to_y(lax.dynamic_index_in_dim(both, 1 - yi, 0, keepdims=False)).reshape(2, 1, block, width)
    pair = jnp.concatenate([stays, comes], axis=1).reshape(2, 2 * block, width)
    pair_mate = to_core(pair)
    te = lax.dynamic_index_in_dim(time_embed, yi, 0, keepdims=True)

    n_copies = ZS if fast else 1
    (attn_pack,) = call(
        pack_attn_body,
        (1,),
        [kept((shard, hidden // 4))] * 3 + [kept((hidden // 4, shard))] + [kept((1, shard))] * 7 + [kept((1, query_bias.shape[0]))] * 2,
        [(sds((n_copies, shard + KINDS, width), BF), kept((n_copies, shard + KINDS, width)))],
        flops=1e6,
        moved=1e6,
    )(
        query_weight, key_weight, value_weight, output_weight,
        *(v[None] for v in (first_gain, first_shift, output_bias, second_gain, second_shift, down_bias, hidden_bias, query_bias, value_bias)),
    )
    (mlp_pack,) = call(
        pack_mlp_body,
        (1,),
        [kept((shard, hidden)), kept((hidden, shard))],
        [(sds((n_copies, 2 * shard, width), BF), kept((n_copies, 2 * shard, width)))],
        flops=1e6,
        moved=2e6,
    )(hidden_weight, down_weight)

    if fast:
        attn_oo = spread_z(attn_pack)
        attn_ox = to_x(attn_oo)
        attn_yo = to_y(attn_oo)
        attn_yx = to_y(attn_ox)
        mlp_oo = spread_z(after(mlp_pack, attn_oo))
    else:
        def natural(values):
            full = lax.all_gather(values, ("a", "b"), axis=0, tiled=True)
            full = full.reshape(ZS, XS, rows, width)
            return full[:, 0], full[:, 1]

        gathered = lax.all_gather(attn_pack[0], ("a", "b"), axis=0, tiled=False)
        matrix = gathered[:, :shard].reshape(ZS, XS, rows, width)
        small = gathered[:, shard:, :shard]
        flat = small[:, :7].transpose(1, 0, 2).reshape(7, width)
        n = shard // 4
        bias = [small[:, 7, k * n : k * n + n].reshape(ZS * XS, -1) for k in range(2)]
        bias = jnp.concatenate([*bias, jnp.zeros((ZS * XS, rows - 2 * (rows // 4)), BF)], axis=1)
        small = jnp.concatenate([flat, bias.reshape(1, width)], axis=0)
        small = small.reshape(KINDS, ZS, XS, rows).transpose(1, 2, 0, 3)
        small = jnp.pad(small, ((0, 0), (0, 0), (0, 0), (0, width - rows)))
        matrix = jnp.concatenate([matrix, small], axis=2)
        attn_oo, attn_ox = matrix[:, 0], matrix[:, 1]
        attn_yo, attn_yx = to_y(attn_oo), to_y(attn_ox)
        h_oo, h_ox = natural(mlp_pack[0, :shard])
        d_oo, d_ox = natural(mlp_pack[0, shard:])
        mlp_oo = jnp.concatenate([h_oo, d_oo], axis=1)
        mlp_ox = jnp.concatenate([h_ox, d_ox], axis=1)

    by_tile = pl.BlockSpec((tile, width), lambda i: (i, 0))
    by_mate = pl.BlockSpec((tile, width), lambda i: ((i + tiles // 2) % tiles, 0))
    row = kept((1, width))
    vecs = kept((KINDS, width))
    square = whole((width, width))
    part_rows = attn_oo.shape[1]
    heads9 = pl.BlockSpec((9, tile, HD), lambda i: (0, i, 0))

    def mine(which):
        return pl.BlockSpec((None, tile, width), lambda i: (which, jnp.minimum(i, tiles // 2 - 1), 0))

    def mate(which):
        return pl.BlockSpec((None, tile, width), lambda i: (which, jnp.maximum(i - tiles // 2, 0), 0))

    def project(first, source, own, oth):
        outs = [
            (sds((width, width), BF), kept((width, width))),
            (sds((KINDS, width), F32), vecs),
            (sds((9, seq, HD), BF), heads9),
        ]
        if first:
            outs += [
                (sds((seq, width), BF), by_tile),
                (sds((width, seq), BF), pl.BlockSpec((width, tile), lambda i: (0, i))),
            ]
        return call(
            functools.partial(project_body, rows=rows, first=first),
            (tiles,),
            [scalar()] + ([mine(0), mate(0), row] if first else [by_tile]) + [whole((ZS, part_rows, width))] * 2,
            outs,
            scratch=[pltpu.VMEM((8, 9 * HD), F32)],
            flops=2 * seq * width * 576,
            moved=8e6,
        )(x_arr, *source, own, oth)

    chunks = tiles
    q_spec = pl.BlockSpec((1, tile, HD), lambda h, i: (h, i, 0))
    k_spec = pl.BlockSpec((1, seq, HD), lambda h, i: (3 + h, 0, 0))
    v_spec = pl.BlockSpec((1, seq, HD), lambda h, i: (6 + h, 0, 0))
    e_spec = pl.BlockSpec((1, seq, tile), lambda h, i: (h, 0, i))
    inv_spec = pl.BlockSpec((1, 1, tile), lambda h, i: (h, 0, i))
    t_spec = pl.BlockSpec((1, HD, tile), lambda h, i: (h, 0, i))

    def attend(qkv):
        return call(
            attend_body,
            (3, chunks),
            [q_spec, k_spec, v_spec],
            [
                (sds((3, seq, seq), BF), e_spec),
                (sds((3, 1, seq), F32), inv_spec),
                (sds((3, HD, seq), BF), t_spec),
                (sds((3, HD, seq), F32), t_spec),
            ],
            flops=3 * 16 * seq * seq * HD,
            moved=8e6,
            trans=3 * seq * seq,
        )(qkv, qkv, qkv)

    def attend_back(qkv, expon, inverse, mixed, grad_mixed):
        full = pl.BlockSpec((1, seq, HD), lambda h, i: (h, 0, 0))
        return call(
            attend_back_body,
            (3, chunks),
            [q_spec, k_spec, v_spec, e_spec, inv_spec, t_spec, t_spec],
            [(sds((3, seq, HD), BF), q_spec), (sds((3, seq, HD), BF), full), (sds((3, seq, HD), BF), full)],
            scratch=[pltpu.VMEM((seq, HD), F32), pltpu.VMEM((seq, HD), F32)],
            flops=3 * 40 * seq * seq * HD,
            moved=9e6,
        )(qkv, qkv, qkv, expon, inverse, mixed, grad_mixed)

    w_o, vec, qkv_o, normed, normed_t = project(True, (pair, pair_mate, te), attn_oo, attn_ox)
    exp_o, inv_o, mixed_o, wide_o = attend(qkv_o)
    normed, exp_o, mlp_oo, attn_yo, attn_yx = lax.optimization_barrier((normed, exp_o, mlp_oo, attn_yo, attn_yx))
    if fast:
        mlp_ox, mlp_yo = to_x(mlp_oo), to_y(mlp_oo)
    else:
        mlp_yo = to_y(mlp_oo)
    w_y, vec_y, qkv_y = project(False, (normed,), attn_yo, attn_yx)
    exp_y, inv_y, mixed_y, wide_y = attend(qkv_y)
    mixed_y, mlp_ox, mlp_yo = lax.optimization_barrier((mixed_y, mlp_ox, mlp_yo))
    h_yx = to_y(mlp_ox[:, :rows])
    d_yx = to_x(mlp_yo[:, rows:]) if fast else to_y(mlp_ox[:, rows:])

    half_t = pl.BlockSpec((3 * HD, tile), lambda i: (0, i))
    flat_o, flat_y = mixed_o.reshape(3 * HD, seq), mixed_y.reshape(3 * HD, seq)
    (attended,) = call(
        outproj_body,
        (tiles,),
        [half_t, half_t, square, square],
        [(sds((seq, width), BF), by_tile)],
        scratch=[pltpu.VMEM((width, 6 * HD), BF)],
        flops=2 * seq * width * 384,
        moved=6e6,
    )(flat_o, flat_y, w_o, w_y)
    attended_mate = to_core(attended)

    part = (ZS, rows, hidden)
    middle, ff, ff_sent, gs, hb_sum, gh_oo, gh_ox, gh_yo, gh_yx, gd_oo, gd_ox, gd_yo, gd_yx = call(
        functools.partial(mlp_body, rows=rows),
        (tiles,),
        [scalar(), mine(0), mate(0), row, by_tile, by_mate, mine(1), mate(1), vecs, vecs] + [whole((ZS, 2 * rows, hidden))] * 3 + [whole(part)] * 2,
        [
            (sds((seq, width), F32), by_tile),
            (sds((seq // 2, width), BF), pl.BlockSpec((tile, width), lambda i: (jnp.minimum(i, tiles // 2 - 1), 0))),
            (sds((seq // 2, width), BF), pl.BlockSpec((tile, width), lambda i: (jnp.maximum(i - tiles // 2, 0), 0))),
            (sds((seq, width), BF), by_tile),
            (sds((2, hidden), F32), kept((2, hidden))),
        ]
        + [(sds(part, BF), kept(part))] * 8,
        scratch=[
            pltpu.VMEM((2, width, hidden), BF),
            pltpu.VMEM((2, width, hidden), BF),
            pltpu.VMEM((2, width, hidden), F32),
            pltpu.VMEM((2, width, hidden), F32),
        ],
        flops=12 * seq * width * hidden * 2,
        moved=24e6,
        trans=seq * hidden * 4,
    )(x_arr, pair, pair_mate, te, attended, attended_mate, pair, pair_mate, vec, vec_y, mlp_oo, mlp_ox, mlp_yo, h_yx, d_yx)
    gs_mate = to_core(gs)

    grad_middle, gx_o, gx_y, wo_o, wo_y, second_sums = call(
        second_back_body,
        (tiles,),
        [by_tile, by_tile, by_mate, mine(1), mate(1), vecs, square, square, half_t, half_t],
        [
            (sds((seq, width), F32), by_tile),
            (sds((3 * HD, seq), BF), half_t),
            (sds((3 * HD, seq), BF), half_t),
            (sds((width, 3 * HD), BF), kept((width, 3 * HD))),
            (sds((width, 3 * HD), BF), kept((width, 3 * HD))),
            (sds((KINDS, width), F32), kept((KINDS, width))),
        ],
        scratch=[pltpu.VMEM((width, 6 * HD), BF), pltpu.VMEM((width, 6 * HD), F32)],
        flops=4 * seq * width * 384,
        moved=16e6,
    )(middle, gs, gs_mate, pair, pair_mate, vec, w_o, w_y, flat_o, flat_y)

    heads = pl.BlockSpec((3, tile, HD), lambda i: (0, i, 0))
    attn_part = (ZS, rows, width)

    def project_back(grads, weights, wo, prev):
        more = prev is not None
        return call(
            functools.partial(project_back_body, rows=rows, more=more),
            (tiles,),
            [scalar(), heads, heads, heads, pl.BlockSpec((width, tile), lambda i: (0, i)), square, whole((width, 3 * HD))]
            + ([by_tile] if more else []),
            [
                (sds(attn_part, BF), kept(attn_part)),
                (sds(attn_part, BF), kept(attn_part)),
                (sds((seq, width), BF if more else F32), by_tile),
                (sds((1, 576), F32), kept((1, 576))),
            ],
            scratch=[pltpu.VMEM((width, 576), F32)],
            flops=4 * seq * width * 576,
            moved=10e6,
        )(x_arr, *grads, normed_t, weights, wo, *((prev,) if more else ()))

    half = tiles // 2
    ff_mate = to_core(ff_sent)
    (out_tokens,) = call(
        output_body,
        (half,),
        [by_tile, by_tile, by_tile, vecs],
        [(sds((seq // 2, width), BF), by_tile)],
        flops=1e6,
        moved=5e6,
    )(middle, ff, ff_mate, vec)
    if fast:
        got_h, got_d = to_x(gh_yx), to_y(gd_yx)
        gx_y, out_tokens, got_h, got_d, gh_ox, gd_yo = lax.optimization_barrier(
            (gx_y, out_tokens, got_h, got_d, gh_ox, gd_yo)
        )
        got_ho, got_do = to_x(gh_ox), to_y(gd_yo)
        got_hs, got_ds = to_y(gh_yo + got_h), to_x(gd_ox + got_d)
    out_got = to_y(out_tokens[block:])
    grads_y = attend_back(qkv_y, exp_y, inv_y, wide_y, gx_y.reshape(3, HD, seq))
    ga_yo, ga_yx, first_part, qkv_sum_y = project_back(grads_y, w_y, wo_y, None)
    if fast:
        gx_o, first_part, out_got, got_ho, got_do, got_hs, got_ds, ga_yo, ga_yx = lax.optimization_barrier(
            (gx_o, first_part, out_got, got_ho, got_do, got_hs, got_ds, ga_yo, ga_yx)
        )
        mlp_all = spread_z(jnp.concatenate([gh_oo + got_ho + got_hs, gd_oo + got_do + got_ds], axis=1))
        ga_sx = to_y(ga_yx)
    grads_o = attend_back(qkv_o, exp_o, inv_o, wide_o, gx_o.reshape(3, HD, seq))
    if fast:
        *grads_o, ga_sx, ga_yo = lax.optimization_barrier((*grads_o, ga_sx, ga_yo))
        ga_so = to_y(ga_yo)
    ga_oo, ga_ox, first, qkv_sum_o = project_back(grads_o, w_o, wo_o, first_part)
    first_mate = to_core(first)
    if fast:
        ga_x = to_x(ga_ox + ga_sx)
        first_mate, mlp_all, ga_so = lax.optimization_barrier((first_mate, mlp_all, ga_so))

    input_grad, first_sums = call(
        first_back_body,
        (tiles,),
        [mine(0), mate(0), row, vecs, by_tile, by_mate, by_tile],
        [(sds((seq, width), BF), by_tile), (sds((KINDS, width), F32), kept((KINDS, width)))],
        flops=1e6,
        moved=12e6,
    )(pair, pair_mate, te, vec, first, first_mate, grad_middle)

    def total(values):
        return jnp.sum(values.astype(F32), axis=0)

    def scatter_slow(oo, ox, yo, yx):
        own, oth = oo + to_y(yo), ox + to_y(yx)
        full = jnp.stack([own, oth], axis=1).reshape(width, -1).astype(F32)
        return lax.psum_scatter(full, ("a", "b"), scatter_dimension=0, tiled=True)

    owners = width // shard

    def pieces(hb_row, qkv_row, shared):
        kinds = [v.reshape(owners, 1, shard) for v in shared + [hb_row]]
        q_part, v_part = qkv_row[:192].reshape(owners, -1), qkv_row[384:].reshape(owners, -1)
        bias = jnp.concatenate([q_part, v_part], axis=1)
        bias = jnp.pad(bias, ((0, 0), (0, shard - bias.shape[1])))
        return jnp.concatenate(kinds + [bias[:, None]], axis=1)

    shared = [first_sums[0], first_sums[1], second_sums[2], second_sums[0], second_sums[1], second_sums[3]]
    small_o = pieces(hb_sum[0], qkv_sum_o[0], shared)
    small_y = pieces(hb_sum[1], qkv_sum_y[0], shared)
    embed = first_sums[2]
    sent = jnp.concatenate([small_y, embed.reshape(owners, 1, shard)], axis=1)
    got = to_y(sent)
    embed_got = got[:, KINDS].reshape(width)
    embed_gradient = jnp.where(yi == 0, jnp.stack([embed, embed_got]), jnp.stack([embed_got, embed]))
    small_sum = small_o + got[:, :KINDS]
    n_head = query_weight.shape[1]
    if fast:
        by_x = small_sum.reshape(ZS, XS, KINDS, shard)
        stays = lax.dynamic_index_in_dim(by_x, xi, 1, keepdims=False)
        other = lax.dynamic_index_in_dim(by_x, 1 - xi, 1, keepdims=False)
        small_x = to_x(other)
        input_grad, small_x, ga_x = lax.optimization_barrier((input_grad, small_x, ga_x))
        small_sum = jnp.pad((stays + small_x).astype(BF), ((0, 0), (0, 0), (0, width - shard)))
        ga = total(spread_z(jnp.concatenate([ga_oo + ga_so + ga_x, small_sum], axis=1)))
        ga, sums = ga[:shard], ga[shard:, :shard]
        mlp_sum = total(mlp_all)
        gh, gd = mlp_sum[:shard], mlp_sum[shard:]
    else:
        sums = lax.psum_scatter(small_sum, ("a", "b"), scatter_dimension=0, tiled=True)[0]
        gh = scatter_slow(gh_oo, gh_ox, gh_yo, gh_yx)
        gd = scatter_slow(gd_oo, gd_ox, gd_yo, gd_yx)
        ga = scatter_slow(ga_oo, ga_ox, ga_yo, ga_yx)

    def placed(mine, got):
        return jnp.where(yi == 0, jnp.stack([mine, got]), jnp.stack([got, mine]))

    block_output = placed(out_tokens[:block], out_got)
    input_gradient = placed(input_grad[:block], to_y(input_grad[block : 2 * block]))
    n_bias = query_bias.shape[0]
    return (
        block_output,
        input_gradient,
        embed_gradient,
        sums[0],
        sums[1],
        ga[:, :n_head],
        sums[7, :n_bias],
        ga[:, n_head : 2 * n_head],
        ga[:, 2 * n_head : 3 * n_head],
        sums[7, n_bias : 2 * n_bias],
        ga[:, 3 * n_head :].T,
        sums[2],
        sums[3],
        sums[4],
        gh,
        sums[6],
        gd.T,
        sums[5],
    )


def solution(mesh):
    dp, tensor = mesh.shape["dp"], mesh.shape["tensor"]
    fine = Mesh(mesh.devices.reshape(dp // 2, 2, tensor // 2, 2), ("a", "b", "y", "c"))
    by_dp, by_tensor = ("a", "b"), ("y", "c")
    both = by_tensor + by_dp
    column, matrix, turned = P(by_dp), P(by_dp, by_tensor), P(by_tensor, by_dp)
    seqs = P(by_dp, by_tensor, None)
    return jax.shard_map(
        functools.partial(body, dp == ZS * XS),
        mesh=fine,
        in_specs=(
            seqs, P(by_dp, None), column, column, matrix, P(both), matrix, matrix, P(both), turned,
            column, column, column, matrix, P(both), turned, column, seqs,
        ),
        out_specs=(
            seqs, seqs, P(by_dp, None), column, column, matrix, P(both), matrix, matrix, P(both), turned,
            column, column, column, matrix, P(both), turned, column,
        ),
        check_vma=False,
    )
```

```python
import functools

import jax
import jax.numpy as jnp
from jax import lax
from jax.experimental import pallas as pl
from jax.experimental.pallas import tpu as pltpu
from jax.sharding import Mesh
from jax.sharding import PartitionSpec as P

HD = 64
EPSILON = 1e-05
SCALE = 0.125
BF = jnp.bfloat16
F32 = jnp.float32
ZS, XS = 4, 2
KINDS = 8
HINT = 1.0
TILE_PROJECT = 256
TILE_OUT = 256
TILE_MLP = 256
TILE_SECOND = 256
TILE_BACK = 256
TILE_FIRST = 256

NN = (((1,), (0,)), ((), ()))
NT = (((1,), (1,)), ((), ()))


def dot(left, right, dims=NN):
    return lax.dot_general(left, right, dims, preferred_element_type=F32)


def call(body, grid, ins, outs, scratch=(), flops=0, moved=0, trans=0, vmem=16):
    return pl.pallas_call(
        body,
        grid=grid,
        in_specs=[s for s in ins],
        out_specs=[s for _, s in outs],
        out_shape=[o for o, _ in outs],
        scratch_shapes=list(scratch),
        compiler_params=pltpu.CompilerParams(vmem_limit_bytes=vmem << 20),
        cost_estimate=pl.CostEstimate(flops=int(flops * HINT), bytes_accessed=int(moved * HINT), transcendentals=int(trans * HINT)),
    )


def whole(shape, n=1):
    zeros = (0,) * len(shape)
    return pl.BlockSpec(shape, lambda *_: zeros, pipeline_mode=pl.Buffered(1))


def kept(shape):
    zeros = (0,) * len(shape)
    return pl.BlockSpec(shape, lambda *_: zeros)


def far(values):
    return pltpu.with_memory_space_constraint(values, pltpu.HBM)


def scalar():
    return pl.BlockSpec(memory_space=pltpu.SMEM)


def sds(shape, dtype):
    return jax.ShapeDtypeStruct(shape, dtype)


def shard_of(refs, z, rows):
    parts = [r[z] for r in refs]
    value = parts[0] if len(parts) == 1 else jnp.concatenate(parts, axis=0)
    return value[:rows], value[rows:]


def normalize(values):
    center = values - jnp.mean(values, axis=-1, keepdims=True)
    spread = jnp.mean(center * center, axis=-1, keepdims=True)
    rate = lax.rsqrt(spread + EPSILON)
    return center * rate, rate


def pack_attn_body(q_ref, k_ref, v_ref, o_ref, fg, fs, ob, sg, ss, db, hb, qb, vb, out_ref):
    shard = q_ref.shape[0]
    low = jnp.concatenate([q_ref[...], k_ref[...], v_ref[...], o_ref[...].T], axis=1)
    n = qb.shape[1]
    bias = jnp.concatenate([qb[...], vb[...], jnp.zeros((1, shard - 2 * n), BF)], axis=1)
    small = jnp.concatenate([r[...].astype(F32) for r in (fg, fs, ob, sg, ss, db, hb)] + [bias.astype(F32)], axis=0)
    small = jnp.concatenate([small, jnp.zeros((KINDS, low.shape[1] - shard), F32)], axis=1).astype(BF)
    for z in range(out_ref.shape[0]):
        out_ref[z, :shard, :] = low
        out_ref[z, shard:, :] = small


def pack_mlp_body(h_ref, d_ref, out_ref):
    shard = h_ref.shape[0]
    high, low = h_ref[...], d_ref[...].T
    for z in range(out_ref.shape[0]):
        out_ref[z, :shard, :] = high
        out_ref[z, shard:, :] = low


def pick(refs):
    step, each = pl.program_id(0), len(refs) // pl.num_programs(0)
    blocks = [r[...] for r in refs]
    tiles = [blocks[k : k + each] for k in range(0, len(blocks), each)]
    tiles = [t[0] if each == 1 else jnp.concatenate(t, axis=0) for t in tiles]
    value = tiles[0]
    for k in range(1, len(tiles)):
        value = jnp.where(step == k, tiles[k], value)
    return value


def project_body(x_ref, *refs, rows, first):
    refs = list(refs)
    if first:
        *tokens, te_ref, own_ref, oth_ref, w_ref, vec_ref, qkv_ref, normed_ref, normed_t_ref, bias_ref = refs
        oth_refs = (oth_ref,)
    else:
        source_ref, own_ref, *oth_refs, w_ref, vec_ref, qkv_ref, bias_ref = refs

    @pl.when(pl.program_id(0) == 0)
    def _():
        x = x_ref[0]
        own, oth = [], []
        for z in range(ZS):
            weight, small = shard_of((own_ref,), z, rows)
            w_ref[pl.ds(pl.multiple_of((2 * z + x) * rows, 32), rows), :] = weight
            own.append(small[:, :rows].astype(F32))
            weight, small = shard_of(oth_refs, z, rows)
            w_ref[pl.ds(pl.multiple_of((2 * z + 1 - x) * rows, 32), rows), :] = weight
            oth.append(small[:, :rows].astype(F32))
        even = jnp.concatenate([v for pair in zip(own, oth) for v in pair], axis=1)
        odd = jnp.concatenate([v for pair in zip(oth, own) for v in pair], axis=1)
        vec = jnp.where(x == 0, even, odd)
        vec_ref[...] = vec
        n = rows // 4
        last = vec[7:8, :]
        parts = [last[:, rows * k : rows * k + n] for k in range(ZS * XS)]
        parts += [jnp.zeros((1, 3 * HD), F32)]
        parts += [last[:, rows * k + n : rows * k + 2 * n] for k in range(ZS * XS)]
        bias_ref[0:1, :] = jnp.concatenate(parts, axis=1)

    if first:
        xhat, _ = normalize(pick(tokens).astype(F32) + te_ref[...].astype(F32))
        normed = (xhat * vec_ref[0:1, :] + vec_ref[1:2, :]).astype(BF)
        normed_ref[...] = normed
        normed_t_ref[...] = normed.T
    else:
        normed = source_ref[...]
    made = dot(normed, w_ref[:, :640])[:, :576] + bias_ref[0:1, :]
    made = made.astype(BF)
    for j in range(9):
        piece = made[:, 64 * j : 64 * j + 64]
        qkv_ref[j] = piece * BF(SCALE) if j < 3 else piece


def attend_body(q_ref, k_ref, v_ref, e_ref, inv_ref, mixed_ref, wide_ref):
    scores = dot(k_ref[0], q_ref[0], NT)
    expon = jnp.exp(scores - jnp.max(scores, axis=0, keepdims=True))
    inverse = 1.0 / jnp.sum(expon, axis=0, keepdims=True)
    low = expon.astype(BF)
    e_ref[0] = low
    inv_ref[0] = inverse
    wide = dot(v_ref[0].T, low) * inverse
    mixed_ref[0] = wide.astype(BF)
    wide_ref[0] = wide


def attend_back_body(q_ref, k_ref, v_ref, e_ref, inv_ref, mixed_ref, gm_ref, dq_ref, dk_ref, dv_ref):
    low = (gm_ref[0].astype(F32) * inv_ref[0]).astype(BF)
    inner = jnp.sum(low.astype(F32) * mixed_ref[0], axis=0, keepdims=True)
    expon = e_ref[0]
    grad_scores = (expon.astype(F32) * (dot(v_ref[0], low) - inner)).astype(BF)
    dv_ref[0] = dot(expon, low, NT).astype(BF)
    dk_ref[0] = dot(grad_scores, q_ref[0]).astype(BF)
    dq_ref[0] = (dot(k_ref[0].T, grad_scores) * SCALE).T.astype(BF)


def outproj_body(m0_ref, m1_ref, w0_ref, w1_ref, out_ref, wo_ref):
    @pl.when(pl.program_id(0) == 0)
    def _():
        wo_ref[...] = jnp.concatenate([w0_ref[:, 576:], w1_ref[:, 576:]], axis=1)

    mixed = jnp.concatenate([m0_ref[...], m1_ref[...]], axis=0).T
    out_ref[...] = dot(mixed, wo_ref[...], NT).astype(BF)


def feed(normed, cot, wh, wd, bias, acc_h, acc_d, hbg_ref):
    pre = dot(normed, wh[...]) + bias
    below = 0.5 + 0.5 * lax.erf(pre * 0.7071067811865476)
    act = (pre * below).astype(BF)
    slope = below + pre * (jnp.exp(-0.5 * pre * pre) * 0.3989422804014327)
    grad = (dot(cot, wd[...]) * slope).astype(BF)
    acc_h[...] += dot(normed.T, grad)
    acc_d[...] += dot(cot.T, act)
    hbg_ref[...] += jnp.sum(grad.astype(F32), axis=0, keepdims=True)
    return dot(act, wd[...], NT), dot(grad, wh[...], NT)


def fill(x, rows, own, oth, wh, wd, acc_h, acc_d, hbg_ref):
    for z in range(ZS):
        for refs, side in ((own, x), (oth, 1 - x)):
            at = pl.multiple_of((2 * z + side) * rows, 32)
            wh[pl.ds(at, rows), :], wd[pl.ds(at, rows), :] = shard_of(refs, z, rows)
    for ref in (acc_h, acc_d, hbg_ref):
        ref[...] = jnp.zeros_like(ref)


def drain(x, rows, acc, own, oth):
    for z in range(ZS):
        own[z] = acc[pl.ds(pl.multiple_of((2 * z + x) * rows, 32), rows), :].astype(BF)
        oth[z] = acc[pl.ds(pl.multiple_of((2 * z + 1 - x) * rows, 32), rows), :].astype(BF)


def mlp_first_body(
    x_ref, s0, s1, s2, s3, te_ref, a0_ref, a1_ref, c0, c1, c2, c3, vec_ref, w_oo, w_ox,
    mid_ref, normed_ref, ff_ref, gs_ref, hbg_ref, gh_o, gh_x, gd_o, gd_x,
    wh, wd, acc_h, acc_d, *, rows,
):
    x = x_ref[0]

    @pl.when(pl.program_id(0) == 0)
    def _():
        fill(x, rows, (w_oo,), (w_ox,), wh, wd, acc_h, acc_d, hbg_ref)

    middle = (
        pick((s0, s1, s2, s3)).astype(F32)
        + te_ref[...].astype(F32)
        + (a0_ref[...].astype(F32) + a1_ref[...].astype(F32))
        + vec_ref[2:3, :]
    )
    mid_ref[...] = middle
    xhat, _ = normalize(middle)
    normed = (xhat * vec_ref[3:4, :] + vec_ref[4:5, :]).astype(BF)
    normed_ref[...] = normed
    ff_ref[...], gs_ref[...] = feed(normed, pick((c0, c1, c2, c3)), wh, wd, vec_ref[6:7, :], acc_h, acc_d, hbg_ref)

    @pl.when(pl.program_id(0) == pl.num_programs(0) - 1)
    def _():
        drain(x, rows, acc_h, gh_o, gh_x)
        drain(x, rows, acc_d, gd_o, gd_x)


def mlp_second_body(
    x_ref, normed_ref, c0, c1, c2, c3, vec_ref, f_ref, g_ref, w_yo, h_yx, d_yx,
    ff0_ref, ff1_ref, gs_ref, hbg_ref, gh_o, gh_x, gd_o, gd_x,
    wh, wd, acc_h, acc_d, *, rows,
):
    x = x_ref[0]

    @pl.when(pl.program_id(0) == 0)
    def _():
        fill(x, rows, (w_yo,), (h_yx, d_yx), wh, wd, acc_h, acc_d, hbg_ref)

    ff, gs = feed(normed_ref[...], pick((c0, c1, c2, c3)), wh, wd, vec_ref[6:7, :], acc_h, acc_d, hbg_ref)
    gs_ref[...] = (g_ref[...] + gs).astype(BF)
    ff = (f_ref[...] + ff).astype(BF)
    half = pl.num_programs(0) // 2

    @pl.when(pl.program_id(0) < half)
    def _():
        ff0_ref[...] = ff

    @pl.when(pl.program_id(0) >= half)
    def _():
        ff1_ref[...] = ff

    @pl.when(pl.program_id(0) == pl.num_programs(0) - 1)
    def _():
        drain(x, rows, acc_h, gh_o, gh_x)
        drain(x, rows, acc_d, gd_o, gd_x)


def second_back_body(mid_ref, g0_ref, g1_ref, c0, c1, c2, c3, vec_ref, w0_ref, w1_ref, m0_ref, m1_ref, gm_ref, x0_ref, x1_ref, wo0_ref, wo1_ref, sum_ref, wo_ref, acc):
    step, last = pl.program_id(0), pl.num_programs(0) - 1

    @pl.when(step == 0)
    def _():
        wo_ref[...] = jnp.concatenate([w0_ref[:, 576:], w1_ref[:, 576:]], axis=1)
        acc[...] = jnp.zeros_like(acc)
        sum_ref[...] = jnp.zeros_like(sum_ref)

    xhat, rate = normalize(mid_ref[...])
    second = g0_ref[...].astype(F32) + g1_ref[...].astype(F32)
    cot = pick((c0, c1, c2, c3)).astype(F32)
    scaled = second * vec_ref[3:4, :]
    inner = jnp.mean(scaled * xhat, axis=-1, keepdims=True)
    grad = cot + rate * (scaled - jnp.mean(scaled, axis=-1, keepdims=True) - xhat * inner)
    gm_ref[...] = grad
    sum_ref[0:1, :] += jnp.sum(second * xhat, axis=0, keepdims=True)
    sum_ref[1:2, :] += jnp.sum(second, axis=0, keepdims=True)
    sum_ref[2:3, :] += jnp.sum(grad, axis=0, keepdims=True)
    sum_ref[3:4, :] += jnp.sum(cot, axis=0, keepdims=True)
    low = grad.astype(BF)
    back = dot(low, wo_ref[...]).astype(BF).T
    x0_ref[...] = back[:192]
    x1_ref[...] = back[192:]
    mixed = jnp.concatenate([m0_ref[...], m1_ref[...]], axis=0)
    acc[...] += dot(low.T, mixed, NT)

    @pl.when(step == last)
    def _():
        wo0_ref[...] = acc[:, :192].astype(BF)
        wo1_ref[...] = acc[:, 192:].astype(BF)


def project_back_body(x_ref, q_ref, k_ref, v_ref, nt_ref, w_ref, wo_ref, *refs, rows, more):
    refs = list(refs)
    prev_ref = refs.pop(0) if more else None
    own_ref, oth_ref, first_ref, sum_ref, acc = refs
    step, last = pl.program_id(0), pl.num_programs(0) - 1
    x = x_ref[0]
    grads = jnp.concatenate([r[h] for r in (q_ref, k_ref, v_ref) for h in range(3)], axis=1)
    made = dot(nt_ref[...], grads)
    total = jnp.sum(grads.astype(F32), axis=0, keepdims=True)

    @pl.when(step == 0)
    def _():
        acc[...] = made
        sum_ref[...] = total

    @pl.when(step > 0)
    def _():
        acc[...] += made
        sum_ref[...] += total

    back = dot(grads, w_ref[:, :576], NT)
    if more:
        back = back + prev_ref[...]
    first_ref[...] = back.astype(first_ref.dtype)

    @pl.when(step == last)
    def _():
        for z in range(ZS):
            for ref, side in ((own_ref, x), (oth_ref, 1 - x)):
                at = pl.multiple_of((2 * z + side) * rows, 32)
                ref[z] = jnp.concatenate(
                    [acc[pl.ds(at, rows), :].astype(BF), wo_ref[pl.ds(at, rows), :]], axis=1
                )


def first_back_body(
    x_ref, s0, s1, s2, s3, te_ref, vec_ref, g0_ref, g1_ref, gm_ref, second_ref, ho_ref, hy_ref, qo_ref, qy_ref,
    out_ref, own_ref, oth_ref, sum_ref, *, rows,
):
    @pl.when(pl.program_id(0) == 0)
    def _():
        sum_ref[...] = jnp.zeros_like(sum_ref)

    xhat, rate = normalize(pick((s0, s1, s2, s3)).astype(F32) + te_ref[...].astype(F32))
    first = g0_ref[...].astype(F32) + g1_ref[...].astype(F32)
    scaled = first * vec_ref[0:1, :]
    inner = jnp.mean(scaled * xhat, axis=-1, keepdims=True)
    grad = gm_ref[...] + rate * (scaled - jnp.mean(scaled, axis=-1, keepdims=True) - xhat * inner)
    out_ref[...] = grad.astype(BF)
    sum_ref[0:1, :] += jnp.sum(first * xhat, axis=0, keepdims=True)
    sum_ref[1:2, :] += jnp.sum(first, axis=0, keepdims=True)
    sum_ref[2:3, :] += jnp.sum(grad, axis=0, keepdims=True)

    @pl.when(pl.program_id(0) == pl.num_programs(0) - 1)
    def _():
        n = rows // 4
        sums = sum_ref[0:3, :]
        shared = [sums[0:2], second_ref[2:3, :], second_ref[0:2, :], second_ref[3:4, :]]
        blank = jnp.zeros((1, rows - 2 * n), F32)
        for hidden, bias, ref, more in ((ho_ref, qo_ref, own_ref, []), (hy_ref, qy_ref, oth_ref, [sums[2:3]])):
            made = []
            kinds = jnp.concatenate(shared + [hidden[...]], axis=0)
            extra = jnp.concatenate(more + [jnp.zeros((KINDS - 1, kinds.shape[1]), F32)], axis=0) if more else None
            for k in range(ZS * XS):
                part = slice(k * rows, k * rows + rows)
                last = [bias[0:1, k * n : k * n + n], bias[0:1, 6 * HD + k * n : 6 * HD + k * n + n], blank]
                piece = [kinds[:, part], jnp.concatenate(last, axis=1)]
                made.append(jnp.concatenate(piece + ([extra[:, part]] if more else []), axis=0))
            for z in range(ZS):
                even, odd = made[2 * z], made[2 * z + 1]
                ref[0, z] = jnp.where(x_ref[0] == 0, even, odd)
                ref[1, z] = jnp.where(x_ref[0] == 0, odd, even)


def final_body(got_ref, p0_ref, p1_ref, p2_ref, p3_ref, q_ref, k_ref, v_ref, o_ref, *small, rows):
    total = got_ref[0].astype(F32)
    for z in range(1, got_ref.shape[0]):
        total = total + got_ref[z].astype(F32)
    width = 3 * HD
    q_ref[...] = total[:, :width]
    k_ref[...] = total[:, width : 2 * width]
    v_ref[...] = total[:, 2 * width : 3 * width]
    o_ref[...] = total[:, 3 * width :].T
    sums = (p0_ref[...] + p1_ref[...]) + (p2_ref[...] + p3_ref[...])
    n = rows // 4
    for k, ref in enumerate(small[:7]):
        ref[...] = sums[k : k + 1]
    small[7][...] = sums[7:8, :n]
    small[8][...] = sums[7:8, n : 2 * n]


def output_body(mid_ref, f0_ref, f1_ref, vec_ref, out_ref):
    out_ref[...] = (
        mid_ref[...] + (f0_ref[...].astype(F32) + f1_ref[...].astype(F32)) + vec_ref[5:6, :]
    ).astype(BF)


def swap(size):
    return [(i, size - 1 - i) for i in range(size)]


def to_y(values):
    return lax.ppermute(values, "y", swap(2))


def to_x(values):
    return lax.ppermute(values, "b", swap(2))


def to_core(values):
    return lax.ppermute(values, "c", swap(2))


def spread_z(values):
    return lax.all_to_all(values, "a", 0, 0, tiled=True)


def after(value, *others):
    return lax.optimization_barrier((value, *others))[0]


def body(
    fast,
    inputs,
    time_embed,
    first_gain,
    first_shift,
    query_weight,
    query_bias,
    key_weight,
    value_weight,
    value_bias,
    output_weight,
    output_bias,
    second_gain,
    second_shift,
    hidden_weight,
    hidden_bias,
    down_weight,
    down_bias,
    cotangent,
):
    _, block, width = inputs.shape
    shard = query_weight.shape[0]
    rows = width // (ZS * XS)
    seq = 4 * block
    hidden = hidden_weight.shape[1]
    yi = lax.axis_index("y")
    xi = lax.axis_index("b") if fast else jnp.int32(0)
    x_arr = xi.astype(jnp.int32)[None]

    n_copies = ZS if fast else 1
    (attn_pack,) = call(
        pack_attn_body,
        (1,),
        [kept((shard, hidden // 4))] * 3 + [kept((hidden // 4, shard))] + [kept((1, shard))] * 7 + [kept((1, query_bias.shape[0]))] * 2,
        [(sds((n_copies, shard + KINDS, width), BF), kept((n_copies, shard + KINDS, width)))],
        flops=1e6,
        moved=1e6,
        vmem=56,
    )(
        query_weight, key_weight, value_weight, output_weight,
        *(v[None] for v in (first_gain, first_shift, output_bias, second_gain, second_shift, down_bias, hidden_bias, query_bias, value_bias)),
    )
    (mlp_pack,) = call(
        pack_mlp_body,
        (1,),
        [kept((shard, hidden)), kept((hidden, shard))],
        [(sds((n_copies, 2 * shard, width), BF), kept((n_copies, 2 * shard, width)))],
        flops=1e6,
        moved=2e6,
        vmem=56,
    )(hidden_weight, down_weight)

    def tokens(values):
        stays = lax.dynamic_index_in_dim(values, yi, 0, keepdims=False)
        comes = to_y(lax.dynamic_index_in_dim(values, 1 - yi, 0, keepdims=False))
        return stays, comes

    def with_mate(stays, comes):
        return stays, comes, to_core(stays), to_core(comes)

    inputs, cotangent = lax.optimization_barrier((inputs, cotangent, attn_pack))[:2]
    start, cot = tokens(inputs), tokens(cotangent)
    te = lax.dynamic_index_in_dim(time_embed, yi, 0, keepdims=True)

    if fast:
        attn_oo = spread_z(attn_pack)
        attn_oo, *comes = lax.optimization_barrier((attn_oo, start[1], cot[1]))
        start, cot = with_mate(start[0], comes[0]), with_mate(cot[0], comes[1])
        attn_ox, attn_yo = to_x(attn_oo), to_y(attn_oo)
        mlp_oo = spread_z(mlp_pack)
        attn_yx = to_y(attn_ox)
    else:
        def natural(values):
            full = lax.all_gather(values, ("a", "b"), axis=0, tiled=True)
            full = full.reshape(ZS, XS, rows, width)
            return full[:, 0], full[:, 1]

        gathered = lax.all_gather(attn_pack[0], ("a", "b"), axis=0, tiled=False)
        matrix = gathered[:, :shard].reshape(ZS, XS, rows, width)
        small = gathered[:, shard:, :shard]
        flat = small[:, :7].transpose(1, 0, 2).reshape(7, width)
        n = shard // 4
        bias = [small[:, 7, k * n : k * n + n].reshape(ZS * XS, -1) for k in range(2)]
        bias = jnp.concatenate([*bias, jnp.zeros((ZS * XS, rows - 2 * (rows // 4)), BF)], axis=1)
        small = jnp.concatenate([flat, bias.reshape(1, width)], axis=0)
        small = small.reshape(KINDS, ZS, XS, rows).transpose(1, 2, 0, 3)
        small = jnp.pad(small, ((0, 0), (0, 0), (0, 0), (0, width - rows)))
        matrix = jnp.concatenate([matrix, small], axis=2)
        attn_oo, attn_ox = matrix[:, 0], matrix[:, 1]
        attn_yo, attn_yx = to_y(attn_oo), to_y(attn_ox)
        start, cot = with_mate(*start), with_mate(*cot)
        h_oo, h_ox = natural(mlp_pack[0, :shard])
        d_oo, d_ox = natural(mlp_pack[0, shard:])
        mlp_oo = jnp.concatenate([h_oo, d_oo], axis=1)
        mlp_ox = jnp.concatenate([h_ox, d_ox], axis=1)

    def by(tile):
        return pl.BlockSpec((tile, width), lambda i: (i, 0))

    def by_mate(tile):
        tiles = seq // tile
        return pl.BlockSpec((tile, width), lambda i: ((i + tiles // 2) % tiles, 0))

    def low_half(tile):
        last = seq // tile // 2 - 1
        return pl.BlockSpec((tile, width), lambda i: (jnp.minimum(i, last), 0))

    def high_half(tile):
        first = seq // tile // 2
        return pl.BlockSpec((tile, width), lambda i: (jnp.maximum(i - first, 0), 0))

    blocks = [whole((block, width))] * 4
    row = kept((1, width))
    vecs = kept((KINDS, width))
    square = whole((width, width))
    n_qkv = 9 * HD

    def project(first, source, *shards):
        tile = TILE_PROJECT
        outs = [
            (sds((width, width), BF), kept((width, width))),
            (sds((KINDS, width), F32), vecs),
            (sds((9, seq, HD), BF), pl.BlockSpec((9, tile, HD), lambda i: (0, i, 0))),
        ]
        if first:
            outs += [
                (sds((seq, width), BF), by(tile)),
                (pltpu.HBM((width, seq), BF), pl.BlockSpec((width, tile), lambda i: (0, i))),
            ]
        return call(
            functools.partial(project_body, rows=rows, first=first),
            (seq // tile,),
            [scalar()] + (blocks + [row] if first else [by(tile)]) + [whole(v.shape) for v in shards],
            outs,
            scratch=[pltpu.VMEM((8, n_qkv), F32)],
            flops=2 * seq * width * n_qkv,
            moved=8e6,
        )(x_arr, *source, *shards)

    q_spec = pl.BlockSpec((1, seq, HD), lambda h: (h, 0, 0))
    k_spec = pl.BlockSpec((1, seq, HD), lambda h: (3 + h, 0, 0))
    v_spec = pl.BlockSpec((1, seq, HD), lambda h: (6 + h, 0, 0))
    e_spec = pl.BlockSpec((1, seq, seq), lambda h: (h, 0, 0))
    inv_spec = pl.BlockSpec((1, 1, seq), lambda h: (h, 0, 0))
    t_spec = pl.BlockSpec((1, HD, seq), lambda h: (h, 0, 0))

    def attend(qkv):
        return call(
            attend_body,
            (3,),
            [q_spec, k_spec, v_spec],
            [
                (pltpu.HBM((3, seq, seq), BF), e_spec),
                (sds((3, 1, seq), F32), inv_spec),
                (sds((3, HD, seq), BF), t_spec),
                (pltpu.HBM((3, HD, seq), F32), t_spec),
            ],
            flops=3 * 16 * seq * seq * HD,
            moved=8e6,
            trans=3 * seq * seq,
        )(qkv, qkv, qkv)

    def attend_back(qkv, expon, inverse, mixed, grad_mixed):
        return call(
            attend_back_body,
            (3,),
            [q_spec, k_spec, v_spec, e_spec, inv_spec, t_spec, t_spec],
            [(sds((3, seq, HD), BF), q_spec)] * 3,
            flops=3 * 40 * seq * seq * HD,
            moved=9e6,
        )(qkv, qkv, qkv, far(expon), inverse, far(mixed), grad_mixed)

    w_o, vec, qkv_o, normed, normed_t = project(True, (*start, te), attn_oo, attn_ox)
    exp_o, inv_o, mixed_o, wide_o = attend(qkv_o)
    normed, exp_o, attn_yo, attn_yx, mlp_oo = lax.optimization_barrier(
        (normed, exp_o, attn_yo, attn_yx, mlp_oo)
    )
    mlp_yo = to_y(mlp_oo)
    if fast:
        mlp_ox = to_x(mlp_oo)
    w_y, vec_y, qkv_y = project(False, (normed,), attn_yo, attn_yx)
    exp_y, inv_y, mixed_y, wide_y = attend(qkv_y)
    mixed_y, mlp_ox, mlp_yo = lax.optimization_barrier((mixed_y, mlp_ox, mlp_yo))
    h_yx = to_y(mlp_ox[:, :rows])
    d_yx = to_x(mlp_yo[:, rows:]) if fast else to_y(mlp_ox[:, rows:])

    tile = TILE_OUT
    half_t = pl.BlockSpec((3 * HD, tile), lambda i: (0, i))
    flat_o, flat_y = mixed_o.reshape(3 * HD, seq), mixed_y.reshape(3 * HD, seq)
    (attended,) = call(
        outproj_body,
        (seq // tile,),
        [half_t, half_t, square, square],
        [(sds((seq, width), BF), by(tile))],
        scratch=[pltpu.VMEM((width, 6 * HD), BF)],
        flops=2 * seq * width * 384,
        moved=6e6,
    )(flat_o, flat_y, w_o, w_y)
    attended_mate = to_core(attended)

    tile = TILE_MLP
    part = (ZS, rows, hidden)
    grad_parts = [(sds((1, hidden), F32), kept((1, hidden)))] + [(sds(part, BF), kept(part))] * 4
    mlp_scratch = [pltpu.VMEM((width, hidden), t) for t in (BF, BF, F32, F32)]
    mlp_cost = dict(flops=12 * seq * width * hidden, moved=16e6, trans=seq * hidden * 2)
    middle, normed_second, ff_part, gs_part, hb_o, gh_oo, gh_ox, gd_oo, gd_ox = call(
        functools.partial(mlp_first_body, rows=rows),
        (seq // tile,),
        [scalar(), *blocks, row, by(tile), by_mate(tile), *blocks, vecs]
        + [whole((ZS, 2 * rows, hidden))] * 2,
        [
            (sds((seq, width), F32), by(tile)),
            (sds((seq, width), BF), by(tile)),
            (sds((seq, width), F32), by(tile)),
            (sds((seq, width), F32), by(tile)),
        ]
        + grad_parts,
        scratch=mlp_scratch,
        **mlp_cost,
    )(x_arr, *start, te, attended, attended_mate, *cot, vec, mlp_oo, mlp_ox)
    if fast:
        got_ho = to_x(gh_ox)
        normed_second, h_yx, d_yx = lax.optimization_barrier((normed_second, h_yx, d_yx))
    ff, ff_sent, gs, hb_y, gh_yo, gh_yx, gd_yo, gd_yx = call(
        functools.partial(mlp_second_body, rows=rows),
        (seq // tile,),
        [scalar(), by(tile), *blocks, vecs, by(tile), by(tile)]
        + [whole((ZS, 2 * rows, hidden)), whole(part), whole(part)],
        [
            (sds((seq // 2, width), BF), low_half(tile)),
            (sds((seq // 2, width), BF), high_half(tile)),
            (sds((seq, width), BF), by(tile)),
        ]
        + grad_parts,
        scratch=mlp_scratch,
        **mlp_cost,
    )(x_arr, normed_second, *cot, vec_y, ff_part, gs_part, mlp_yo, h_yx, d_yx)
    if fast:
        gs, got_ho = lax.optimization_barrier((gs, got_ho))
    gs_mate = to_core(gs)
    ff_mate = to_core(ff_sent)

    tile = TILE_SECOND
    half_t = pl.BlockSpec((3 * HD, tile), lambda i: (0, i))
    grad_middle, gx_o, gx_y, wo_o, wo_y, second_sums = call(
        second_back_body,
        (seq // tile,),
        [by(tile), by(tile), by_mate(tile), *blocks, vecs, square, square, half_t, half_t],
        [
            (pltpu.HBM((seq, width), F32), by(tile)),
            (sds((3 * HD, seq), BF), half_t),
            (sds((3 * HD, seq), BF), half_t),
            (sds((width, 3 * HD), BF), kept((width, 3 * HD))),
            (sds((width, 3 * HD), BF), kept((width, 3 * HD))),
            (sds((KINDS, width), F32), vecs),
        ],
        scratch=[pltpu.VMEM((width, 6 * HD), BF), pltpu.VMEM((width, 6 * HD), F32)],
        flops=4 * seq * width * 384,
        moved=16e6,
    )(middle, gs, gs_mate, *cot, vec, w_o, w_y, flat_o, flat_y)
    if fast:
        got_h, got_d = to_x(gh_yx), to_y(gd_yx)
        gx_y, got_h, got_d, gd_yo = lax.optimization_barrier((gx_y, got_h, got_d, gd_yo))
        got_hs, got_ds = to_y(gh_yo + got_h), to_x(gd_ox + got_d)

    def project_back(grads, weights, wo, prev):
        tile = TILE_BACK
        more = prev is not None
        heads = pl.BlockSpec((3, tile, HD), lambda i: (0, i, 0))
        attn_part = (ZS, rows, width)
        return call(
            functools.partial(project_back_body, rows=rows, more=more),
            (seq // tile,),
            [scalar(), heads, heads, heads, pl.BlockSpec((width, tile), lambda i: (0, i)), square, whole((width, 3 * HD))]
            + ([by(tile)] if more else []),
            [
                (sds(attn_part, BF), kept(attn_part)),
                (sds(attn_part, BF), kept(attn_part)),
                ((sds((seq, width), BF) if more else pltpu.HBM((seq, width), F32)), by(tile)),
                (sds((1, n_qkv), F32), kept((1, n_qkv))),
            ],
            scratch=[pltpu.VMEM((width, n_qkv), F32)],
            flops=4 * seq * width * n_qkv,
            moved=10e6,
        )(x_arr, *grads, far(normed_t), weights, wo, *((far(prev),) if more else ()))

    grads_y = attend_back(qkv_y, exp_y, inv_y, wide_y, gx_y.reshape(3, HD, seq))
    if fast:
        *grads_y, gd_yo = lax.optimization_barrier((*grads_y, gd_yo))
        got_do = to_y(gd_yo)
    ga_yo, ga_yx, first_part, qkv_sum_y = project_back(grads_y, w_y, wo_y, None)
    tile = TILE_OUT
    (out_tokens,) = call(
        output_body,
        (seq // tile // 2,),
        [by(tile), by(tile), by(tile), vecs],
        [(sds((seq // 2, width), BF), by(tile))],
        flops=1e6,
        moved=5e6,
    )(middle, ff, ff_mate, vec)
    gx_o, first_part, out_tokens = lax.optimization_barrier((gx_o, first_part, out_tokens))
    out_got = to_y(out_tokens[block:])
    if fast:
        gx_o, ga_yx, got_hs = lax.optimization_barrier((gx_o, ga_yx, got_hs))
        ga_d = to_x(ga_yx)
    grads_o = attend_back(qkv_o, exp_o, inv_o, wide_o, gx_o.reshape(3, HD, seq))
    if fast:
        *grads_o, got_ds, got_do, ga_d, out_got = lax.optimization_barrier(
            (*grads_o, got_ds, got_do, ga_d, out_got)
        )
        mlp_all = spread_z(jnp.concatenate([gh_oo + got_ho + got_hs, gd_oo + got_do + got_ds], axis=1))
        ga_s = to_y(ga_yo + ga_d)
    ga_oo, ga_ox, first, qkv_sum_o = project_back(grads_o, w_o, wo_o, first_part)
    if fast:
        ga_x = to_x(ga_ox)
        first, ga_s = lax.optimization_barrier((first, ga_s))
    first_mate = to_core(first)

    tile = TILE_FIRST
    hb_spec, qkv_spec = kept((1, hidden)), kept((1, n_qkv))
    small_o_shape, small_y_shape = (XS, ZS, KINDS, rows), (XS, ZS, 2 * KINDS, rows)
    input_grad, small_o, small_y, first_sums = call(
        functools.partial(first_back_body, rows=rows),
        (seq // tile,),
        [scalar(), *blocks, row, vecs, by(tile), by_mate(tile), by(tile), vecs, hb_spec, hb_spec, qkv_spec, qkv_spec],
        [
            (sds((seq, width), BF), by(tile)),
            (sds(small_o_shape, F32), kept(small_o_shape)),
            (sds(small_y_shape, F32), kept(small_y_shape)),
            (sds((KINDS, width), F32), vecs),
        ],
        flops=1e6,
        moved=12e6,
    )(x_arr, *start, te, vec, first, first_mate, far(grad_middle), second_sums, hb_o, hb_y, qkv_sum_o, qkv_sum_y)

    if fast:
        small_o, small_y, input_grad, ga_x = lax.optimization_barrier((small_o, small_y, input_grad, ga_x))
        ga_all = spread_z(ga_oo + ga_s + ga_x)
    small_got = to_y(small_y)
    small_sum = small_o + small_got[:, :, :KINDS]
    embed = first_sums[2]
    embed_got = jnp.where(xi == 0, small_got, small_got[::-1])[:, :, KINDS].transpose(1, 0, 2).reshape(width)
    embed_gradient = jnp.where(yi == 0, jnp.stack([embed, embed_got]), jnp.stack([embed_got, embed]))
    n_bias = query_bias.shape[0]
    n_head = query_weight.shape[1]
    if fast:
        small_sum = small_sum[0] + to_x(small_sum[1])
        zi = lax.axis_index("a")
        pieces = [lax.dynamic_index_in_dim(small_sum, (zi + k) % ZS, 0, keepdims=False) for k in range(ZS)]
        pieces = [lax.ppermute(v, "a", [(i, (i + k) % ZS) for i in range(ZS)]) if k else v for k, v in enumerate(pieces)]
        *weights, fg, fs, ob, sg, ss, db, hb, qb, vb = call(
            functools.partial(final_body, rows=rows),
            (1,),
            [kept(ga_all.shape)] + [kept((KINDS, rows))] * ZS,
            [(sds((shard, n_head), F32), kept((shard, n_head)))] * 3
            + [(sds((n_head, shard), F32), kept((n_head, shard)))]
            + [(sds((1, shard), F32), kept((1, shard)))] * 7
            + [(sds((1, n_bias), F32), kept((1, n_bias)))] * 2,
            flops=1e6,
            moved=2e6,
        )(ga_all, *pieces)
        vectors = [v[0] for v in (fg, fs, ob, sg, ss, db, hb, qb, vb)]
        mlp_sum = jnp.sum(mlp_all.astype(F32), axis=0)
        gh, gd = mlp_sum[:shard], mlp_sum[shard:].T
    else:

        def scatter(values):
            return lax.psum_scatter(values, ("a", "b"), scatter_dimension=0, tiled=True)

        def scatter_slow(oo, ox, yo, yx):
            own, oth = oo + to_y(yo), ox + to_y(yx)
            return scatter(jnp.stack([own, oth], axis=1).reshape(width, -1).astype(F32))

        kinds = small_sum.transpose(2, 1, 0, 3)
        bias = kinds[7].reshape(ZS * XS, rows)
        split = rows // 4
        vectors = [scatter(v) for v in kinds[:7].reshape(7, width)]
        vectors += [scatter(bias[:, k * split : k * split + split].reshape(-1)) for k in range(2)]
        gh = scatter_slow(gh_oo, gh_ox, gh_yo, gh_yx)
        gd = scatter_slow(gd_oo, gd_ox, gd_yo, gd_yx).T
        ga = scatter_slow(ga_oo, ga_ox, ga_yo, ga_yx)
        weights = [ga[:, k * n_head : k * n_head + n_head] for k in range(4)]
        weights[3] = weights[3].T

    def placed(stays, got):
        return jnp.where(yi == 0, jnp.stack([stays, got]), jnp.stack([got, stays]))

    block_output = placed(out_tokens[:block], out_got)
    input_gradient = placed(input_grad[:block], to_y(input_grad[block : 2 * block]))

    fg, fs, ob, sg, ss, db, hb, qb, vb = vectors
    return (
        block_output, input_gradient, embed_gradient, fg, fs, weights[0], qb, weights[1], weights[2], vb,
        weights[3], ob, sg, ss, gh, hb, gd, db,
    )


def solution(mesh):
    dp, tensor = mesh.shape["dp"], mesh.shape["tensor"]
    fine = Mesh(mesh.devices.reshape(dp // 2, 2, tensor // 2, 2), ("a", "b", "y", "c"))
    by_dp, by_tensor = ("a", "b"), ("y", "c")
    both = by_tensor + by_dp
    column, matrix, turned = P(by_dp), P(by_dp, by_tensor), P(by_tensor, by_dp)
    seqs = P(by_dp, by_tensor, None)
    return jax.shard_map(
        functools.partial(body, dp == ZS * XS),
        mesh=fine,
        in_specs=(
            seqs, P(by_dp, None), column, column, matrix, P(both), matrix, matrix, P(both), turned,
            column, column, column, matrix, P(both), turned, column, seqs,
        ),
        out_specs=(
            seqs, seqs, P(by_dp, None), column, column, matrix, P(both), matrix, matrix, P(both), turned,
            column, column, column, matrix, P(both), turned, column,
        ),
        check_vma=False,
    )
```

```python
import functools

import jax
import jax.numpy as jnp
from jax import lax
from jax.experimental import pallas as pl
from jax.experimental.pallas import tpu as pltpu
from jax.sharding import Mesh
from jax.sharding import PartitionSpec as P

HD = 64
EPSILON = 1e-05
SCALE = 0.125
BF = jnp.bfloat16
F32 = jnp.float32
ZS, XS = 4, 2
KINDS = 8
HINT = 1.0
TILE_PROJECT = 256
TILE_OUT = 256
TILE_MLP = 256
TILE_SECOND = 256
TILE_BACK = 256
TILE_FIRST = 256

NN = (((1,), (0,)), ((), ()))
NT = (((1,), (1,)), ((), ()))


def dot(left, right, dims=NN):
    return lax.dot_general(left, right, dims, preferred_element_type=F32)


def call(body, grid, ins, outs, scratch=(), flops=0, moved=0, trans=0, vmem=16):
    return pl.pallas_call(
        body,
        grid=grid,
        in_specs=[s for s in ins],
        out_specs=[s for _, s in outs],
        out_shape=[o for o, _ in outs],
        scratch_shapes=list(scratch),
        compiler_params=pltpu.CompilerParams(vmem_limit_bytes=vmem << 20),
        cost_estimate=pl.CostEstimate(flops=int(flops * HINT), bytes_accessed=int(moved * HINT), transcendentals=int(trans * HINT)),
    )


def whole(shape, n=1):
    zeros = (0,) * len(shape)
    return pl.BlockSpec(shape, lambda *_: zeros, pipeline_mode=pl.Buffered(1))


def kept(shape):
    zeros = (0,) * len(shape)
    return pl.BlockSpec(shape, lambda *_: zeros)


def far(values):
    return pltpu.with_memory_space_constraint(values, pltpu.HBM)


def scalar():
    return pl.BlockSpec(memory_space=pltpu.SMEM)


def sds(shape, dtype):
    return jax.ShapeDtypeStruct(shape, dtype)


def shard_of(refs, z, rows):
    parts = [r[z] for r in refs]
    value = parts[0] if len(parts) == 1 else jnp.concatenate(parts, axis=0)
    return value[:rows], value[rows:]


def normalize(values):
    center = values - jnp.mean(values, axis=-1, keepdims=True)
    spread = jnp.mean(center * center, axis=-1, keepdims=True)
    rate = lax.rsqrt(spread + EPSILON)
    return center * rate, rate


def pack_body(q_ref, k_ref, v_ref, o_ref, h_ref, d_ref, fg, fs, ob, sg, ss, db, hb, qb, vb, attn_ref, mlp_ref):
    shard = q_ref.shape[0]
    low = jnp.concatenate([q_ref[...], k_ref[...], v_ref[...], o_ref[...].T], axis=1)
    n = qb.shape[1]
    bias = jnp.concatenate([qb[...], vb[...], jnp.zeros((1, shard - 2 * n), BF)], axis=1)
    small = jnp.concatenate([r[...].astype(F32) for r in (fg, fs, ob, sg, ss, db, hb)] + [bias.astype(F32)], axis=0)
    small = jnp.concatenate([small, jnp.zeros((KINDS, low.shape[1] - shard), F32)], axis=1).astype(BF)
    high, down = h_ref[...], d_ref[...].T
    for z in range(attn_ref.shape[0]):
        attn_ref[z, :shard, :] = low
        attn_ref[z, shard:, :] = small
        mlp_ref[z, :shard, :] = high
        mlp_ref[z, shard:, :] = down


def pick(refs):
    step, each = pl.program_id(0), len(refs) // pl.num_programs(0)
    blocks = [r[...] for r in refs]
    tiles = [blocks[k : k + each] for k in range(0, len(blocks), each)]
    tiles = [t[0] if each == 1 else jnp.concatenate(t, axis=0) for t in tiles]
    value = tiles[0]
    for k in range(1, len(tiles)):
        value = jnp.where(step == k, tiles[k], value)
    return value


def project_body(x_ref, *refs, rows, first):
    refs = list(refs)
    if first:
        *tokens, te_ref, own_ref, oth_ref, w_ref, vec_ref, qkv_ref, normed_ref, normed_t_ref, bias_ref = refs
        oth_refs = (oth_ref,)
    else:
        source_ref, own_ref, *oth_refs, w_ref, vec_ref, qkv_ref, bias_ref = refs

    @pl.when(pl.program_id(0) == 0)
    def _():
        x = x_ref[0]
        own, oth = [], []
        for z in range(ZS):
            weight, small = shard_of((own_ref,), z, rows)
            w_ref[pl.ds(pl.multiple_of((2 * z + x) * rows, 32), rows), :] = weight
            own.append(small[:, :rows].astype(F32))
            weight, small = shard_of(oth_refs, z, rows)
            w_ref[pl.ds(pl.multiple_of((2 * z + 1 - x) * rows, 32), rows), :] = weight
            oth.append(small[:, :rows].astype(F32))
        even = jnp.concatenate([v for pair in zip(own, oth) for v in pair], axis=1)
        odd = jnp.concatenate([v for pair in zip(oth, own) for v in pair], axis=1)
        vec = jnp.where(x == 0, even, odd)
        vec_ref[...] = vec
        n = rows // 4
        last = vec[7:8, :]
        parts = [last[:, rows * k : rows * k + n] for k in range(ZS * XS)]
        parts += [jnp.zeros((1, 3 * HD), F32)]
        parts += [last[:, rows * k + n : rows * k + 2 * n] for k in range(ZS * XS)]
        bias_ref[0:1, :] = jnp.concatenate(parts, axis=1)

    if first:
        xhat, _ = normalize(pick(tokens).astype(F32) + te_ref[...].astype(F32))
        normed = (xhat * vec_ref[0:1, :] + vec_ref[1:2, :]).astype(BF)
        normed_ref[...] = normed
        normed_t_ref[...] = normed.T
    else:
        normed = source_ref[...]
    made = dot(normed, w_ref[:, :640])[:, :576] + bias_ref[0:1, :]
    made = made.astype(BF)
    for j in range(9):
        piece = made[:, 64 * j : 64 * j + 64]
        qkv_ref[j] = piece * BF(SCALE) if j < 3 else piece


def attend_body(q_ref, k_ref, v_ref, e_ref, inv_ref, mixed_ref, wide_ref):
    scores = dot(k_ref[0], q_ref[0], NT)
    expon = jnp.exp(scores - jnp.max(scores, axis=0, keepdims=True))
    inverse = 1.0 / jnp.sum(expon, axis=0, keepdims=True)
    low = expon.astype(BF)
    e_ref[0] = low
    inv_ref[0] = inverse
    wide = dot(v_ref[0].T, low) * inverse
    mixed_ref[0] = wide.astype(BF)
    wide_ref[0] = wide


def attend_back_body(q_ref, k_ref, v_ref, e_ref, inv_ref, mixed_ref, gm_ref, dq_ref, dk_ref, dv_ref):
    low = (gm_ref[0].astype(F32) * inv_ref[0]).astype(BF)
    inner = jnp.sum(low.astype(F32) * mixed_ref[0], axis=0, keepdims=True)
    expon = e_ref[0]
    grad_scores = (expon.astype(F32) * (dot(v_ref[0], low) - inner)).astype(BF)
    dv_ref[0] = dot(expon, low, NT).astype(BF)
    dk_ref[0] = dot(grad_scores, q_ref[0]).astype(BF)
    dq_ref[0] = (dot(k_ref[0].T, grad_scores) * SCALE).T.astype(BF)


def outproj_body(m0_ref, m1_ref, w0_ref, w1_ref, out_ref, wo_ref):
    @pl.when(pl.program_id(0) == 0)
    def _():
        wo_ref[...] = jnp.concatenate([w0_ref[:, 576:], w1_ref[:, 576:]], axis=1)

    mixed = jnp.concatenate([m0_ref[...], m1_ref[...]], axis=0).T
    out_ref[...] = dot(mixed, wo_ref[...], NT).astype(BF)


def feed(normed, cot, wh, wd, bias, acc_h, acc_d, hbg_ref):
    pre = dot(normed, wh[...]) + bias
    below = 0.5 + 0.5 * lax.erf(pre * 0.7071067811865476)
    act = (pre * below).astype(BF)
    slope = below + pre * (jnp.exp(-0.5 * pre * pre) * 0.3989422804014327)
    grad = (dot(cot, wd[...]) * slope).astype(BF)
    acc_h[...] += dot(normed.T, grad)
    acc_d[...] += dot(cot.T, act)
    hbg_ref[...] += jnp.sum(grad.astype(F32), axis=0, keepdims=True)
    return dot(act, wd[...], NT), dot(grad, wh[...], NT)


def fill(x, rows, own, oth, wh, wd, acc_h, acc_d, hbg_ref):
    for z in range(ZS):
        for refs, side in ((own, x), (oth, 1 - x)):
            at = pl.multiple_of((2 * z + side) * rows, 32)
            wh[pl.ds(at, rows), :], wd[pl.ds(at, rows), :] = shard_of(refs, z, rows)
    for ref in (acc_h, acc_d, hbg_ref):
        ref[...] = jnp.zeros_like(ref)


def drain(x, rows, acc, own, oth):
    for z in range(ZS):
        own[z] = acc[pl.ds(pl.multiple_of((2 * z + x) * rows, 32), rows), :].astype(BF)
        oth[z] = acc[pl.ds(pl.multiple_of((2 * z + 1 - x) * rows, 32), rows), :].astype(BF)


def mlp_first_body(
    x_ref, s0, s1, s2, s3, te_ref, a0_ref, a1_ref, c0, c1, c2, c3, vec_ref, w_oo, w_ox,
    mid_ref, normed_ref, ff_ref, gs_ref, hbg_ref, gh_o, gh_x, gd_o, gd_x,
    wh, wd, acc_h, acc_d, *, rows,
):
    x = x_ref[0]

    @pl.when(pl.program_id(0) == 0)
    def _():
        fill(x, rows, (w_oo,), (w_ox,), wh, wd, acc_h, acc_d, hbg_ref)

    middle = (
        pick((s0, s1, s2, s3)).astype(F32)
        + te_ref[...].astype(F32)
        + (a0_ref[...].astype(F32) + a1_ref[...].astype(F32))
        + vec_ref[2:3, :]
    )
    mid_ref[...] = middle
    xhat, _ = normalize(middle)
    normed = (xhat * vec_ref[3:4, :] + vec_ref[4:5, :]).astype(BF)
    normed_ref[...] = normed
    ff_ref[...], gs_ref[...] = feed(normed, pick((c0, c1, c2, c3)), wh, wd, vec_ref[6:7, :], acc_h, acc_d, hbg_ref)

    @pl.when(pl.program_id(0) == pl.num_programs(0) - 1)
    def _():
        drain(x, rows, acc_h, gh_o, gh_x)
        drain(x, rows, acc_d, gd_o, gd_x)


def mlp_second_body(
    x_ref, normed_ref, c0, c1, c2, c3, vec_ref, f_ref, g_ref, w_yo, h_yx, d_yx,
    ff0_ref, ff1_ref, gs_ref, hbg_ref, gh_o, gh_x, gd_o, gd_x,
    wh, wd, acc_h, acc_d, *, rows,
):
    x = x_ref[0]

    @pl.when(pl.program_id(0) == 0)
    def _():
        fill(x, rows, (w_yo,), (h_yx, d_yx), wh, wd, acc_h, acc_d, hbg_ref)

    ff, gs = feed(normed_ref[...], pick((c0, c1, c2, c3)), wh, wd, vec_ref[6:7, :], acc_h, acc_d, hbg_ref)
    gs_ref[...] = (g_ref[...] + gs).astype(BF)
    ff = (f_ref[...] + ff).astype(BF)
    half = pl.num_programs(0) // 2

    @pl.when(pl.program_id(0) < half)
    def _():
        ff0_ref[...] = ff

    @pl.when(pl.program_id(0) >= half)
    def _():
        ff1_ref[...] = ff

    @pl.when(pl.program_id(0) == pl.num_programs(0) - 1)
    def _():
        drain(x, rows, acc_h, gh_o, gh_x)
        drain(x, rows, acc_d, gd_o, gd_x)


def second_back_body(mid_ref, g0_ref, g1_ref, c0, c1, c2, c3, vec_ref, w0_ref, w1_ref, m0_ref, m1_ref, gm_ref, x0_ref, x1_ref, wo0_ref, wo1_ref, sum_ref, wo_ref, acc):
    step, last = pl.program_id(0), pl.num_programs(0) - 1

    @pl.when(step == 0)
    def _():
        wo_ref[...] = jnp.concatenate([w0_ref[:, 576:], w1_ref[:, 576:]], axis=1)
        acc[...] = jnp.zeros_like(acc)
        sum_ref[...] = jnp.zeros_like(sum_ref)

    xhat, rate = normalize(mid_ref[...])
    second = g0_ref[...].astype(F32) + g1_ref[...].astype(F32)
    cot = pick((c0, c1, c2, c3)).astype(F32)
    scaled = second * vec_ref[3:4, :]
    inner = jnp.mean(scaled * xhat, axis=-1, keepdims=True)
    grad = cot + rate * (scaled - jnp.mean(scaled, axis=-1, keepdims=True) - xhat * inner)
    gm_ref[...] = grad
    sum_ref[0:1, :] += jnp.sum(second * xhat, axis=0, keepdims=True)
    sum_ref[1:2, :] += jnp.sum(second, axis=0, keepdims=True)
    sum_ref[2:3, :] += jnp.sum(grad, axis=0, keepdims=True)
    sum_ref[3:4, :] += jnp.sum(cot, axis=0, keepdims=True)
    low = grad.astype(BF)
    back = dot(low, wo_ref[...]).astype(BF).T
    x0_ref[...] = back[:192]
    x1_ref[...] = back[192:]
    mixed = jnp.concatenate([m0_ref[...], m1_ref[...]], axis=0)
    acc[...] += dot(low.T, mixed, NT)

    @pl.when(step == last)
    def _():
        wo0_ref[...] = acc[:, :192].astype(BF)
        wo1_ref[...] = acc[:, 192:].astype(BF)


def project_back_body(x_ref, q_ref, k_ref, v_ref, nt_ref, w_ref, wo_ref, *refs, rows, more):
    refs = list(refs)
    prev_ref = refs.pop(0) if more else None
    own_ref, oth_ref, first_ref, sum_ref, acc = refs
    step, last = pl.program_id(0), pl.num_programs(0) - 1
    x = x_ref[0]
    grads = jnp.concatenate([r[h] for r in (q_ref, k_ref, v_ref) for h in range(3)], axis=1)
    made = dot(nt_ref[...], grads)
    total = jnp.sum(grads.astype(F32), axis=0, keepdims=True)

    @pl.when(step == 0)
    def _():
        acc[...] = made
        sum_ref[...] = total

    @pl.when(step > 0)
    def _():
        acc[...] += made
        sum_ref[...] += total

    back = dot(grads, w_ref[:, :576], NT)
    if more:
        back = back + prev_ref[...]
    first_ref[...] = back.astype(first_ref.dtype)

    @pl.when(step == last)
    def _():
        for z in range(ZS):
            for ref, side in ((own_ref, x), (oth_ref, 1 - x)):
                at = pl.multiple_of((2 * z + side) * rows, 32)
                ref[z] = jnp.concatenate(
                    [acc[pl.ds(at, rows), :].astype(BF), wo_ref[pl.ds(at, rows), :]], axis=1
                )


def first_back_body(
    x_ref, s0, s1, s2, s3, te_ref, vec_ref, g0_ref, g1_ref, gm_ref, second_ref, ho_ref, hy_ref, qo_ref, qy_ref,
    out_ref, own_ref, oth_ref, sum_ref, *, rows,
):
    @pl.when(pl.program_id(0) == 0)
    def _():
        sum_ref[...] = jnp.zeros_like(sum_ref)

    xhat, rate = normalize(pick((s0, s1, s2, s3)).astype(F32) + te_ref[...].astype(F32))
    first = g0_ref[...].astype(F32) + g1_ref[...].astype(F32)
    scaled = first * vec_ref[0:1, :]
    inner = jnp.mean(scaled * xhat, axis=-1, keepdims=True)
    grad = gm_ref[...] + rate * (scaled - jnp.mean(scaled, axis=-1, keepdims=True) - xhat * inner)
    out_ref[...] = grad.astype(BF)
    sum_ref[0:1, :] += jnp.sum(first * xhat, axis=0, keepdims=True)
    sum_ref[1:2, :] += jnp.sum(first, axis=0, keepdims=True)
    sum_ref[2:3, :] += jnp.sum(grad, axis=0, keepdims=True)

    @pl.when(pl.program_id(0) == pl.num_programs(0) - 1)
    def _():
        n = rows // 4
        sums = sum_ref[0:3, :]
        shared = [sums[0:2], second_ref[2:3, :], second_ref[0:2, :], second_ref[3:4, :]]
        blank = jnp.zeros((1, rows - 2 * n), F32)
        for hidden, bias, ref, more in ((ho_ref, qo_ref, own_ref, []), (hy_ref, qy_ref, oth_ref, [sums[2:3]])):
            made = []
            kinds = jnp.concatenate(shared + [hidden[...]], axis=0)
            extra = jnp.concatenate(more + [jnp.zeros((KINDS - 1, kinds.shape[1]), F32)], axis=0) if more else None
            for k in range(ZS * XS):
                part = slice(k * rows, k * rows + rows)
                last = [bias[0:1, k * n : k * n + n], bias[0:1, 6 * HD + k * n : 6 * HD + k * n + n], blank]
                piece = [kinds[:, part], jnp.concatenate(last, axis=1)]
                made.append(jnp.concatenate(piece + ([extra[:, part]] if more else []), axis=0))
            for z in range(ZS):
                even, odd = made[2 * z], made[2 * z + 1]
                ref[0, z] = jnp.where(x_ref[0] == 0, even, odd)
                ref[1, z] = jnp.where(x_ref[0] == 0, odd, even)


def final_body(got_ref, p0_ref, p1_ref, p2_ref, p3_ref, q_ref, k_ref, v_ref, o_ref, *small, rows):
    total = got_ref[0].astype(F32)
    for z in range(1, got_ref.shape[0]):
        total = total + got_ref[z].astype(F32)
    width = 3 * HD
    q_ref[...] = total[:, :width]
    k_ref[...] = total[:, width : 2 * width]
    v_ref[...] = total[:, 2 * width : 3 * width]
    o_ref[...] = total[:, 3 * width :].T
    sums = (p0_ref[...] + p1_ref[...]) + (p2_ref[...] + p3_ref[...])
    n = rows // 4
    for k, ref in enumerate(small[:7]):
        ref[...] = sums[k : k + 1]
    small[7][...] = sums[7:8, :n]
    small[8][...] = sums[7:8, n : 2 * n]


def output_body(mid_ref, f0_ref, f1_ref, vec_ref, out_ref):
    out_ref[...] = (
        mid_ref[...] + (f0_ref[...].astype(F32) + f1_ref[...].astype(F32)) + vec_ref[5:6, :]
    ).astype(BF)


def swap(size):
    return [(i, size - 1 - i) for i in range(size)]


def to_y(values):
    return lax.ppermute(values, "y", swap(2))


def to_x(values):
    return lax.ppermute(values, "b", swap(2))


def to_core(values):
    return lax.ppermute(values, "c", swap(2))


def spread_z(values):
    return lax.all_to_all(values, "a", 0, 0, tiled=True)


def body(
    fast,
    inputs,
    time_embed,
    first_gain,
    first_shift,
    query_weight,
    query_bias,
    key_weight,
    value_weight,
    value_bias,
    output_weight,
    output_bias,
    second_gain,
    second_shift,
    hidden_weight,
    hidden_bias,
    down_weight,
    down_bias,
    cotangent,
):
    _, block, width = inputs.shape
    shard = query_weight.shape[0]
    rows = width // (ZS * XS)
    seq = 4 * block
    hidden = hidden_weight.shape[1]
    yi = lax.axis_index("y")
    xi = lax.axis_index("b") if fast else jnp.int32(0)
    x_arr = xi.astype(jnp.int32)[None]

    n_copies = ZS if fast else 1
    attn_pack, mlp_pack = call(
        pack_body,
        (1,),
        [kept((shard, hidden // 4))] * 3
        + [kept((hidden // 4, shard)), kept((shard, hidden)), kept((hidden, shard))]
        + [kept((1, shard))] * 7
        + [kept((1, query_bias.shape[0]))] * 2,
        [
            (sds((n_copies, shard + KINDS, width), BF), kept((n_copies, shard + KINDS, width))),
            (sds((n_copies, 2 * shard, width), BF), kept((n_copies, 2 * shard, width))),
        ],
        flops=1e6,
        moved=2e6,
        vmem=56,
    )(
        query_weight, key_weight, value_weight, output_weight, hidden_weight, down_weight,
        *(v[None] for v in (first_gain, first_shift, output_bias, second_gain, second_shift, down_bias, hidden_bias, query_bias, value_bias)),
    )

    inputs, cotangent, attn_pack = lax.optimization_barrier((inputs, cotangent, attn_pack))
    both = jnp.concatenate([inputs, cotangent], axis=1)
    stays = lax.dynamic_index_in_dim(both, yi, 0, keepdims=False)
    comes = to_y(lax.dynamic_index_in_dim(both, 1 - yi, 0, keepdims=False))
    stays_mate = to_core(stays)
    te = lax.dynamic_index_in_dim(time_embed, yi, 0, keepdims=True)

    if fast:
        attn_oo = spread_z(attn_pack)
        attn_oo, comes, stays_mate = lax.optimization_barrier((attn_oo, comes, stays_mate))
        comes_mate = to_core(comes)
        attn_ox, attn_yo = to_x(attn_oo), to_y(attn_oo)
        attn_ox, attn_yo = lax.optimization_barrier((attn_ox, attn_yo))
        mlp_oo = spread_z(mlp_pack)
        attn_yx = (to_y(attn_ox[:, : rows // 2]), to_x(attn_yo[:, rows // 2 :]))
    else:
        def natural(values):
            full = lax.all_gather(values, ("a", "b"), axis=0, tiled=True)
            full = full.reshape(ZS, XS, rows, width)
            return full[:, 0], full[:, 1]

        gathered = lax.all_gather(attn_pack[0], ("a", "b"), axis=0, tiled=False)
        matrix = gathered[:, :shard].reshape(ZS, XS, rows, width)
        small = gathered[:, shard:, :shard]
        flat = small[:, :7].transpose(1, 0, 2).reshape(7, width)
        n = shard // 4
        bias = [small[:, 7, k * n : k * n + n].reshape(ZS * XS, -1) for k in range(2)]
        bias = jnp.concatenate([*bias, jnp.zeros((ZS * XS, rows - 2 * (rows // 4)), BF)], axis=1)
        small = jnp.concatenate([flat, bias.reshape(1, width)], axis=0)
        small = small.reshape(KINDS, ZS, XS, rows).transpose(1, 2, 0, 3)
        small = jnp.pad(small, ((0, 0), (0, 0), (0, 0), (0, width - rows)))
        matrix = jnp.concatenate([matrix, small], axis=2)
        attn_oo, attn_ox = matrix[:, 0], matrix[:, 1]
        attn_yo, attn_yx = to_y(attn_oo), (to_y(attn_ox),)
        comes_mate = to_core(comes)
        h_oo, h_ox = natural(mlp_pack[0, :shard])
        d_oo, d_ox = natural(mlp_pack[0, shard:])
        mlp_oo = jnp.concatenate([h_oo, d_oo], axis=1)
        mlp_ox = jnp.concatenate([h_ox, d_ox], axis=1)

    def by(tile):
        return pl.BlockSpec((tile, width), lambda i: (i, 0))

    def by_mate(tile):
        tiles = seq // tile
        return pl.BlockSpec((tile, width), lambda i: ((i + tiles // 2) % tiles, 0))

    def low_half(tile):
        last = seq // tile // 2 - 1
        return pl.BlockSpec((tile, width), lambda i: (jnp.minimum(i, last), 0))

    def high_half(tile):
        first = seq // tile // 2
        return pl.BlockSpec((tile, width), lambda i: (jnp.maximum(i - first, 0), 0))

    tokens = tuple(far(v) for v in (stays, comes, stays_mate, comes_mate))
    start_blocks = [pl.BlockSpec((block, width), lambda *_: (0, 0), pipeline_mode=pl.Buffered(1))] * 4
    cot_blocks = [pl.BlockSpec((block, width), lambda *_: (1, 0), pipeline_mode=pl.Buffered(1))] * 4
    row = kept((1, width))
    vecs = kept((KINDS, width))
    square = whole((width, width))
    n_qkv = 9 * HD

    def project(first, source, *shards):
        tile = TILE_PROJECT
        outs = [
            (sds((width, width), BF), kept((width, width))),
            (sds((KINDS, width), F32), vecs),
            (pltpu.HBM((9, seq, HD), BF), pl.BlockSpec((9, tile, HD), lambda i: (0, i, 0))),
        ]
        if first:
            outs += [
                (pltpu.HBM((seq, width), BF), by(tile)),
                (pltpu.HBM((width, seq), BF), pl.BlockSpec((width, tile), lambda i: (0, i))),
            ]
        return call(
            functools.partial(project_body, rows=rows, first=first),
            (seq // tile,),
            [scalar()] + (start_blocks + [row] if first else [by(tile)]) + [whole(v.shape) for v in shards],
            outs,
            scratch=[pltpu.VMEM((8, n_qkv), F32)],
            flops=2 * seq * width * n_qkv,
            moved=8e6,
        )(x_arr, *source, *shards)

    q_spec = pl.BlockSpec((1, seq, HD), lambda h: (h, 0, 0))
    k_spec = pl.BlockSpec((1, seq, HD), lambda h: (3 + h, 0, 0))
    v_spec = pl.BlockSpec((1, seq, HD), lambda h: (6 + h, 0, 0))
    e_spec = pl.BlockSpec((1, seq, seq), lambda h: (h, 0, 0))
    inv_spec = pl.BlockSpec((1, 1, seq), lambda h: (h, 0, 0))
    t_spec = pl.BlockSpec((1, HD, seq), lambda h: (h, 0, 0))

    def attend(qkv):
        return call(
            attend_body,
            (3,),
            [q_spec, k_spec, v_spec],
            [
                (pltpu.HBM((3, seq, seq), BF), e_spec),
                (sds((3, 1, seq), F32), inv_spec),
                (sds((3, HD, seq), BF), t_spec),
                (pltpu.HBM((3, HD, seq), F32), t_spec),
            ],
            flops=3 * 16 * seq * seq * HD,
            moved=8e6,
            trans=3 * seq * seq,
        )(*[far(qkv)] * 3)

    def attend_back(qkv, expon, inverse, mixed, grad_mixed):
        return call(
            attend_back_body,
            (3,),
            [q_spec, k_spec, v_spec, e_spec, inv_spec, t_spec, t_spec],
            [(pltpu.HBM((3, seq, HD), BF), q_spec)] * 3,
            flops=3 * 40 * seq * seq * HD,
            moved=9e6,
        )(*[far(qkv)] * 3, far(expon), inverse, far(mixed), grad_mixed)

    w_o, vec, qkv_o, normed, normed_t = project(True, (*tokens, te), attn_oo, attn_ox)
    qkv_o, attn_yx, mlp_oo = lax.optimization_barrier((qkv_o, attn_yx, mlp_oo))
    mlp_yo = to_y(mlp_oo)
    if fast:
        mlp_ox = to_x(mlp_oo)
    exp_o, inv_o, mixed_o, wide_o = attend(qkv_o)
    normed, exp_o = lax.optimization_barrier((normed, exp_o))
    w_y, vec_y, qkv_y = project(False, (far(normed),), attn_yo, *attn_yx)
    exp_y, inv_y, mixed_y, wide_y = attend(qkv_y)
    mixed_y, mlp_ox, mlp_yo = lax.optimization_barrier((mixed_y, mlp_ox, mlp_yo))
    h_yx = to_y(mlp_ox[:, :rows])
    d_yx = to_x(mlp_yo[:, rows:]) if fast else to_y(mlp_ox[:, rows:])

    tile = TILE_OUT
    half_t = pl.BlockSpec((3 * HD, tile), lambda i: (0, i))
    flat_o, flat_y = mixed_o.reshape(3 * HD, seq), mixed_y.reshape(3 * HD, seq)
    (attended,) = call(
        outproj_body,
        (seq // tile,),
        [half_t, half_t, square, square],
        [(sds((seq, width), BF), by(tile))],
        scratch=[pltpu.VMEM((width, 6 * HD), BF)],
        flops=2 * seq * width * 384,
        moved=6e6,
    )(flat_o, flat_y, w_o, w_y)
    attended_mate = to_core(attended)

    tile = TILE_MLP
    part = (ZS, rows, hidden)
    grad_parts = [(sds((1, hidden), F32), kept((1, hidden)))] + [(sds(part, BF), kept(part))] * 4
    mlp_scratch = [pltpu.VMEM((width, hidden), t) for t in (BF, BF, F32, F32)]
    mlp_cost = dict(flops=12 * seq * width * hidden, moved=16e6, trans=seq * hidden * 2)
    middle, normed_second, ff_part, gs_part, hb_o, gh_oo, gh_ox, gd_oo, gd_ox = call(
        functools.partial(mlp_first_body, rows=rows),
        (seq // tile,),
        [scalar(), *start_blocks, row, by(tile), by_mate(tile), *cot_blocks, vecs]
        + [whole((ZS, 2 * rows, hidden))] * 2,
        [
            (sds((seq, width), F32), by(tile)),
            (sds((seq, width), BF), by(tile)),
            (sds((seq, width), F32), by(tile)),
            (sds((seq, width), F32), by(tile)),
        ]
        + grad_parts,
        scratch=mlp_scratch,
        **mlp_cost,
    )(x_arr, *tokens, te, attended, attended_mate, *tokens, vec, mlp_oo, mlp_ox)
    if fast:
        got_ho = to_x(gh_ox)
        normed_second, h_yx, d_yx = lax.optimization_barrier((normed_second, h_yx, d_yx))
    ff, ff_sent, gs, hb_y, gh_yo, gh_yx, gd_yo, gd_yx = call(
        functools.partial(mlp_second_body, rows=rows),
        (seq // tile,),
        [scalar(), by(tile), *cot_blocks, vecs, by(tile), by(tile)]
        + [whole((ZS, 2 * rows, hidden)), whole(part), whole(part)],
        [
            (sds((seq // 2, width), BF), low_half(tile)),
            (sds((seq // 2, width), BF), high_half(tile)),
            (sds((seq, width), BF), by(tile)),
        ]
        + grad_parts,
        scratch=mlp_scratch,
        **mlp_cost,
    )(x_arr, normed_second, *tokens, vec_y, ff_part, gs_part, mlp_yo, h_yx, d_yx)
    if fast:
        gs, got_ho = lax.optimization_barrier((gs, got_ho))
    gs_mate = to_core(gs)
    ff_mate = to_core(ff_sent)

    tile = TILE_SECOND
    half_t = pl.BlockSpec((3 * HD, tile), lambda i: (0, i))
    grad_middle, gx_o, gx_y, wo_o, wo_y, second_sums = call(
        second_back_body,
        (seq // tile,),
        [by(tile), by(tile), by_mate(tile), *cot_blocks, vecs, square, square, half_t, half_t],
        [
            (pltpu.HBM((seq, width), F32), by(tile)),
            (sds((3 * HD, seq), BF), half_t),
            (sds((3 * HD, seq), BF), half_t),
            (pltpu.HBM((width, 3 * HD), BF), kept((width, 3 * HD))),
            (pltpu.HBM((width, 3 * HD), BF), kept((width, 3 * HD))),
            (sds((KINDS, width), F32), vecs),
        ],
        scratch=[pltpu.VMEM((width, 6 * HD), BF), pltpu.VMEM((width, 6 * HD), F32)],
        flops=4 * seq * width * 384,
        moved=16e6,
    )(middle, gs, gs_mate, *tokens, vec, w_o, w_y, flat_o, flat_y)
    if fast:
        got_h, got_d = to_x(gh_yx), to_y(gd_yx)
        gx_y, got_h, got_d = lax.optimization_barrier((gx_y, got_h, got_d))
        got_hs, got_ds = to_y(gh_yo + got_h), to_x(gd_ox + got_d)

    def project_back(grads, weights, wo, prev):
        tile = TILE_BACK
        more = prev is not None
        heads = pl.BlockSpec((3, tile, HD), lambda i: (0, i, 0))
        attn_part = (ZS, rows, width)
        return call(
            functools.partial(project_back_body, rows=rows, more=more),
            (seq // tile,),
            [scalar(), heads, heads, heads, pl.BlockSpec((width, tile), lambda i: (0, i)), square, whole((width, 3 * HD))]
            + ([by(tile)] if more else []),
            [
                (pltpu.HBM(attn_part, BF), kept(attn_part)),
                (pltpu.HBM(attn_part, BF), kept(attn_part)),
                ((sds((seq, width), BF) if more else pltpu.HBM((seq, width), F32)), by(tile)),
                (sds((1, n_qkv), F32), kept((1, n_qkv))),
            ],
            scratch=[pltpu.VMEM((width, n_qkv), F32)],
            flops=4 * seq * width * n_qkv,
            moved=10e6,
        )(x_arr, *(far(v) for v in grads), far(normed_t), weights, far(wo), *((far(prev),) if more else ()))

    grads_y = attend_back(qkv_y, exp_y, inv_y, wide_y, gx_y.reshape(3, HD, seq))
    ga_yo, ga_yx, first_part, qkv_sum_y = project_back(grads_y, w_y, wo_y, None)
    tile = TILE_OUT
    (out_tokens,) = call(
        output_body,
        (seq // tile // 2,),
        [by(tile), by(tile), by(tile), vecs],
        [(sds((seq // 2, width), BF), by(tile))],
        flops=1e6,
        moved=5e6,
    )(middle, ff, ff_mate, vec)
    gx_o, first_part, out_tokens = lax.optimization_barrier((gx_o, first_part, out_tokens))
    out_got = to_y(out_tokens[block:])
    if fast:
        gx_o, ga_yx, got_hs, got_ds, gd_yo = lax.optimization_barrier((gx_o, ga_yx, got_hs, got_ds, gd_yo))
        got_do = to_y(gd_yo)
        ga_d = to_x(ga_yx)
    grads_o = attend_back(qkv_o, exp_o, inv_o, wide_o, gx_o.reshape(3, HD, seq))
    if fast:
        *grads_o, got_do, ga_d = lax.optimization_barrier((*grads_o, got_do, ga_d))
        mlp_all = spread_z(jnp.concatenate([gh_oo + got_ho + got_hs, gd_oo + got_do + got_ds], axis=1))
        ga_s = to_y(ga_yo + ga_d)
    ga_oo, ga_ox, first, qkv_sum_o = project_back(grads_o, w_o, wo_o, first_part)
    if fast:
        ga_x = to_x(ga_ox)
    first_mate = to_core(first)

    tile = TILE_FIRST
    hb_spec, qkv_spec = kept((1, hidden)), kept((1, n_qkv))
    small_o_shape, small_y_shape = (XS, ZS, KINDS, rows), (XS, ZS, 2 * KINDS, rows)
    input_grad, small_o, small_y, first_sums = call(
        functools.partial(first_back_body, rows=rows),
        (seq // tile,),
        [scalar(), *start_blocks, row, vecs, by(tile), by_mate(tile), by(tile), vecs, hb_spec, hb_spec, qkv_spec, qkv_spec],
        [
            (sds((seq, width), BF), by(tile)),
            (sds(small_o_shape, F32), kept(small_o_shape)),
            (sds(small_y_shape, F32), kept(small_y_shape)),
            (sds((KINDS, width), F32), vecs),
        ],
        flops=1e6,
        moved=12e6,
    )(x_arr, *tokens, te, vec, first, first_mate, far(grad_middle), second_sums, hb_o, hb_y, qkv_sum_o, qkv_sum_y)

    if fast:
        input_grad, ga_x, ga_s, mlp_all = lax.optimization_barrier((input_grad, ga_x, ga_s, mlp_all))
        ga_all = spread_z(ga_oo + ga_s + ga_x)
    small_got = to_y(small_y)
    small_sum = small_o + small_got[:, :, :KINDS]
    embed = first_sums[2]
    embed_got = jnp.where(xi == 0, small_got, small_got[::-1])[:, :, KINDS].transpose(1, 0, 2).reshape(width)
    embed_gradient = jnp.where(yi == 0, jnp.stack([embed, embed_got]), jnp.stack([embed_got, embed]))
    n_bias = query_bias.shape[0]
    n_head = query_weight.shape[1]
    if fast:
        small_sum = small_sum[0] + to_x(small_sum[1])
        zi = lax.axis_index("a")
        pieces = [lax.dynamic_index_in_dim(small_sum, (zi + k) % ZS, 0, keepdims=False) for k in range(ZS)]
        pieces = [lax.ppermute(v, "a", [(i, (i + k) % ZS) for i in range(ZS)]) if k else v for k, v in enumerate(pieces)]
        *weights, fg, fs, ob, sg, ss, db, hb, qb, vb = call(
            functools.partial(final_body, rows=rows),
            (1,),
            [kept(ga_all.shape)] + [kept((KINDS, rows))] * ZS,
            [(sds((shard, n_head), F32), kept((shard, n_head)))] * 3
            + [(sds((n_head, shard), F32), kept((n_head, shard)))]
            + [(sds((1, shard), F32), kept((1, shard)))] * 7
            + [(sds((1, n_bias), F32), kept((1, n_bias)))] * 2,
            flops=1e6,
            moved=2e6,
        )(ga_all, *pieces)
        vectors = [v[0] for v in (fg, fs, ob, sg, ss, db, hb, qb, vb)]
        mlp_sum = jnp.sum(mlp_all.astype(F32), axis=0)
        gh, gd = mlp_sum[:shard], mlp_sum[shard:].T
    else:

        def scatter(values):
            return lax.psum_scatter(values, ("a", "b"), scatter_dimension=0, tiled=True)

        def scatter_slow(oo, ox, yo, yx):
            own, oth = oo + to_y(yo), ox + to_y(yx)
            return scatter(jnp.stack([own, oth], axis=1).reshape(width, -1).astype(F32))

        kinds = small_sum.transpose(2, 1, 0, 3)
        bias = kinds[7].reshape(ZS * XS, rows)
        split = rows // 4
        vectors = [scatter(v) for v in kinds[:7].reshape(7, width)]
        vectors += [scatter(bias[:, k * split : k * split + split].reshape(-1)) for k in range(2)]
        gh = scatter_slow(gh_oo, gh_ox, gh_yo, gh_yx)
        gd = scatter_slow(gd_oo, gd_ox, gd_yo, gd_yx).T
        ga = scatter_slow(ga_oo, ga_ox, ga_yo, ga_yx)
        weights = [ga[:, k * n_head : k * n_head + n_head] for k in range(4)]
        weights[3] = weights[3].T

    def placed(stays, got):
        return jnp.where(yi == 0, jnp.stack([stays, got]), jnp.stack([got, stays]))

    block_output = placed(out_tokens[:block], out_got)
    input_gradient = placed(input_grad[:block], to_y(input_grad[block : 2 * block]))

    fg, fs, ob, sg, ss, db, hb, qb, vb = vectors
    return (
        block_output, input_gradient, embed_gradient, fg, fs, weights[0], qb, weights[1], weights[2], vb,
        weights[3], ob, sg, ss, gh, hb, gd, db,
    )


def solution(mesh):
    dp, tensor = mesh.shape["dp"], mesh.shape["tensor"]
    fine = Mesh(mesh.devices.reshape(dp // 2, 2, tensor // 2, 2), ("a", "b", "y", "c"))
    by_dp, by_tensor = ("a", "b"), ("y", "c")
    both = by_tensor + by_dp
    column, matrix, turned = P(by_dp), P(by_dp, by_tensor), P(by_tensor, by_dp)
    seqs = P(by_dp, by_tensor, None)
    return jax.shard_map(
        functools.partial(body, dp == ZS * XS),
        mesh=fine,
        in_specs=(
            seqs, P(by_dp, None), column, column, matrix, P(both), matrix, matrix, P(both), turned,
            column, column, column, matrix, P(both), turned, column, seqs,
        ),
        out_specs=(
            seqs, seqs, P(by_dp, None), column, column, matrix, P(both), matrix, matrix, P(both), turned,
            column, column, column, matrix, P(both), turned, column,
        ),
        check_vma=False,
    )
```

```python
import functools

import jax
import jax.numpy as jnp
from jax import lax
from jax.experimental import pallas as pl
from jax.experimental.pallas import tpu as pltpu
from jax.sharding import Mesh
from jax.sharding import PartitionSpec as P

HD = 64
EPSILON = 1e-05
SCALE = 0.125
BF = jnp.bfloat16
F32 = jnp.float32
ZS, XS = 4, 2
KINDS = 8
HINT = 1.0
TILE_PROJECT = 512
TILE_OUT = 256
TILE_MLP = 512
TILE_SECOND = 512
TILE_BACK = 1024
TILE_FIRST = 512

NN = (((1,), (0,)), ((), ()))
NT = (((1,), (1,)), ((), ()))


def dot(left, right, dims=NN):
    return lax.dot_general(left, right, dims, preferred_element_type=F32)


def call(body, grid, ins, outs, scratch=(), flops=0, moved=0, trans=0, vmem=16):
    return pl.pallas_call(
        body,
        grid=grid,
        in_specs=[s for s in ins],
        out_specs=[s for _, s in outs],
        out_shape=[o for o, _ in outs],
        scratch_shapes=list(scratch),
        compiler_params=pltpu.CompilerParams(vmem_limit_bytes=vmem << 20),
        cost_estimate=pl.CostEstimate(flops=int(flops * HINT), bytes_accessed=int(moved * HINT), transcendentals=int(trans * HINT)),
    )


def whole(shape, n=1):
    zeros = (0,) * len(shape)
    return pl.BlockSpec(shape, lambda *_: zeros, pipeline_mode=pl.Buffered(1))


def kept(shape):
    zeros = (0,) * len(shape)
    return pl.BlockSpec(shape, lambda *_: zeros)


def far(values):
    return pltpu.with_memory_space_constraint(values, pltpu.HBM)


def scalar():
    return pl.BlockSpec(memory_space=pltpu.SMEM)


def sds(shape, dtype):
    return jax.ShapeDtypeStruct(shape, dtype)


def shard_of(refs, z, rows):
    parts = [r[z] for r in refs]
    value = parts[0] if len(parts) == 1 else jnp.concatenate(parts, axis=0)
    return value[:rows], value[rows:]


def normalize(values):
    center = values - jnp.mean(values, axis=-1, keepdims=True)
    spread = jnp.mean(center * center, axis=-1, keepdims=True)
    rate = lax.rsqrt(spread + EPSILON)
    return center * rate, rate


def pack_body(q_ref, k_ref, v_ref, o_ref, h_ref, d_ref, fg, fs, ob, sg, ss, db, hb, qb, vb, attn_ref, mlp_ref):
    shard = q_ref.shape[0]
    low = jnp.concatenate([q_ref[...], k_ref[...], v_ref[...], o_ref[...].T], axis=1)
    n = qb.shape[1]
    bias = jnp.concatenate([qb[...], vb[...], jnp.zeros((1, shard - 2 * n), BF)], axis=1)
    small = jnp.concatenate([r[...].astype(F32) for r in (fg, fs, ob, sg, ss, db, hb)] + [bias.astype(F32)], axis=0)
    small = jnp.concatenate([small, jnp.zeros((KINDS, low.shape[1] - shard), F32)], axis=1).astype(BF)
    high, down = h_ref[...], d_ref[...].T
    for z in range(attn_ref.shape[0]):
        attn_ref[z, :shard, :] = low
        attn_ref[z, shard:, :] = small
        mlp_ref[z, :shard, :] = high
        mlp_ref[z, shard:, :] = down


def pick(refs):
    step, each = pl.program_id(0), len(refs) // pl.num_programs(0)
    blocks = [r[...] for r in refs]
    tiles = [blocks[k : k + each] for k in range(0, len(blocks), each)]
    tiles = [t[0] if each == 1 else jnp.concatenate(t, axis=0) for t in tiles]
    value = tiles[0]
    for k in range(1, len(tiles)):
        value = jnp.where(step == k, tiles[k], value)
    return value


def project_body(x_ref, *refs, rows, first):
    refs = list(refs)
    if first:
        *tokens, te_ref, own_ref, oth_ref, w_ref, vec_ref, qkv_ref, normed_ref, normed_t_ref, bias_ref = refs
        oth_refs = (oth_ref,)
    else:
        source_ref, own_ref, *oth_refs, w_ref, vec_ref, qkv_ref, bias_ref = refs

    @pl.when(pl.program_id(0) == 0)
    def _():
        x = x_ref[0]
        own, oth = [], []
        for z in range(ZS):
            weight, small = shard_of((own_ref,), z, rows)
            w_ref[pl.ds(pl.multiple_of((2 * z + x) * rows, 32), rows), :] = weight
            own.append(small[:, :rows].astype(F32))
            weight, small = shard_of(oth_refs, z, rows)
            w_ref[pl.ds(pl.multiple_of((2 * z + 1 - x) * rows, 32), rows), :] = weight
            oth.append(small[:, :rows].astype(F32))
        even = jnp.concatenate([v for pair in zip(own, oth) for v in pair], axis=1)
        odd = jnp.concatenate([v for pair in zip(oth, own) for v in pair], axis=1)
        vec = jnp.where(x == 0, even, odd)
        vec_ref[...] = vec
        n = rows // 4
        last = vec[7:8, :]
        parts = [last[:, rows * k : rows * k + n] for k in range(ZS * XS)]
        parts += [jnp.zeros((1, 3 * HD), F32)]
        parts += [last[:, rows * k + n : rows * k + 2 * n] for k in range(ZS * XS)]
        bias_ref[0:1, :] = jnp.concatenate(parts, axis=1)

    if first:
        xhat, _ = normalize(pick(tokens).astype(F32) + te_ref[...].astype(F32))
        normed = (xhat * vec_ref[0:1, :] + vec_ref[1:2, :]).astype(BF)
        normed_ref[...] = normed
        normed_t_ref[...] = normed.T
    else:
        normed = source_ref[...]
    made = dot(normed, w_ref[:, :640])[:, :576] + bias_ref[0:1, :]
    made = made.astype(BF)
    for j in range(9):
        piece = made[:, 64 * j : 64 * j + 64]
        qkv_ref[j] = piece * BF(SCALE) if j < 3 else piece


def attend_body(q_ref, k_ref, v_ref, e_ref, inv_ref, mixed_ref, wide_ref):
    scores = dot(k_ref[0], q_ref[0], NT)
    expon = jnp.exp(scores - jnp.max(scores, axis=0, keepdims=True))
    inverse = 1.0 / jnp.sum(expon, axis=0, keepdims=True)
    low = expon.astype(BF)
    e_ref[0] = low
    inv_ref[0] = inverse
    wide = dot(v_ref[0].T, low) * inverse
    mixed_ref[0] = wide.astype(BF)
    wide_ref[0] = wide


def attend_back_body(q_ref, k_ref, v_ref, e_ref, inv_ref, mixed_ref, gm_ref, dq_ref, dk_ref, dv_ref):
    low = (gm_ref[0].astype(F32) * inv_ref[0]).astype(BF)
    inner = jnp.sum(low.astype(F32) * mixed_ref[0], axis=0, keepdims=True)
    expon = e_ref[0]
    grad_scores = (expon.astype(F32) * (dot(v_ref[0], low) - inner)).astype(BF)
    dv_ref[0] = dot(expon, low, NT).astype(BF)
    dk_ref[0] = dot(grad_scores, q_ref[0]).astype(BF)
    dq_ref[0] = (dot(k_ref[0].T, grad_scores) * SCALE).T.astype(BF)


def outproj_body(m0_ref, m1_ref, w0_ref, w1_ref, out_ref, wo_ref):
    @pl.when(pl.program_id(0) == 0)
    def _():
        wo_ref[...] = jnp.concatenate([w0_ref[:, 576:], w1_ref[:, 576:]], axis=1)

    mixed = jnp.concatenate([m0_ref[...], m1_ref[...]], axis=0).T
    out_ref[...] = dot(mixed, wo_ref[...], NT).astype(BF)


def feed(normed, cot, wh, wd, bias, acc_h, acc_d, hbg_ref):
    pre = dot(normed, wh[...]) + bias
    below = 0.5 + 0.5 * lax.erf(pre * 0.7071067811865476)
    act = (pre * below).astype(BF)
    slope = below + pre * (jnp.exp(-0.5 * pre * pre) * 0.3989422804014327)
    grad = (dot(cot, wd[...]) * slope).astype(BF)
    acc_h[...] += dot(normed.T, grad)
    acc_d[...] += dot(cot.T, act)
    hbg_ref[...] += jnp.sum(grad.astype(F32), axis=0, keepdims=True)
    return dot(act, wd[...], NT), dot(grad, wh[...], NT)


def fill(x, rows, own, oth, wh, wd, acc_h, acc_d, hbg_ref):
    for z in range(ZS):
        for refs, side in ((own, x), (oth, 1 - x)):
            at = pl.multiple_of((2 * z + side) * rows, 32)
            wh[pl.ds(at, rows), :], wd[pl.ds(at, rows), :] = shard_of(refs, z, rows)
    for ref in (acc_h, acc_d, hbg_ref):
        ref[...] = jnp.zeros_like(ref)


def drain(x, rows, acc, own, oth):
    for z in range(ZS):
        own[z] = acc[pl.ds(pl.multiple_of((2 * z + x) * rows, 32), rows), :].astype(BF)
        oth[z] = acc[pl.ds(pl.multiple_of((2 * z + 1 - x) * rows, 32), rows), :].astype(BF)


def mlp_first_body(
    x_ref, s0, s1, s2, s3, te_ref, a0_ref, a1_ref, c0, c1, c2, c3, vec_ref, w_oo, w_ox,
    mid_ref, normed_ref, ff_ref, gs_ref, hbg_ref, gh_o, gh_x, gd_o, gd_x,
    wh, wd, acc_h, acc_d, *, rows,
):
    x = x_ref[0]

    @pl.when(pl.program_id(0) == 0)
    def _():
        fill(x, rows, (w_oo,), (w_ox,), wh, wd, acc_h, acc_d, hbg_ref)

    middle = (
        pick((s0, s1, s2, s3)).astype(F32)
        + te_ref[...].astype(F32)
        + (a0_ref[...].astype(F32) + a1_ref[...].astype(F32))
        + vec_ref[2:3, :]
    )
    mid_ref[...] = middle
    xhat, _ = normalize(middle)
    normed = (xhat * vec_ref[3:4, :] + vec_ref[4:5, :]).astype(BF)
    normed_ref[...] = normed
    ff_ref[...], gs_ref[...] = feed(normed, pick((c0, c1, c2, c3)), wh, wd, vec_ref[6:7, :], acc_h, acc_d, hbg_ref)

    @pl.when(pl.program_id(0) == pl.num_programs(0) - 1)
    def _():
        drain(x, rows, acc_h, gh_o, gh_x)
        drain(x, rows, acc_d, gd_o, gd_x)


def mlp_second_body(
    x_ref, normed_ref, c0, c1, c2, c3, vec_ref, f_ref, g_ref, w_yo, h_yx, d_yx,
    ff0_ref, ff1_ref, gs_ref, hbg_ref, gh_o, gh_x, gd_o, gd_x,
    wh, wd, acc_h, acc_d, *, rows,
):
    x = x_ref[0]

    @pl.when(pl.program_id(0) == 0)
    def _():
        fill(x, rows, (w_yo,), (h_yx, d_yx), wh, wd, acc_h, acc_d, hbg_ref)

    ff, gs = feed(normed_ref[...], pick((c0, c1, c2, c3)), wh, wd, vec_ref[6:7, :], acc_h, acc_d, hbg_ref)
    gs_ref[...] = (g_ref[...] + gs).astype(BF)
    ff = (f_ref[...] + ff).astype(BF)
    half = pl.num_programs(0) // 2

    @pl.when(pl.program_id(0) < half)
    def _():
        ff0_ref[...] = ff

    @pl.when(pl.program_id(0) >= half)
    def _():
        ff1_ref[...] = ff

    @pl.when(pl.program_id(0) == pl.num_programs(0) - 1)
    def _():
        drain(x, rows, acc_h, gh_o, gh_x)
        drain(x, rows, acc_d, gd_o, gd_x)


def second_back_body(mid_ref, g0_ref, g1_ref, c0, c1, c2, c3, vec_ref, w0_ref, w1_ref, m0_ref, m1_ref, gm_ref, x0_ref, x1_ref, wo0_ref, wo1_ref, sum_ref, wo_ref, acc):
    step, last = pl.program_id(0), pl.num_programs(0) - 1

    @pl.when(step == 0)
    def _():
        wo_ref[...] = jnp.concatenate([w0_ref[:, 576:], w1_ref[:, 576:]], axis=1)
        acc[...] = jnp.zeros_like(acc)
        sum_ref[...] = jnp.zeros_like(sum_ref)

    xhat, rate = normalize(mid_ref[...])
    second = g0_ref[...].astype(F32) + g1_ref[...].astype(F32)
    cot = pick((c0, c1, c2, c3)).astype(F32)
    scaled = second * vec_ref[3:4, :]
    inner = jnp.mean(scaled * xhat, axis=-1, keepdims=True)
    grad = cot + rate * (scaled - jnp.mean(scaled, axis=-1, keepdims=True) - xhat * inner)
    gm_ref[...] = grad
    sum_ref[0:1, :] += jnp.sum(second * xhat, axis=0, keepdims=True)
    sum_ref[1:2, :] += jnp.sum(second, axis=0, keepdims=True)
    sum_ref[2:3, :] += jnp.sum(grad, axis=0, keepdims=True)
    sum_ref[3:4, :] += jnp.sum(cot, axis=0, keepdims=True)
    low = grad.astype(BF)
    back = dot(low, wo_ref[...]).astype(BF).T
    x0_ref[...] = back[:192]
    x1_ref[...] = back[192:]
    mixed = jnp.concatenate([m0_ref[...], m1_ref[...]], axis=0)
    acc[...] += dot(low.T, mixed, NT)

    @pl.when(step == last)
    def _():
        wo0_ref[...] = acc[:, :192].astype(BF)
        wo1_ref[...] = acc[:, 192:].astype(BF)


def project_back_body(x_ref, q_ref, k_ref, v_ref, nt_ref, w_ref, wo_ref, *refs, rows, more):
    refs = list(refs)
    prev_ref = refs.pop(0) if more else None
    own_ref, oth_ref, first_ref, sum_ref, acc = refs
    step, last = pl.program_id(0), pl.num_programs(0) - 1
    x = x_ref[0]
    grads = jnp.concatenate([r[h] for r in (q_ref, k_ref, v_ref) for h in range(3)], axis=1)
    made = dot(nt_ref[...], grads)
    total = jnp.sum(grads.astype(F32), axis=0, keepdims=True)

    @pl.when(step == 0)
    def _():
        acc[...] = made
        sum_ref[...] = total

    @pl.when(step > 0)
    def _():
        acc[...] += made
        sum_ref[...] += total

    back = dot(grads, w_ref[:, :576], NT)
    if more:
        back = back + prev_ref[...]
    first_ref[...] = back.astype(first_ref.dtype)

    @pl.when(step == last)
    def _():
        for z in range(ZS):
            for ref, side in ((own_ref, x), (oth_ref, 1 - x)):
                at = pl.multiple_of((2 * z + side) * rows, 32)
                ref[z] = jnp.concatenate(
                    [acc[pl.ds(at, rows), :].astype(BF), wo_ref[pl.ds(at, rows), :]], axis=1
                )


def first_back_body(
    x_ref, s0, s1, s2, s3, te_ref, vec_ref, g0_ref, g1_ref, gm_ref, second_ref, ho_ref, hy_ref, qo_ref, qy_ref,
    out_ref, own_ref, oth_ref, sum_ref, *, rows,
):
    @pl.when(pl.program_id(0) == 0)
    def _():
        sum_ref[...] = jnp.zeros_like(sum_ref)

    xhat, rate = normalize(pick((s0, s1, s2, s3)).astype(F32) + te_ref[...].astype(F32))
    first = g0_ref[...].astype(F32) + g1_ref[...].astype(F32)
    scaled = first * vec_ref[0:1, :]
    inner = jnp.mean(scaled * xhat, axis=-1, keepdims=True)
    grad = gm_ref[...] + rate * (scaled - jnp.mean(scaled, axis=-1, keepdims=True) - xhat * inner)
    out_ref[...] = grad.astype(BF)
    sum_ref[0:1, :] += jnp.sum(first * xhat, axis=0, keepdims=True)
    sum_ref[1:2, :] += jnp.sum(first, axis=0, keepdims=True)
    sum_ref[2:3, :] += jnp.sum(grad, axis=0, keepdims=True)

    @pl.when(pl.program_id(0) == pl.num_programs(0) - 1)
    def _():
        n = rows // 4
        sums = sum_ref[0:3, :]
        shared = [sums[0:2], second_ref[2:3, :], second_ref[0:2, :], second_ref[3:4, :]]
        blank = jnp.zeros((1, rows - 2 * n), F32)
        for hidden, bias, ref, more in ((ho_ref, qo_ref, own_ref, []), (hy_ref, qy_ref, oth_ref, [sums[2:3]])):
            made = []
            kinds = jnp.concatenate(shared + [hidden[...]], axis=0)
            extra = jnp.concatenate(more + [jnp.zeros((KINDS - 1, kinds.shape[1]), F32)], axis=0) if more else None
            for k in range(ZS * XS):
                part = slice(k * rows, k * rows + rows)
                last = [bias[0:1, k * n : k * n + n], bias[0:1, 6 * HD + k * n : 6 * HD + k * n + n], blank]
                piece = [kinds[:, part], jnp.concatenate(last, axis=1)]
                made.append(jnp.concatenate(piece + ([extra[:, part]] if more else []), axis=0))
            for z in range(ZS):
                even, odd = made[2 * z], made[2 * z + 1]
                ref[0, z] = jnp.where(x_ref[0] == 0, even, odd)
                ref[1, z] = jnp.where(x_ref[0] == 0, odd, even)


def final_body(got_ref, p0_ref, p1_ref, p2_ref, p3_ref, q_ref, k_ref, v_ref, o_ref, *small, rows):
    total = got_ref[0].astype(F32)
    for z in range(1, got_ref.shape[0]):
        total = total + got_ref[z].astype(F32)
    width = 3 * HD
    q_ref[...] = total[:, :width]
    k_ref[...] = total[:, width : 2 * width]
    v_ref[...] = total[:, 2 * width : 3 * width]
    o_ref[...] = total[:, 3 * width :].T
    sums = (p0_ref[...] + p1_ref[...]) + (p2_ref[...] + p3_ref[...])
    n = rows // 4
    for k, ref in enumerate(small[:7]):
        ref[...] = sums[k : k + 1]
    small[7][...] = sums[7:8, :n]
    small[8][...] = sums[7:8, n : 2 * n]


def output_body(mid_ref, f0_ref, f1_ref, vec_ref, out_ref):
    out_ref[...] = (
        mid_ref[...] + (f0_ref[...].astype(F32) + f1_ref[...].astype(F32)) + vec_ref[5:6, :]
    ).astype(BF)


def swap(size):
    return [(i, size - 1 - i) for i in range(size)]


def to_y(values):
    return lax.ppermute(values, "y", swap(2))


def to_x(values):
    return lax.ppermute(values, "b", swap(2))


def to_core(values):
    return lax.ppermute(values, "c", swap(2))


def spread_z(values):
    return lax.all_to_all(values, "a", 0, 0, tiled=True)


def body(
    fast,
    inputs,
    time_embed,
    first_gain,
    first_shift,
    query_weight,
    query_bias,
    key_weight,
    value_weight,
    value_bias,
    output_weight,
    output_bias,
    second_gain,
    second_shift,
    hidden_weight,
    hidden_bias,
    down_weight,
    down_bias,
    cotangent,
):
    _, block, width = inputs.shape
    shard = query_weight.shape[0]
    rows = width // (ZS * XS)
    seq = 4 * block
    hidden = hidden_weight.shape[1]
    yi = lax.axis_index("y")
    xi = lax.axis_index("b") if fast else jnp.int32(0)
    x_arr = xi.astype(jnp.int32)[None]

    n_copies = ZS if fast else 1
    attn_pack, mlp_pack = call(
        pack_body,
        (1,),
        [kept((shard, hidden // 4))] * 3
        + [kept((hidden // 4, shard)), kept((shard, hidden)), kept((hidden, shard))]
        + [kept((1, shard))] * 7
        + [kept((1, query_bias.shape[0]))] * 2,
        [
            (sds((n_copies, shard + KINDS, width), BF), kept((n_copies, shard + KINDS, width))),
            (sds((n_copies, 2 * shard, width), BF), kept((n_copies, 2 * shard, width))),
        ],
        flops=1e6,
        moved=2e6,
        vmem=56,
    )(
        query_weight, key_weight, value_weight, output_weight, hidden_weight, down_weight,
        *(v[None] for v in (first_gain, first_shift, output_bias, second_gain, second_shift, down_bias, hidden_bias, query_bias, value_bias)),
    )

    inputs, cotangent, attn_pack = lax.optimization_barrier((inputs, cotangent, attn_pack))
    both = jnp.concatenate([inputs, cotangent], axis=1)
    stays = lax.dynamic_index_in_dim(both, yi, 0, keepdims=False)
    comes = to_y(lax.dynamic_index_in_dim(both, 1 - yi, 0, keepdims=False))
    stays_mate = to_core(stays)
    te = lax.dynamic_index_in_dim(time_embed, yi, 0, keepdims=True)

    if fast:
        attn_oo = spread_z(attn_pack)
        attn_oo, comes, stays_mate = lax.optimization_barrier((attn_oo, comes, stays_mate))
        comes_mate = to_core(comes)
        attn_ox, attn_yo = to_x(attn_oo), to_y(attn_oo)
        attn_ox, attn_yo = lax.optimization_barrier((attn_ox, attn_yo))
        mlp_oo = spread_z(mlp_pack)
        attn_yx = (to_y(attn_ox[:, : rows // 2]), to_x(attn_yo[:, rows // 2 :]))
    else:
        def natural(values):
            full = lax.all_gather(values, ("a", "b"), axis=0, tiled=True)
            full = full.reshape(ZS, XS, rows, width)
            return full[:, 0], full[:, 1]

        gathered = lax.all_gather(attn_pack[0], ("a", "b"), axis=0, tiled=False)
        matrix = gathered[:, :shard].reshape(ZS, XS, rows, width)
        small = gathered[:, shard:, :shard]
        flat = small[:, :7].transpose(1, 0, 2).reshape(7, width)
        n = shard // 4
        bias = [small[:, 7, k * n : k * n + n].reshape(ZS * XS, -1) for k in range(2)]
        bias = jnp.concatenate([*bias, jnp.zeros((ZS * XS, rows - 2 * (rows // 4)), BF)], axis=1)
        small = jnp.concatenate([flat, bias.reshape(1, width)], axis=0)
        small = small.reshape(KINDS, ZS, XS, rows).transpose(1, 2, 0, 3)
        small = jnp.pad(small, ((0, 0), (0, 0), (0, 0), (0, width - rows)))
        matrix = jnp.concatenate([matrix, small], axis=2)
        attn_oo, attn_ox = matrix[:, 0], matrix[:, 1]
        attn_yo, attn_yx = to_y(attn_oo), (to_y(attn_ox),)
        comes_mate = to_core(comes)
        h_oo, h_ox = natural(mlp_pack[0, :shard])
        d_oo, d_ox = natural(mlp_pack[0, shard:])
        mlp_oo = jnp.concatenate([h_oo, d_oo], axis=1)
        mlp_ox = jnp.concatenate([h_ox, d_ox], axis=1)

    def by(tile):
        return pl.BlockSpec((tile, width), lambda i: (i, 0))

    def by_mate(tile):
        tiles = seq // tile
        return pl.BlockSpec((tile, width), lambda i: ((i + tiles // 2) % tiles, 0))

    def low_half(tile):
        last = seq // tile // 2 - 1
        return pl.BlockSpec((tile, width), lambda i: (jnp.minimum(i, last), 0))

    def high_half(tile):
        first = seq // tile // 2
        return pl.BlockSpec((tile, width), lambda i: (jnp.maximum(i - first, 0), 0))

    tokens = tuple(far(v) for v in (stays, comes, stays_mate, comes_mate))
    start_blocks = [pl.BlockSpec((block, width), lambda *_: (0, 0), pipeline_mode=pl.Buffered(1))] * 4
    cot_blocks = [pl.BlockSpec((block, width), lambda *_: (1, 0), pipeline_mode=pl.Buffered(1))] * 4
    row = kept((1, width))
    vecs = kept((KINDS, width))
    square = whole((width, width))
    n_qkv = 9 * HD

    def project(first, source, *shards):
        tile = TILE_PROJECT
        outs = [
            (sds((width, width), BF), kept((width, width))),
            (sds((KINDS, width), F32), vecs),
            (pltpu.HBM((9, seq, HD), BF), pl.BlockSpec((9, tile, HD), lambda i: (0, i, 0))),
        ]
        if first:
            outs += [
                (pltpu.HBM((seq, width), BF), by(tile)),
                (pltpu.HBM((width, seq), BF), pl.BlockSpec((width, tile), lambda i: (0, i))),
            ]
        return call(
            functools.partial(project_body, rows=rows, first=first),
            (seq // tile,),
            [scalar()] + (start_blocks + [row] if first else [by(tile)]) + [whole(v.shape) for v in shards],
            outs,
            scratch=[pltpu.VMEM((8, n_qkv), F32)],
            flops=2 * seq * width * n_qkv,
            moved=8e6,
        )(x_arr, *source, *shards)

    q_spec = pl.BlockSpec((1, seq, HD), lambda h: (h, 0, 0))
    k_spec = pl.BlockSpec((1, seq, HD), lambda h: (3 + h, 0, 0))
    v_spec = pl.BlockSpec((1, seq, HD), lambda h: (6 + h, 0, 0))
    e_spec = pl.BlockSpec((1, seq, seq), lambda h: (h, 0, 0))
    inv_spec = pl.BlockSpec((1, 1, seq), lambda h: (h, 0, 0))
    t_spec = pl.BlockSpec((1, HD, seq), lambda h: (h, 0, 0))

    def attend(qkv):
        return call(
            attend_body,
            (3,),
            [q_spec, k_spec, v_spec],
            [
                (pltpu.HBM((3, seq, seq), BF), e_spec),
                (sds((3, 1, seq), F32), inv_spec),
                (sds((3, HD, seq), BF), t_spec),
                (pltpu.HBM((3, HD, seq), F32), t_spec),
            ],
            flops=3 * 16 * seq * seq * HD,
            moved=8e6,
            trans=3 * seq * seq,
        )(*[far(qkv)] * 3)

    def attend_back(qkv, expon, inverse, mixed, grad_mixed, keep):
        made = keep((3, seq, HD), BF)
        return call(
            attend_back_body,
            (3,),
            [q_spec, k_spec, v_spec, e_spec, inv_spec, t_spec, t_spec],
            [(made, q_spec)] * 3,
            flops=3 * 40 * seq * seq * HD,
            moved=9e6,
        )(*[far(qkv)] * 3, far(expon), inverse, far(mixed), grad_mixed)

    w_o, vec, qkv_o, normed, normed_t = project(True, (*tokens, te), attn_oo, attn_ox)
    qkv_o, attn_yx, mlp_oo = lax.optimization_barrier((qkv_o, attn_yx, mlp_oo))
    mlp_yo = to_y(mlp_oo)
    if fast:
        mlp_ox = to_x(mlp_oo)
    exp_o, inv_o, mixed_o, wide_o = attend(qkv_o)
    normed, exp_o = lax.optimization_barrier((normed, exp_o))
    w_y, vec_y, qkv_y = project(False, (far(normed),), attn_yo, *attn_yx)
    exp_y, inv_y, mixed_y, wide_y = attend(qkv_y)
    mixed_y, mlp_ox, mlp_yo = lax.optimization_barrier((mixed_y, mlp_ox, mlp_yo))
    h_yx = to_y(mlp_ox[:, :rows])
    d_yx = to_x(mlp_yo[:, rows:]) if fast else to_y(mlp_ox[:, rows:])

    tile = TILE_OUT
    half_t = pl.BlockSpec((3 * HD, tile), lambda i: (0, i))
    flat_o, flat_y = mixed_o.reshape(3 * HD, seq), mixed_y.reshape(3 * HD, seq)
    (attended,) = call(
        outproj_body,
        (seq // tile,),
        [half_t, half_t, square, square],
        [(sds((seq, width), BF), by(tile))],
        scratch=[pltpu.VMEM((width, 6 * HD), BF)],
        flops=2 * seq * width * 384,
        moved=6e6,
    )(flat_o, flat_y, w_o, w_y)
    attended_mate = to_core(attended)

    tile = TILE_MLP
    part = (ZS, rows, hidden)
    grad_parts = [(sds((1, hidden), F32), kept((1, hidden)))] + [(sds(part, BF), kept(part))] * 4
    mlp_scratch = [pltpu.VMEM((width, hidden), t) for t in (BF, BF, F32, F32)]
    mlp_cost = dict(flops=12 * seq * width * hidden, moved=16e6, trans=seq * hidden * 2, vmem=24)
    middle, normed_second, ff_part, gs_part, hb_o, gh_oo, gh_ox, gd_oo, gd_ox = call(
        functools.partial(mlp_first_body, rows=rows),
        (seq // tile,),
        [scalar(), *start_blocks, row, by(tile), by_mate(tile), *cot_blocks, vecs]
        + [whole((ZS, 2 * rows, hidden))] * 2,
        [
            (sds((seq, width), F32), by(tile)),
            (sds((seq, width), BF), by(tile)),
            (sds((seq, width), F32), by(tile)),
            (sds((seq, width), F32), by(tile)),
        ]
        + grad_parts,
        scratch=mlp_scratch,
        **mlp_cost,
    )(x_arr, *tokens, te, attended, attended_mate, *tokens, vec, mlp_oo, mlp_ox)
    if fast:
        got_ho = to_x(gh_ox)
        normed_second, h_yx, d_yx = lax.optimization_barrier((normed_second, h_yx, d_yx))
    ff, ff_sent, gs, hb_y, gh_yo, gh_yx, gd_yo, gd_yx = call(
        functools.partial(mlp_second_body, rows=rows),
        (seq // tile,),
        [scalar(), by(tile), *cot_blocks, vecs, by(tile), by(tile)]
        + [whole((ZS, 2 * rows, hidden)), whole(part), whole(part)],
        [
            (sds((seq // 2, width), BF), low_half(tile)),
            (sds((seq // 2, width), BF), high_half(tile)),
            (sds((seq, width), BF), by(tile)),
        ]
        + grad_parts,
        scratch=mlp_scratch,
        **mlp_cost,
    )(x_arr, normed_second, *tokens, vec_y, ff_part, gs_part, mlp_yo, h_yx, d_yx)
    if fast:
        gs, got_ho = lax.optimization_barrier((gs, got_ho))
    gs_mate = to_core(gs)
    ff_mate = to_core(ff_sent)

    tile = TILE_SECOND
    half_t = pl.BlockSpec((3 * HD, tile), lambda i: (0, i))
    grad_middle, gx_o, gx_y, wo_o, wo_y, second_sums = call(
        second_back_body,
        (seq // tile,),
        [by(tile), by(tile), by_mate(tile), *cot_blocks, vecs, square, square, half_t, half_t],
        [
            (pltpu.HBM((seq, width), F32), by(tile)),
            (sds((3 * HD, seq), BF), half_t),
            (sds((3 * HD, seq), BF), half_t),
            (pltpu.HBM((width, 3 * HD), BF), kept((width, 3 * HD))),
            (pltpu.HBM((width, 3 * HD), BF), kept((width, 3 * HD))),
            (sds((KINDS, width), F32), vecs),
        ],
        scratch=[pltpu.VMEM((width, 6 * HD), BF), pltpu.VMEM((width, 6 * HD), F32)],
        flops=4 * seq * width * 384,
        moved=16e6,
    )(middle, gs, gs_mate, *tokens, vec, w_o, w_y, flat_o, flat_y)
    if fast:
        got_h, got_d = to_x(gh_yx), to_y(gd_yx)
        gx_y, got_h, got_d = lax.optimization_barrier((gx_y, got_h, got_d))
        got_hs, got_ds = to_y(gh_yo + got_h), to_x(gd_ox + got_d)

    def project_back(grads, weights, wo, prev):
        tile = TILE_BACK
        more = prev is not None
        heads = pl.BlockSpec((3, tile, HD), lambda i: (0, i, 0))
        attn_part = (ZS, rows, width)
        return call(
            functools.partial(project_back_body, rows=rows, more=more),
            (seq // tile,),
            [scalar(), heads, heads, heads, pl.BlockSpec((width, tile), lambda i: (0, i)), square, whole((width, 3 * HD))]
            + ([by(tile)] if more else []),
            [
                (pltpu.HBM(attn_part, BF), kept(attn_part)),
                (pltpu.HBM(attn_part, BF), kept(attn_part)),
                ((sds((seq, width), BF) if more else pltpu.HBM((seq, width), F32)), by(tile)),
                (sds((1, n_qkv), F32), kept((1, n_qkv))),
            ],
            scratch=[pltpu.VMEM((width, n_qkv), F32)],
            flops=4 * seq * width * n_qkv,
            moved=10e6,
        )(x_arr, *(far(v) if more else v for v in grads), far(normed_t), weights, far(wo), *((far(prev),) if more else ()))

    grads_y = attend_back(qkv_y, exp_y, inv_y, wide_y, gx_y.reshape(3, HD, seq), sds)
    ga_yo, ga_yx, first_part, qkv_sum_y = project_back(grads_y, w_y, wo_y, None)
    tile = TILE_OUT
    (out_tokens,) = call(
        output_body,
        (seq // tile // 2,),
        [by(tile), by(tile), by(tile), vecs],
        [(sds((seq // 2, width), BF), by(tile))],
        flops=1e6,
        moved=5e6,
    )(middle, ff, ff_mate, vec)
    gx_o, first_part, out_tokens = lax.optimization_barrier((gx_o, first_part, out_tokens))
    if fast:
        gx_o, ga_yx, got_hs, got_ds, gd_yo = lax.optimization_barrier((gx_o, ga_yx, got_hs, got_ds, gd_yo))
        got_do = to_y(gd_yo)
        ga_d = to_x(ga_yx)
    grads_o = attend_back(qkv_o, exp_o, inv_o, wide_o, gx_o.reshape(3, HD, seq), pltpu.HBM)
    if fast:
        *grads_o, got_do, ga_d, out_tokens = lax.optimization_barrier((*grads_o, got_do, ga_d, out_tokens))
        out_got = to_y(out_tokens[block:])
        mlp_all = spread_z(jnp.concatenate([gh_oo + got_ho + got_hs, gd_oo + got_do + got_ds], axis=1))
        ga_s = to_y(ga_yo + ga_d)
    ga_oo, ga_ox, first, qkv_sum_o = project_back(grads_o, w_o, wo_o, first_part)
    if fast:
        ga_x = to_x(ga_ox)
        first, out_got = lax.optimization_barrier((first, out_got))
    first_mate = to_core(first)

    tile = TILE_FIRST
    hb_spec, qkv_spec = kept((1, hidden)), kept((1, n_qkv))
    small_o_shape, small_y_shape = (XS, ZS, KINDS, rows), (XS, ZS, 2 * KINDS, rows)
    input_grad, small_o, small_y, first_sums = call(
        functools.partial(first_back_body, rows=rows),
        (seq // tile,),
        [scalar(), *start_blocks, row, vecs, by(tile), by_mate(tile), by(tile), vecs, hb_spec, hb_spec, qkv_spec, qkv_spec],
        [
            (sds((seq, width), BF), by(tile)),
            (sds(small_o_shape, F32), kept(small_o_shape)),
            (sds(small_y_shape, F32), kept(small_y_shape)),
            (sds((KINDS, width), F32), vecs),
        ],
        flops=0,
        moved=0,
    )(x_arr, *tokens, te, vec, first, first_mate, far(grad_middle), second_sums, hb_o, hb_y, qkv_sum_o, qkv_sum_y)

    small_got = to_y(small_y)
    if fast:
        small_got, input_grad, ga_x, ga_s, mlp_all = lax.optimization_barrier(
            (small_got, input_grad, ga_x, ga_s, mlp_all)
        )
        ga_all = spread_z(ga_oo + ga_s + ga_x)
    small_sum = small_o + small_got[:, :, :KINDS]
    embed = first_sums[2]
    embed_got = jnp.where(xi == 0, small_got, small_got[::-1])[:, :, KINDS].transpose(1, 0, 2).reshape(width)
    embed_gradient = jnp.where(yi == 0, jnp.stack([embed, embed_got]), jnp.stack([embed_got, embed]))
    n_bias = query_bias.shape[0]
    n_head = query_weight.shape[1]
    if fast:
        small_sum = small_sum[0] + to_x(small_sum[1])
        zi = lax.axis_index("a")
        pieces = [lax.dynamic_index_in_dim(small_sum, (zi + k) % ZS, 0, keepdims=False) for k in range(ZS)]
        pieces = [lax.ppermute(v, "a", [(i, (i + k) % ZS) for i in range(ZS)]) if k else v for k, v in enumerate(pieces)]
        *weights, fg, fs, ob, sg, ss, db, hb, qb, vb = call(
            functools.partial(final_body, rows=rows),
            (1,),
            [kept(ga_all.shape)] + [kept((KINDS, rows))] * ZS,
            [(sds((shard, n_head), F32), kept((shard, n_head)))] * 3
            + [(sds((n_head, shard), F32), kept((n_head, shard)))]
            + [(sds((1, shard), F32), kept((1, shard)))] * 7
            + [(sds((1, n_bias), F32), kept((1, n_bias)))] * 2,
            flops=1e6,
            moved=2e6,
        )(ga_all, *pieces)
        vectors = [v[0] for v in (fg, fs, ob, sg, ss, db, hb, qb, vb)]
        mlp_sum = jnp.sum(mlp_all.astype(F32), axis=0)
        gh, gd = mlp_sum[:shard], mlp_sum[shard:].T
    else:

        def scatter(values):
            return lax.psum_scatter(values, ("a", "b"), scatter_dimension=0, tiled=True)

        def scatter_slow(oo, ox, yo, yx):
            own, oth = oo + to_y(yo), ox + to_y(yx)
            return scatter(jnp.stack([own, oth], axis=1).reshape(width, -1).astype(F32))

        kinds = small_sum.transpose(2, 1, 0, 3)
        bias = kinds[7].reshape(ZS * XS, rows)
        split = rows // 4
        vectors = [scatter(v) for v in kinds[:7].reshape(7, width)]
        vectors += [scatter(bias[:, k * split : k * split + split].reshape(-1)) for k in range(2)]
        gh = scatter_slow(gh_oo, gh_ox, gh_yo, gh_yx)
        gd = scatter_slow(gd_oo, gd_ox, gd_yo, gd_yx).T
        ga = scatter_slow(ga_oo, ga_ox, ga_yo, ga_yx)
        weights = [ga[:, k * n_head : k * n_head + n_head] for k in range(4)]
        weights[3] = weights[3].T

    def placed(stays, got):
        return jnp.where(yi == 0, jnp.stack([stays, got]), jnp.stack([got, stays]))

    if not fast:
        out_got = to_y(out_tokens[block:])
    block_output = placed(out_tokens[:block], out_got)
    input_gradient = placed(input_grad[:block], to_y(input_grad[block : 2 * block]))

    fg, fs, ob, sg, ss, db, hb, qb, vb = vectors
    return (
        block_output, input_gradient, embed_gradient, fg, fs, weights[0], qb, weights[1], weights[2], vb,
        weights[3], ob, sg, ss, gh, hb, gd, db,
    )


def solution(mesh):
    dp, tensor = mesh.shape["dp"], mesh.shape["tensor"]
    fine = Mesh(mesh.devices.reshape(dp // 2, 2, tensor // 2, 2), ("a", "b", "y", "c"))
    by_dp, by_tensor = ("a", "b"), ("y", "c")
    both = by_tensor + by_dp
    column, matrix, turned = P(by_dp), P(by_dp, by_tensor), P(by_tensor, by_dp)
    seqs = P(by_dp, by_tensor, None)
    return jax.shard_map(
        functools.partial(body, dp == ZS * XS),
        mesh=fine,
        in_specs=(
            seqs, P(by_dp, None), column, column, matrix, P(both), matrix, matrix, P(both), turned,
            column, column, column, matrix, P(both), turned, column, seqs,
        ),
        out_specs=(
            seqs, seqs, P(by_dp, None), column, column, matrix, P(both), matrix, matrix, P(both), turned,
            column, column, column, matrix, P(both), turned, column,
        ),
        check_vma=False,
    )
```

```python
import functools

import jax
import jax.numpy as jnp
from jax import lax
from jax.experimental import pallas as pl
from jax.experimental.pallas import tpu as pltpu
from jax.sharding import Mesh
from jax.sharding import PartitionSpec as P

HD = 64
EPSILON = 1e-05
SCALE = 0.125
BF = jnp.bfloat16
F32 = jnp.float32
ZS, XS = 4, 2
KINDS = 8
HINT = 1.0
TILE_PROJECT = 512
TILE_OUT = 256
TILE_MLP = 512
TILE_SECOND = 512
TILE_BACK = 1024
TILE_FIRST = 512

NN = (((1,), (0,)), ((), ()))
NT = (((1,), (1,)), ((), ()))


def dot(left, right, dims=NN):
    return lax.dot_general(left, right, dims, preferred_element_type=F32)


def call(body, grid, ins, outs, scratch=(), flops=0, moved=0, trans=0, vmem=16):
    return pl.pallas_call(
        body,
        grid=grid,
        in_specs=[s for s in ins],
        out_specs=[s for _, s in outs],
        out_shape=[o for o, _ in outs],
        scratch_shapes=list(scratch),
        compiler_params=pltpu.CompilerParams(vmem_limit_bytes=vmem << 20),
        cost_estimate=pl.CostEstimate(flops=int(flops * HINT), bytes_accessed=int(moved * HINT), transcendentals=int(trans * HINT)),
    )


def whole(shape, n=1):
    zeros = (0,) * len(shape)
    return pl.BlockSpec(shape, lambda *_: zeros, pipeline_mode=pl.Buffered(1))


def kept(shape):
    zeros = (0,) * len(shape)
    return pl.BlockSpec(shape, lambda *_: zeros)


def far(values):
    return pltpu.with_memory_space_constraint(values, pltpu.HBM)


def scalar():
    return pl.BlockSpec(memory_space=pltpu.SMEM)


def sds(shape, dtype):
    return jax.ShapeDtypeStruct(shape, dtype)


def place(x_ref, k, side, rows):
    x = x_ref[0] if side == 0 else 1 - x_ref[0]
    return pl.multiple_of((2 * lax.rem(x_ref[1] + k, ZS) + x) * rows, 32)


def shard_of(refs, z, rows):
    parts = [r[z] for r in refs]
    value = parts[0] if len(parts) == 1 else jnp.concatenate(parts, axis=0)
    return value[:rows], value[rows:]


def normalize(values):
    center = values - jnp.mean(values, axis=-1, keepdims=True)
    spread = jnp.mean(center * center, axis=-1, keepdims=True)
    rate = lax.rsqrt(spread + EPSILON)
    return center * rate, rate


def pack_body(q_ref, k_ref, v_ref, o_ref, h_ref, d_ref, fg, fs, ob, sg, ss, db, hb, qb, vb, attn_ref, mlp_ref):
    shard = q_ref.shape[0]
    low = jnp.concatenate([q_ref[...], k_ref[...], v_ref[...], o_ref[...].T], axis=1)
    n = qb.shape[1]
    bias = jnp.concatenate([qb[...], vb[...], jnp.zeros((1, shard - 2 * n), BF)], axis=1)
    small = jnp.concatenate([r[...].astype(F32) for r in (fg, fs, ob, sg, ss, db, hb)] + [bias.astype(F32)], axis=0)
    small = jnp.concatenate([small, jnp.zeros((KINDS, low.shape[1] - shard), F32)], axis=1).astype(BF)
    high, down = h_ref[...], d_ref[...]
    attn_ref[:shard, :] = low
    attn_ref[shard:, :] = small
    for z in range(mlp_ref.shape[0]):
        mlp_ref[z, :shard, :] = high
        mlp_ref[z, shard:, :] = down


def pick(refs):
    step, each = pl.program_id(0), len(refs) // pl.num_programs(0)
    blocks = [r[...] for r in refs]
    tiles = [blocks[k : k + each] for k in range(0, len(blocks), each)]
    tiles = [t[0] if each == 1 else jnp.concatenate(t, axis=0) for t in tiles]
    value = tiles[0]
    for k in range(1, len(tiles)):
        value = jnp.where(step == k, tiles[k], value)
    return value


def project_body(x_ref, *refs, rows, first):
    refs = list(refs)
    if first:
        *tokens, te_ref, own_ref, oth_ref, w_ref, vec_ref, qkv_ref, normed_ref, normed_t_ref, bias_ref = refs
        oth_refs = (oth_ref,)
    else:
        source_ref, own_ref, *oth_refs, w_ref, vec_ref, qkv_ref, bias_ref = refs

    @pl.when(pl.program_id(0) == 0)
    def _():
        own, oth = [], []
        for k in range(ZS):
            weight, small = shard_of((own_ref,), k, rows)
            w_ref[pl.ds(place(x_ref, k, 0, rows), rows), :] = weight
            own.append(small[:, :rows].astype(F32))
            weight, small = shard_of(oth_refs, k, rows)
            w_ref[pl.ds(place(x_ref, k, 1, rows), rows), :] = weight
            oth.append(small[:, :rows].astype(F32))
        even = jnp.concatenate([v for pair in zip(own, oth) for v in pair], axis=1)
        odd = jnp.concatenate([v for pair in zip(oth, own) for v in pair], axis=1)
        vec = jnp.where(x_ref[0] == 0, even, odd)
        vec = pltpu.roll(vec, x_ref[1] * (2 * rows), 1)
        vec_ref[...] = vec
        n = rows // 4
        last = vec[7:8, :]
        parts = [last[:, rows * k : rows * k + n] for k in range(ZS * XS)]
        parts += [jnp.zeros((1, 3 * HD), F32)]
        parts += [last[:, rows * k + n : rows * k + 2 * n] for k in range(ZS * XS)]
        bias_ref[0:1, :] = jnp.concatenate(parts, axis=1)

    if first:
        xhat, _ = normalize(pick(tokens).astype(F32) + te_ref[...].astype(F32))
        normed = (xhat * vec_ref[0:1, :] + vec_ref[1:2, :]).astype(BF)
        normed_ref[...] = normed
        normed_t_ref[...] = normed.T
    else:
        normed = source_ref[...]
    made = dot(normed, w_ref[:, :640])[:, :576] + bias_ref[0:1, :]
    made = made.astype(BF)
    for j in range(9):
        piece = made[:, 64 * j : 64 * j + 64]
        qkv_ref[j] = piece * BF(SCALE) if j < 3 else piece


def attend_body(q_ref, k_ref, v_ref, e_ref, inv_ref, mixed_ref, wide_ref):
    scores = dot(k_ref[0], q_ref[0], NT)
    expon = jnp.exp(scores - jnp.max(scores, axis=0, keepdims=True))
    inverse = 1.0 / jnp.sum(expon, axis=0, keepdims=True)
    low = expon.astype(BF)
    e_ref[0] = low
    inv_ref[0] = inverse
    wide = dot(v_ref[0].T, low) * inverse
    mixed_ref[0] = wide.astype(BF)
    wide_ref[0] = wide


def attend_back_body(q_ref, k_ref, v_ref, e_ref, inv_ref, mixed_ref, gm_ref, dq_ref, dk_ref, dv_ref):
    low = (gm_ref[0].astype(F32) * inv_ref[0]).astype(BF)
    inner = jnp.sum(low.astype(F32) * mixed_ref[0], axis=0, keepdims=True)
    expon = e_ref[0]
    grad_scores = (expon.astype(F32) * (dot(v_ref[0], low) - inner)).astype(BF)
    dv_ref[0] = dot(expon, low, NT).astype(BF)
    dk_ref[0] = dot(grad_scores, q_ref[0]).astype(BF)
    dq_ref[0] = (dot(k_ref[0].T, grad_scores) * SCALE).T.astype(BF)


def outproj_body(m0_ref, m1_ref, w0_ref, w1_ref, out_ref, wo_ref):
    @pl.when(pl.program_id(0) == 0)
    def _():
        wo_ref[...] = jnp.concatenate([w0_ref[:, 576:], w1_ref[:, 576:]], axis=1)

    mixed = jnp.concatenate([m0_ref[...], m1_ref[...]], axis=0).T
    out_ref[...] = dot(mixed, wo_ref[...], NT).astype(BF)


def feed(normed, cot, wh, wd, bias, acc_h, acc_d, hbg_ref):
    pre = dot(normed, wh[...]) + bias
    below = 0.5 + 0.5 * lax.erf(pre * 0.7071067811865476)
    act = (pre * below).astype(BF)
    slope = below + pre * (jnp.exp(-0.5 * pre * pre) * 0.3989422804014327)
    grad = (dot(cot, wd[...]) * slope).astype(BF)
    acc_h[...] += dot(normed.T, grad)
    acc_d[...] += dot(cot.T, act)
    hbg_ref[...] += jnp.sum(grad.astype(F32), axis=0, keepdims=True)
    return dot(act, wd[...], NT), dot(grad, wh[...], NT)


def fill(x, rows, own, oth, wh, wd, acc_h, acc_d, hbg_ref):
    for z in range(ZS):
        for refs, side in ((own, x), (oth, 1 - x)):
            at = pl.multiple_of((2 * z + side) * rows, 32)
            wh[pl.ds(at, rows), :], wd[pl.ds(at, rows), :] = shard_of(refs, z, rows)
    for ref in (acc_h, acc_d, hbg_ref):
        ref[...] = jnp.zeros_like(ref)


def drain(x, rows, acc, own, oth):
    for z in range(ZS):
        own[z] = acc[pl.ds(pl.multiple_of((2 * z + x) * rows, 32), rows), :].astype(BF)
        oth[z] = acc[pl.ds(pl.multiple_of((2 * z + 1 - x) * rows, 32), rows), :].astype(BF)


def mlp_first_body(
    x_ref, s0, s1, s2, s3, te_ref, a0_ref, a1_ref, c0, c1, c2, c3, vec_ref, w_oo, w_ox,
    mid_ref, normed_ref, ff_ref, gs_ref, hbg_ref, gh_o, gh_x, gd_o, gd_x,
    wh, wd, acc_h, acc_d, *, rows,
):
    x = x_ref[0]

    @pl.when(pl.program_id(0) == 0)
    def _():
        fill(x, rows, (w_oo,), (w_ox,), wh, wd, acc_h, acc_d, hbg_ref)

    middle = (
        pick((s0, s1, s2, s3)).astype(F32)
        + te_ref[...].astype(F32)
        + (a0_ref[...].astype(F32) + a1_ref[...].astype(F32))
        + vec_ref[2:3, :]
    )
    mid_ref[...] = middle
    xhat, _ = normalize(middle)
    normed = (xhat * vec_ref[3:4, :] + vec_ref[4:5, :]).astype(BF)
    normed_ref[...] = normed
    ff_ref[...], gs_ref[...] = feed(normed, pick((c0, c1, c2, c3)), wh, wd, vec_ref[6:7, :], acc_h, acc_d, hbg_ref)

    @pl.when(pl.program_id(0) == pl.num_programs(0) - 1)
    def _():
        drain(x, rows, acc_h, gh_o, gh_x)
        drain(x, rows, acc_d, gd_o, gd_x)


def mlp_second_body(
    x_ref, normed_ref, c0, c1, c2, c3, vec_ref, f_ref, g_ref, w_yo, h_yx, d_yx,
    ff0_ref, ff1_ref, gs_ref, hbg_ref, gh_o, gh_x, gd_o, gd_x,
    wh, wd, acc_h, acc_d, *, rows,
):
    x = x_ref[0]

    @pl.when(pl.program_id(0) == 0)
    def _():
        fill(x, rows, (w_yo,), (h_yx, d_yx), wh, wd, acc_h, acc_d, hbg_ref)

    ff, gs = feed(normed_ref[...], pick((c0, c1, c2, c3)), wh, wd, vec_ref[6:7, :], acc_h, acc_d, hbg_ref)
    gs_ref[...] = (g_ref[...] + gs).astype(BF)
    ff = (f_ref[...] + ff).astype(BF)
    half = pl.num_programs(0) // 2

    @pl.when(pl.program_id(0) < half)
    def _():
        ff0_ref[...] = ff

    @pl.when(pl.program_id(0) >= half)
    def _():
        ff1_ref[...] = ff

    @pl.when(pl.program_id(0) == pl.num_programs(0) - 1)
    def _():
        drain(x, rows, acc_h, gh_o, gh_x)
        drain(x, rows, acc_d, gd_o, gd_x)


def second_back_body(mid_ref, g0_ref, g1_ref, c0, c1, c2, c3, vec_ref, w0_ref, w1_ref, m0_ref, m1_ref, gm_ref, x0_ref, x1_ref, wo0_ref, wo1_ref, sum_ref, wo_ref, acc):
    step, last = pl.program_id(0), pl.num_programs(0) - 1

    @pl.when(step == 0)
    def _():
        wo_ref[...] = jnp.concatenate([w0_ref[:, 576:], w1_ref[:, 576:]], axis=1)
        acc[...] = jnp.zeros_like(acc)
        sum_ref[...] = jnp.zeros_like(sum_ref)

    xhat, rate = normalize(mid_ref[...])
    second = g0_ref[...].astype(F32) + g1_ref[...].astype(F32)
    cot = pick((c0, c1, c2, c3)).astype(F32)
    scaled = second * vec_ref[3:4, :]
    inner = jnp.mean(scaled * xhat, axis=-1, keepdims=True)
    grad = cot + rate * (scaled - jnp.mean(scaled, axis=-1, keepdims=True) - xhat * inner)
    gm_ref[...] = grad
    sum_ref[0:1, :] += jnp.sum(second * xhat, axis=0, keepdims=True)
    sum_ref[1:2, :] += jnp.sum(second, axis=0, keepdims=True)
    sum_ref[2:3, :] += jnp.sum(grad, axis=0, keepdims=True)
    sum_ref[3:4, :] += jnp.sum(cot, axis=0, keepdims=True)
    low = grad.astype(BF)
    back = dot(low, wo_ref[...]).astype(BF).T
    x0_ref[...] = back[:192]
    x1_ref[...] = back[192:]
    mixed = jnp.concatenate([m0_ref[...], m1_ref[...]], axis=0)
    acc[...] += dot(low.T, mixed, NT)

    @pl.when(step == last)
    def _():
        wo0_ref[...] = acc[:, :192].astype(BF)
        wo1_ref[...] = acc[:, 192:].astype(BF)


def project_back_body(x_ref, q_ref, k_ref, v_ref, nt_ref, w_ref, wo_ref, *refs, rows, more):
    refs = list(refs)
    prev_ref = refs.pop(0) if more else None
    own_ref, oth_ref, first_ref, sum_ref, acc = refs
    step, last = pl.program_id(0), pl.num_programs(0) - 1
    x = x_ref[0]
    grads = jnp.concatenate([r[h] for r in (q_ref, k_ref, v_ref) for h in range(3)], axis=1)
    made = dot(nt_ref[...], grads)
    total = jnp.sum(grads.astype(F32), axis=0, keepdims=True)

    @pl.when(step == 0)
    def _():
        acc[...] = made
        sum_ref[...] = total

    @pl.when(step > 0)
    def _():
        acc[...] += made
        sum_ref[...] += total

    back = dot(grads, w_ref[:, :576], NT)
    if more:
        back = back + prev_ref[...]
    first_ref[...] = back.astype(first_ref.dtype)

    @pl.when(step == last)
    def _():
        for z in range(ZS):
            for ref, side in ((own_ref, x), (oth_ref, 1 - x)):
                at = pl.multiple_of((2 * z + side) * rows, 32)
                ref[z] = jnp.concatenate(
                    [acc[pl.ds(at, rows), :].astype(BF), wo_ref[pl.ds(at, rows), :]], axis=1
                )


def first_back_body(
    x_ref, s0, s1, s2, s3, te_ref, vec_ref, g0_ref, g1_ref, gm_ref, second_ref, ho_ref, hy_ref, qo_ref, qy_ref,
    stays_ref, sent_ref, own_ref, oth_ref, sum_ref, *, rows,
):
    @pl.when(pl.program_id(0) == 0)
    def _():
        sum_ref[...] = jnp.zeros_like(sum_ref)

    xhat, rate = normalize(pick((s0, s1, s2, s3)).astype(F32) + te_ref[...].astype(F32))
    first = g0_ref[...].astype(F32) + g1_ref[...].astype(F32)
    scaled = first * vec_ref[0:1, :]
    inner = jnp.mean(scaled * xhat, axis=-1, keepdims=True)
    grad = gm_ref[...] + rate * (scaled - jnp.mean(scaled, axis=-1, keepdims=True) - xhat * inner)

    @pl.when(pl.program_id(0) == 0)
    def _():
        half = grad.shape[0] // 2
        stays_ref[...] = grad[:half].astype(BF)
        sent_ref[...] = grad[half:].astype(BF)

    sum_ref[0:1, :] += jnp.sum(first * xhat, axis=0, keepdims=True)
    sum_ref[1:2, :] += jnp.sum(first, axis=0, keepdims=True)
    sum_ref[2:3, :] += jnp.sum(grad, axis=0, keepdims=True)

    @pl.when(pl.program_id(0) == pl.num_programs(0) - 1)
    def _():
        n = rows // 4
        sums = sum_ref[0:3, :]
        shared = [sums[0:2], second_ref[2:3, :], second_ref[0:2, :], second_ref[3:4, :]]
        blank = jnp.zeros((1, rows - 2 * n), F32)
        for hidden, bias, ref, more in ((ho_ref, qo_ref, own_ref, []), (hy_ref, qy_ref, oth_ref, [sums[2:3]])):
            made = []
            kinds = jnp.concatenate(shared + [hidden[...]], axis=0)
            extra = jnp.concatenate(more + [jnp.zeros((KINDS - 1, kinds.shape[1]), F32)], axis=0) if more else None
            for k in range(ZS * XS):
                part = slice(k * rows, k * rows + rows)
                last = [bias[0:1, k * n : k * n + n], bias[0:1, 6 * HD + k * n : 6 * HD + k * n + n], blank]
                piece = [kinds[:, part], jnp.concatenate(last, axis=1)]
                made.append(jnp.concatenate(piece + ([extra[:, part]] if more else []), axis=0))
            for z in range(ZS):
                even, odd = made[2 * z], made[2 * z + 1]
                ref[0, z] = jnp.where(x_ref[0] == 0, even, odd)
                ref[1, z] = jnp.where(x_ref[0] == 0, odd, even)


def final_body(got_ref, p0_ref, p1_ref, p2_ref, p3_ref, q_ref, k_ref, v_ref, o_ref, *small, rows):
    total = got_ref[0].astype(F32)
    for z in range(1, got_ref.shape[0]):
        total = total + got_ref[z].astype(F32)
    width = 3 * HD
    q_ref[...] = total[:, :width]
    k_ref[...] = total[:, width : 2 * width]
    v_ref[...] = total[:, 2 * width : 3 * width]
    o_ref[...] = total[:, 3 * width :].T
    sums = (p0_ref[...] + p1_ref[...]) + (p2_ref[...] + p3_ref[...])
    n = rows // 4
    for k, ref in enumerate(small[:7]):
        ref[...] = sums[k : k + 1]
    small[7][...] = sums[7:8, :n]
    small[8][...] = sums[7:8, n : 2 * n]


def output_body(mid_ref, f0_ref, f1_ref, vec_ref, stays_ref, sent_ref):
    made = (mid_ref[...] + (f0_ref[...].astype(F32) + f1_ref[...].astype(F32)) + vec_ref[5:6, :]).astype(BF)

    @pl.when(pl.program_id(0) == 0)
    def _():
        stays_ref[...] = made

    @pl.when(pl.program_id(0) == 1)
    def _():
        sent_ref[...] = made


def swap(size):
    return [(i, size - 1 - i) for i in range(size)]


def to_y(values):
    return lax.ppermute(values, "y", swap(2))


def to_x(values):
    return lax.ppermute(values, "b", swap(2))


def to_core(values):
    return lax.ppermute(values, "c", swap(2))


def gather_z(values):
    got = [lax.ppermute(values, "a", [((i + k) % ZS, i) for i in range(ZS)]) for k in range(1, ZS)]
    return jnp.stack([values] + got)


def spread_z(values):
    return lax.all_to_all(values, "a", 0, 0, tiled=True)


def body(
    fast,
    inputs,
    time_embed,
    first_gain,
    first_shift,
    query_weight,
    query_bias,
    key_weight,
    value_weight,
    value_bias,
    output_weight,
    output_bias,
    second_gain,
    second_shift,
    hidden_weight,
    hidden_bias,
    down_weight,
    down_bias,
    cotangent,
):
    _, block, width = inputs.shape
    shard = query_weight.shape[0]
    rows = width // (ZS * XS)
    seq = 4 * block
    hidden = hidden_weight.shape[1]
    yi = lax.axis_index("y")
    xi = lax.axis_index("b") if fast else jnp.int32(0)
    zi = lax.axis_index("a") if fast else jnp.int32(0)
    x_arr = jnp.stack([xi.astype(jnp.int32), zi.astype(jnp.int32)])

    n_copies = ZS if fast else 1
    attn_pack, mlp_pack = call(
        pack_body,
        (1,),
        [kept((shard, hidden // 4))] * 3
        + [kept((hidden // 4, shard)), kept((shard, hidden)), kept((shard, hidden))]
        + [kept((1, shard))] * 7
        + [kept((1, query_bias.shape[0]))] * 2,
        [
            (sds((shard + KINDS, width), BF), kept((shard + KINDS, width))),
            (sds((n_copies, 2 * shard, width), BF), kept((n_copies, 2 * shard, width))),
        ],
        flops=1e6,
        moved=2e6,
        vmem=56,
    )(
        query_weight, key_weight, value_weight, output_weight, hidden_weight, down_weight.T,
        *(v[None] for v in (first_gain, first_shift, output_bias, second_gain, second_shift, down_bias, hidden_bias, query_bias, value_bias)),
    )

    inputs, cotangent, attn_pack = lax.optimization_barrier((inputs, cotangent, attn_pack))
    both = jnp.concatenate([inputs, cotangent], axis=1)
    stays = lax.dynamic_index_in_dim(both, yi, 0, keepdims=False)
    comes = to_y(lax.dynamic_index_in_dim(both, 1 - yi, 0, keepdims=False))
    stays_mate = to_core(stays)
    te = lax.dynamic_index_in_dim(time_embed, yi, 0, keepdims=True)

    if fast:
        attn_oo = gather_z(attn_pack)
        attn_oo, mlp_pack = lax.optimization_barrier((attn_oo, mlp_pack))
        attn_oo, comes, stays_mate = lax.optimization_barrier((attn_oo, comes, stays_mate))
        comes_mate = to_core(comes)
        attn_ox, attn_yo = to_x(attn_oo), to_y(attn_oo)
        attn_ox, attn_yo = lax.optimization_barrier((attn_ox, attn_yo))
        mlp_oo = spread_z(mlp_pack)
        attn_yx = (to_y(attn_ox[:, : rows // 2]), to_x(attn_yo[:, rows // 2 :]))
    else:
        def natural(values):
            full = lax.all_gather(values, ("a", "b"), axis=0, tiled=True)
            full = full.reshape(ZS, XS, rows, width)
            return full[:, 0], full[:, 1]

        gathered = lax.all_gather(attn_pack, ("a", "b"), axis=0, tiled=False)
        matrix = gathered[:, :shard].reshape(ZS, XS, rows, width)
        small = gathered[:, shard:, :shard]
        flat = small[:, :7].transpose(1, 0, 2).reshape(7, width)
        n = shard // 4
        bias = [small[:, 7, k * n : k * n + n].reshape(ZS * XS, -1) for k in range(2)]
        bias = jnp.concatenate([*bias, jnp.zeros((ZS * XS, rows - 2 * (rows // 4)), BF)], axis=1)
        small = jnp.concatenate([flat, bias.reshape(1, width)], axis=0)
        small = small.reshape(KINDS, ZS, XS, rows).transpose(1, 2, 0, 3)
        small = jnp.pad(small, ((0, 0), (0, 0), (0, 0), (0, width - rows)))
        matrix = jnp.concatenate([matrix, small], axis=2)
        attn_oo, attn_ox = matrix[:, 0], matrix[:, 1]
        attn_yo, attn_yx = to_y(attn_oo), (to_y(attn_ox),)
        comes_mate = to_core(comes)
        h_oo, h_ox = natural(mlp_pack[0, :shard])
        d_oo, d_ox = natural(mlp_pack[0, shard:])
        mlp_oo = jnp.concatenate([h_oo, d_oo], axis=1)
        mlp_ox = jnp.concatenate([h_ox, d_ox], axis=1)

    def by(tile):
        return pl.BlockSpec((tile, width), lambda i: (i, 0))

    def by_mate(tile):
        tiles = seq // tile
        return pl.BlockSpec((tile, width), lambda i: ((i + tiles // 2) % tiles, 0))

    def low_half(tile):
        last = seq // tile // 2 - 1
        return pl.BlockSpec((tile, width), lambda i: (jnp.minimum(i, last), 0))

    def high_half(tile):
        first = seq // tile // 2
        return pl.BlockSpec((tile, width), lambda i: (jnp.maximum(i - first, 0), 0))

    tokens = tuple(far(v) for v in (stays, comes, stays_mate, comes_mate))
    start_blocks = [pl.BlockSpec((block, width), lambda *_: (0, 0), pipeline_mode=pl.Buffered(1))] * 4
    cot_blocks = [pl.BlockSpec((block, width), lambda *_: (1, 0), pipeline_mode=pl.Buffered(1))] * 4
    row = kept((1, width))
    vecs = kept((KINDS, width))
    square = whole((width, width))
    n_qkv = 9 * HD

    def project(first, source, *shards):
        tile = TILE_PROJECT
        outs = [
            (sds((width, width), BF), kept((width, width))),
            (sds((KINDS, width), F32), vecs),
            (pltpu.HBM((9, seq, HD), BF), pl.BlockSpec((9, tile, HD), lambda i: (0, i, 0))),
        ]
        if first:
            outs += [
                (pltpu.HBM((seq, width), BF), by(tile)),
                (pltpu.HBM((width, seq), BF), pl.BlockSpec((width, tile), lambda i: (0, i))),
            ]
        return call(
            functools.partial(project_body, rows=rows, first=first),
            (seq // tile,),
            [scalar()] + (start_blocks + [row] if first else [by(tile)]) + [whole(v.shape) for v in shards],
            outs,
            scratch=[pltpu.VMEM((8, n_qkv), F32)],
            flops=2 * seq * width * n_qkv,
            moved=8e6,
        )(x_arr, *source, *shards)

    q_spec = pl.BlockSpec((1, seq, HD), lambda h: (h, 0, 0))
    k_spec = pl.BlockSpec((1, seq, HD), lambda h: (3 + h, 0, 0))
    v_spec = pl.BlockSpec((1, seq, HD), lambda h: (6 + h, 0, 0))
    e_spec = pl.BlockSpec((1, seq, seq), lambda h: (h, 0, 0))
    inv_spec = pl.BlockSpec((1, 1, seq), lambda h: (h, 0, 0))
    t_spec = pl.BlockSpec((1, HD, seq), lambda h: (h, 0, 0))

    def attend(qkv):
        return call(
            attend_body,
            (3,),
            [q_spec, k_spec, v_spec],
            [
                (pltpu.HBM((3, seq, seq), BF), e_spec),
                (sds((3, 1, seq), F32), inv_spec),
                (sds((3, HD, seq), BF), t_spec),
                (pltpu.HBM((3, HD, seq), F32), t_spec),
            ],
            flops=3 * 16 * seq * seq * HD,
            moved=8e6,
            trans=3 * seq * seq,
        )(*[far(qkv)] * 3)

    def attend_back(qkv, expon, inverse, mixed, grad_mixed, keep):
        made = keep((3, seq, HD), BF)
        return call(
            attend_back_body,
            (3,),
            [q_spec, k_spec, v_spec, e_spec, inv_spec, t_spec, t_spec],
            [(made, q_spec)] * 3,
            flops=3 * 40 * seq * seq * HD,
            moved=9e6,
        )(*[far(qkv)] * 3, far(expon), inverse, far(mixed), grad_mixed)

    w_o, vec, qkv_o, normed, normed_t = project(True, (*tokens, te), attn_oo, attn_ox)
    qkv_o, attn_yx, mlp_oo = lax.optimization_barrier((qkv_o, attn_yx, mlp_oo))
    mlp_yo = to_y(mlp_oo)
    if fast:
        mlp_ox = to_x(mlp_oo)
    exp_o, inv_o, mixed_o, wide_o = attend(qkv_o)
    normed, exp_o = lax.optimization_barrier((normed, exp_o))
    w_y, vec_y, qkv_y = project(False, (far(normed),), attn_yo, *attn_yx)
    exp_y, inv_y, mixed_y, wide_y = attend(qkv_y)
    mixed_y, mlp_ox, mlp_yo = lax.optimization_barrier((mixed_y, mlp_ox, mlp_yo))
    h_yx = to_y(mlp_ox[:, :rows])
    d_yx = to_x(mlp_yo[:, rows:]) if fast else to_y(mlp_ox[:, rows:])

    tile = TILE_OUT
    half_t = pl.BlockSpec((3 * HD, tile), lambda i: (0, i))
    flat_o, flat_y = mixed_o.reshape(3 * HD, seq), mixed_y.reshape(3 * HD, seq)
    (attended,) = call(
        outproj_body,
        (seq // tile,),
        [half_t, half_t, square, square],
        [(sds((seq, width), BF), by(tile))],
        scratch=[pltpu.VMEM((width, 6 * HD), BF)],
        flops=2 * seq * width * 384,
        moved=6e6,
    )(flat_o, flat_y, w_o, w_y)
    attended_mate = to_core(attended)

    tile = TILE_MLP
    part = (ZS, rows, hidden)
    grad_parts = [(sds((1, hidden), F32), kept((1, hidden)))] + [(sds(part, BF), kept(part))] * 4
    mlp_scratch = [pltpu.VMEM((width, hidden), t) for t in (BF, BF, F32, F32)]
    mlp_cost = dict(flops=12 * seq * width * hidden, moved=16e6, trans=seq * hidden * 2, vmem=24)
    middle, normed_second, ff_part, gs_part, hb_o, gh_oo, gh_ox, gd_oo, gd_ox = call(
        functools.partial(mlp_first_body, rows=rows),
        (seq // tile,),
        [scalar(), *start_blocks, row, by(tile), by_mate(tile), *cot_blocks, vecs]
        + [whole((ZS, 2 * rows, hidden))] * 2,
        [
            (sds((seq, width), F32), by(tile)),
            (sds((seq, width), BF), by(tile)),
            (sds((seq, width), F32), by(tile)),
            (sds((seq, width), F32), by(tile)),
        ]
        + grad_parts,
        scratch=mlp_scratch,
        **mlp_cost,
    )(x_arr, *tokens, te, attended, attended_mate, *tokens, vec, mlp_oo, mlp_ox)
    if fast:
        got_ho = to_x(gh_ox)
        normed_second, h_yx, d_yx = lax.optimization_barrier((normed_second, h_yx, d_yx))
    ff, ff_sent, gs, hb_y, gh_yo, gh_yx, gd_yo, gd_yx = call(
        functools.partial(mlp_second_body, rows=rows),
        (seq // tile,),
        [scalar(), by(tile), *cot_blocks, vecs, by(tile), by(tile)]
        + [whole((ZS, 2 * rows, hidden)), whole(part), whole(part)],
        [
            (sds((seq // 2, width), BF), low_half(tile)),
            (sds((seq // 2, width), BF), high_half(tile)),
            (sds((seq, width), BF), by(tile)),
        ]
        + grad_parts,
        scratch=mlp_scratch,
        **mlp_cost,
    )(x_arr, normed_second, *tokens, vec_y, ff_part, gs_part, mlp_yo, h_yx, d_yx)
    if fast:
        gs, got_ho = lax.optimization_barrier((gs, got_ho))
    gs_mate = to_core(gs)
    ff_mate = to_core(ff_sent)

    tile = TILE_SECOND
    half_t = pl.BlockSpec((3 * HD, tile), lambda i: (0, i))
    grad_middle, gx_o, gx_y, wo_o, wo_y, second_sums = call(
        second_back_body,
        (seq // tile,),
        [by(tile), by(tile), by_mate(tile), *cot_blocks, vecs, square, square, half_t, half_t],
        [
            (pltpu.HBM((seq, width), F32), by(tile)),
            (sds((3 * HD, seq), BF), half_t),
            (sds((3 * HD, seq), BF), half_t),
            (pltpu.HBM((width, 3 * HD), BF), kept((width, 3 * HD))),
            (pltpu.HBM((width, 3 * HD), BF), kept((width, 3 * HD))),
            (sds((KINDS, width), F32), vecs),
        ],
        scratch=[pltpu.VMEM((width, 6 * HD), BF), pltpu.VMEM((width, 6 * HD), F32)],
        flops=4 * seq * width * 384,
        moved=16e6,
    )(middle, gs, gs_mate, *tokens, vec, w_o, w_y, flat_o, flat_y)
    if fast:
        got_h, got_d = to_x(gh_yx), to_y(gd_yx)
        gx_y, got_h, got_d = lax.optimization_barrier((gx_y, got_h, got_d))
        got_hs, got_ds = to_y(gh_yo + got_h), to_x(gd_ox + got_d)

    def project_back(grads, weights, wo, prev):
        tile = TILE_BACK
        more = prev is not None
        heads = pl.BlockSpec((3, tile, HD), lambda i: (0, i, 0))
        attn_part = (ZS, rows, width)
        return call(
            functools.partial(project_back_body, rows=rows, more=more),
            (seq // tile,),
            [scalar(), heads, heads, heads, pl.BlockSpec((width, tile), lambda i: (0, i)), square, whole((width, 3 * HD))]
            + ([by(tile)] if more else []),
            [
                (pltpu.HBM(attn_part, BF), kept(attn_part)),
                (pltpu.HBM(attn_part, BF), kept(attn_part)),
                ((sds((seq, width), BF) if more else pltpu.HBM((seq, width), F32)), by(tile)),
                (sds((1, n_qkv), F32), kept((1, n_qkv))),
            ],
            scratch=[pltpu.VMEM((width, n_qkv), F32)],
            flops=4 * seq * width * n_qkv,
            moved=10e6,
        )(x_arr, *(far(v) if more else v for v in grads), far(normed_t), weights, far(wo), *((far(prev),) if more else ()))

    grads_y = attend_back(qkv_y, exp_y, inv_y, wide_y, gx_y.reshape(3, HD, seq), sds)
    ga_yo, ga_yx, first_part, qkv_sum_y = project_back(grads_y, w_y, wo_y, None)
    tile = block
    out_stays, out_tokens = call(
        output_body,
        (2,),
        [by(tile), by(tile), by(tile), vecs],
        [(sds((block, width), BF), kept((block, width)))] * 2,
        flops=1e6,
        moved=5e6,
    )(middle, ff, ff_mate, vec)
    gx_o, first_part, out_tokens = lax.optimization_barrier((gx_o, first_part, out_tokens))
    if fast:
        gx_o, ga_yx, got_hs, got_ds, gd_yo = lax.optimization_barrier((gx_o, ga_yx, got_hs, got_ds, gd_yo))
        got_do = to_y(gd_yo)
        ga_d = to_x(ga_yx)
    grads_o = attend_back(qkv_o, exp_o, inv_o, wide_o, gx_o.reshape(3, HD, seq), pltpu.HBM)
    if fast:
        *grads_o, got_do, ga_d, out_tokens = lax.optimization_barrier((*grads_o, got_do, ga_d, out_tokens))
        out_got = to_y(out_tokens)
        mlp_all = spread_z(jnp.concatenate([gh_oo + got_ho + got_hs, gd_oo + got_do + got_ds], axis=1))
        ga_s = to_y(ga_yo + ga_d)
    ga_oo, ga_ox, first, qkv_sum_o = project_back(grads_o, w_o, wo_o, first_part)
    if fast:
        ga_x = to_x(ga_ox)
        first, out_got = lax.optimization_barrier((first, out_got))
    first_mate = to_core(first)

    tile = TILE_FIRST
    hb_spec, qkv_spec = kept((1, hidden)), kept((1, n_qkv))
    small_o_shape, small_y_shape = (XS, ZS, KINDS, rows), (XS, ZS, 2 * KINDS, rows)
    in_stays, input_grad, small_o, small_y, first_sums = call(
        functools.partial(first_back_body, rows=rows),
        (seq // tile,),
        [scalar(), *start_blocks, row, vecs, by(tile), by_mate(tile), by(tile), vecs, hb_spec, hb_spec, qkv_spec, qkv_spec],
        [(sds((seq // 4, width), BF), kept((seq // 4, width)))] * 2
        + [
            (sds(small_o_shape, F32), kept(small_o_shape)),
            (sds(small_y_shape, F32), kept(small_y_shape)),
            (sds((KINDS, width), F32), vecs),
        ],
        flops=0,
        moved=0,
    )(x_arr, *tokens, te, vec, first, first_mate, far(grad_middle), second_sums, hb_o, hb_y, qkv_sum_o, qkv_sum_y)

    small_got = to_y(small_y)
    if fast:
        small_got, input_grad, ga_x, ga_s, mlp_all = lax.optimization_barrier(
            (small_got, input_grad, ga_x, ga_s, mlp_all)
        )
        ga_all = spread_z(ga_oo + ga_s + ga_x)
    small_sum = small_o + small_got[:, :, :KINDS]
    embed = first_sums[2]
    embed_got = jnp.where(xi == 0, small_got, small_got[::-1])[:, :, KINDS].transpose(1, 0, 2).reshape(width)
    embed_gradient = jnp.where(yi == 0, jnp.stack([embed, embed_got]), jnp.stack([embed_got, embed]))
    n_bias = query_bias.shape[0]
    n_head = query_weight.shape[1]
    if fast:
        small_sum = small_sum[0] + to_x(small_sum[1])
        zi = lax.axis_index("a")
        pieces = [lax.dynamic_index_in_dim(small_sum, (zi + k) % ZS, 0, keepdims=False) for k in range(ZS)]
        pieces = [lax.ppermute(v, "a", [(i, (i + k) % ZS) for i in range(ZS)]) if k else v for k, v in enumerate(pieces)]
        *weights, fg, fs, ob, sg, ss, db, hb, qb, vb = call(
            functools.partial(final_body, rows=rows),
            (1,),
            [kept(ga_all.shape)] + [kept((KINDS, rows))] * ZS,
            [(sds((shard, n_head), F32), kept((shard, n_head)))] * 3
            + [(sds((n_head, shard), F32), kept((n_head, shard)))]
            + [(sds((1, shard), F32), kept((1, shard)))] * 7
            + [(sds((1, n_bias), F32), kept((1, n_bias)))] * 2,
            flops=1e6,
            moved=2e6,
        )(ga_all, *pieces)
        vectors = [v[0] for v in (fg, fs, ob, sg, ss, db, hb, qb, vb)]
        mlp_sum = jnp.sum(mlp_all.astype(F32), axis=0)
        gh, gd = mlp_sum[:shard], mlp_sum[shard:].T
    else:

        def scatter(values):
            return lax.psum_scatter(values, ("a", "b"), scatter_dimension=0, tiled=True)

        def scatter_slow(oo, ox, yo, yx):
            own, oth = oo + to_y(yo), ox + to_y(yx)
            return scatter(jnp.stack([own, oth], axis=1).reshape(width, -1).astype(F32))

        kinds = small_sum.transpose(2, 1, 0, 3)
        bias = kinds[7].reshape(ZS * XS, rows)
        split = rows // 4
        vectors = [scatter(v) for v in kinds[:7].reshape(7, width)]
        vectors += [scatter(bias[:, k * split : k * split + split].reshape(-1)) for k in range(2)]
        gh = scatter_slow(gh_oo, gh_ox, gh_yo, gh_yx)
        gd = scatter_slow(gd_oo, gd_ox, gd_yo, gd_yx).T
        ga = scatter_slow(ga_oo, ga_ox, ga_yo, ga_yx)
        weights = [ga[:, k * n_head : k * n_head + n_head] for k in range(4)]
        weights[3] = weights[3].T

    def placed(stays, got):
        return jnp.where(yi == 0, jnp.stack([stays, got]), jnp.stack([got, stays]))

    if not fast:
        out_got = to_y(out_tokens)
    block_output = placed(out_stays, out_got)
    input_gradient = placed(in_stays, to_y(input_grad))

    fg, fs, ob, sg, ss, db, hb, qb, vb = vectors
    return (
        block_output, input_gradient, embed_gradient, fg, fs, weights[0], qb, weights[1], weights[2], vb,
        weights[3], ob, sg, ss, gh, hb, gd, db,
    )


def solution(mesh):
    dp, tensor = mesh.shape["dp"], mesh.shape["tensor"]
    fine = Mesh(mesh.devices.reshape(dp // 2, 2, tensor // 2, 2), ("a", "b", "y", "c"))
    by_dp, by_tensor = ("a", "b"), ("y", "c")
    both = by_tensor + by_dp
    column, matrix, turned = P(by_dp), P(by_dp, by_tensor), P(by_tensor, by_dp)
    seqs = P(by_dp, by_tensor, None)
    return jax.shard_map(
        functools.partial(body, dp == ZS * XS),
        mesh=fine,
        in_specs=(
            seqs, P(by_dp, None), column, column, matrix, P(both), matrix, matrix, P(both), turned,
            column, column, column, matrix, P(both), turned, column, seqs,
        ),
        out_specs=(
            seqs, seqs, P(by_dp, None), column, column, matrix, P(both), matrix, matrix, P(both), turned,
            column, column, column, matrix, P(both), turned, column,
        ),
        check_vma=False,
    )
```

```python
import functools

import jax
import jax.numpy as jnp
from jax import lax
from jax.experimental import pallas as pl
from jax.experimental.pallas import tpu as pltpu
from jax.sharding import Mesh
from jax.sharding import PartitionSpec as P

HD = 64
EPSILON = 1e-05
SCALE = 0.125
BF = jnp.bfloat16
F32 = jnp.float32
ZS, XS = 4, 2
KINDS = 8
HINT = 1.0
TILE_PROJECT = 512
TILE_OUT = 512
TILE_MLP = 512
TILE_SECOND = 512
TILE_BACK = 1024
TILE_FIRST = 512

NN = (((1,), (0,)), ((), ()))
NT = (((1,), (1,)), ((), ()))


def dot(left, right, dims=NN):
    return lax.dot_general(left, right, dims, preferred_element_type=F32)


def call(body, grid, ins, outs, scratch=(), flops=0, moved=0, trans=0, vmem=16):
    return pl.pallas_call(
        body,
        grid=grid,
        in_specs=[s for s in ins],
        out_specs=[s for _, s in outs],
        out_shape=[o for o, _ in outs],
        scratch_shapes=list(scratch),
        compiler_params=pltpu.CompilerParams(vmem_limit_bytes=vmem << 20),
        cost_estimate=pl.CostEstimate(flops=int(flops * HINT), bytes_accessed=int(moved * HINT), transcendentals=int(trans * HINT)),
    )


def whole(shape, n=1):
    zeros = (0,) * len(shape)
    return pl.BlockSpec(shape, lambda *_: zeros, pipeline_mode=pl.Buffered(1))


def kept(shape):
    zeros = (0,) * len(shape)
    return pl.BlockSpec(shape, lambda *_: zeros)


def far(values):
    return pltpu.with_memory_space_constraint(values, pltpu.HBM)


def scalar():
    return pl.BlockSpec(memory_space=pltpu.SMEM)


def sds(shape, dtype):
    return jax.ShapeDtypeStruct(shape, dtype)


def place(x_ref, k, side, rows):
    x = x_ref[0] if side == 0 else 1 - x_ref[0]
    return pl.multiple_of((2 * lax.rem(x_ref[1] + k, ZS) + x) * rows, 32)


def shard_of(refs, z, rows):
    parts = [r[z] for r in refs]
    value = parts[0] if len(parts) == 1 else jnp.concatenate(parts, axis=0)
    return value[:rows], value[rows:]


def normalize(values):
    center = values - jnp.mean(values, axis=-1, keepdims=True)
    spread = jnp.mean(center * center, axis=-1, keepdims=True)
    rate = lax.rsqrt(spread + EPSILON)
    return center * rate, rate


def pack_body(q_ref, k_ref, v_ref, o_ref, h_ref, d_ref, fg, fs, ob, sg, ss, db, hb, qb, vb, attn_ref, mlp_ref):
    shard = q_ref.shape[0]
    low = jnp.concatenate([q_ref[...], k_ref[...], v_ref[...], o_ref[...].T], axis=1)
    n = qb.shape[1]
    bias = jnp.concatenate([qb[...], vb[...], jnp.zeros((1, shard - 2 * n), BF)], axis=1)
    small = jnp.concatenate([r[...].astype(F32) for r in (fg, fs, ob, sg, ss, db, hb)] + [bias.astype(F32)], axis=0)
    small = jnp.concatenate([small, jnp.zeros((KINDS, low.shape[1] - shard), F32)], axis=1).astype(BF)
    high, down = h_ref[...], d_ref[...]
    attn_ref[:shard, :] = low
    attn_ref[shard:, :] = small
    for z in range(mlp_ref.shape[0]):
        mlp_ref[z, :shard, :] = high
        mlp_ref[z, shard:, :] = down


def pick(refs):
    step, each = pl.program_id(0), len(refs) // pl.num_programs(0)
    blocks = [r[...] for r in refs]
    tiles = [blocks[k : k + each] for k in range(0, len(blocks), each)]
    tiles = [t[0] if each == 1 else jnp.concatenate(t, axis=0) for t in tiles]
    value = tiles[0]
    for k in range(1, len(tiles)):
        value = jnp.where(step == k, tiles[k], value)
    return value


def project_body(x_ref, *refs, rows, first):
    refs = list(refs)
    if first:
        *tokens, te_ref, own_ref, oth_ref, w_ref, vec_ref, qkv_ref, normed_ref, bias_ref = refs
        oth_refs = (oth_ref,)
    else:
        source_ref, own_ref, *oth_refs, w_ref, vec_ref, qkv_ref, normed_t_ref, bias_ref = refs

    @pl.when(pl.program_id(0) == 0)
    def _():
        own, oth = [], []
        for k in range(ZS):
            weight, small = shard_of((own_ref,), k, rows)
            w_ref[pl.ds(place(x_ref, k, 0, rows), rows), :] = weight
            own.append(small[:, :rows].astype(F32))
            weight, small = shard_of(oth_refs, k, rows)
            w_ref[pl.ds(place(x_ref, k, 1, rows), rows), :] = weight
            oth.append(small[:, :rows].astype(F32))
        even = jnp.concatenate([v for pair in zip(own, oth) for v in pair], axis=1)
        odd = jnp.concatenate([v for pair in zip(oth, own) for v in pair], axis=1)
        vec = jnp.where(x_ref[0] == 0, even, odd)
        vec = pltpu.roll(vec, x_ref[1] * (2 * rows), 1)
        vec_ref[...] = vec
        n = rows // 4
        last = vec[7:8, :]
        parts = [last[:, rows * k : rows * k + n] for k in range(ZS * XS)]
        parts += [jnp.zeros((1, 3 * HD), F32)]
        parts += [last[:, rows * k + n : rows * k + 2 * n] for k in range(ZS * XS)]
        bias_ref[0:1, :] = jnp.concatenate(parts, axis=1)

    if first:
        xhat, _ = normalize(pick(tokens).astype(F32) + te_ref[...].astype(F32))
        normed = (xhat * vec_ref[0:1, :] + vec_ref[1:2, :]).astype(BF)
        normed_ref[...] = normed
    else:
        normed = source_ref[...]
        normed_t_ref[...] = normed.T
    made = dot(normed, w_ref[:, :640])[:, :576] + bias_ref[0:1, :]
    made = made.astype(BF)
    for j in range(9):
        piece = made[:, 64 * j : 64 * j + 64]
        qkv_ref[j] = piece * BF(SCALE) if j < 3 else piece


def attend_body(q_ref, k_ref, v_ref, e_ref, inv_ref, mixed_ref, wide_ref):
    scores = dot(k_ref[0], q_ref[0], NT)
    expon = jnp.exp(scores - jnp.max(scores, axis=0, keepdims=True))
    inverse = 1.0 / jnp.sum(expon, axis=0, keepdims=True)
    low = expon.astype(BF)
    e_ref[0] = low
    inv_ref[0] = inverse
    wide = dot(v_ref[0].T, low) * inverse
    mixed_ref[0] = wide.astype(BF)
    wide_ref[0] = wide


def attend_back_body(q_ref, k_ref, v_ref, e_ref, inv_ref, mixed_ref, gm_ref, dq_ref, dk_ref, dv_ref):
    low = (gm_ref[0].astype(F32) * inv_ref[0]).astype(BF)
    inner = jnp.sum(low.astype(F32) * mixed_ref[0], axis=0, keepdims=True)
    expon = e_ref[0]
    grad_scores = (expon.astype(F32) * (dot(v_ref[0], low) - inner)).astype(BF)
    dv_ref[0] = dot(expon, low, NT).astype(BF)
    dk_ref[0] = dot(grad_scores, q_ref[0]).astype(BF)
    dq_ref[0] = (dot(k_ref[0].T, grad_scores) * SCALE).T.astype(BF)


def outproj_body(m0_ref, m1_ref, w0_ref, w1_ref, out_ref, wo_ref):
    @pl.when(pl.program_id(0) == 0)
    def _():
        wo_ref[...] = jnp.concatenate([w0_ref[:, 576:], w1_ref[:, 576:]], axis=1)

    mixed = jnp.concatenate([m0_ref[...], m1_ref[...]], axis=0).T
    out_ref[...] = dot(mixed, wo_ref[...], NT).astype(BF)


def feed(normed, cot, wh, wd, bias, acc_h, acc_d, hbg_ref):
    pre = dot(normed, wh[...]) + bias
    below = 0.5 + 0.5 * lax.erf(pre * 0.7071067811865476)
    act = (pre * below).astype(BF)
    slope = below + pre * (jnp.exp(-0.5 * pre * pre) * 0.3989422804014327)
    grad = (dot(cot, wd[...]) * slope).astype(BF)
    acc_h[...] += dot(normed.T, grad)
    acc_d[...] += dot(cot.T, act)
    hbg_ref[...] += jnp.sum(grad.astype(F32), axis=0, keepdims=True)
    return dot(act, wd[...], NT), dot(grad, wh[...], NT)


def fill(x, rows, own, oth, wh, wd, acc_h, acc_d, hbg_ref):
    for z in range(ZS):
        for refs, side in ((own, x), (oth, 1 - x)):
            at = pl.multiple_of((2 * z + side) * rows, 32)
            wh[pl.ds(at, rows), :], wd[pl.ds(at, rows), :] = shard_of(refs, z, rows)
    for ref in (acc_h, acc_d, hbg_ref):
        ref[...] = jnp.zeros_like(ref)


def drain(x, rows, acc, own, oth):
    for z in range(ZS):
        own[z] = acc[pl.ds(pl.multiple_of((2 * z + x) * rows, 32), rows), :].astype(BF)
        oth[z] = acc[pl.ds(pl.multiple_of((2 * z + 1 - x) * rows, 32), rows), :].astype(BF)


def mlp_first_body(
    x_ref, s0, s1, s2, s3, te_ref, a0_ref, a1_ref, c0, c1, c2, c3, vec_ref, w_oo, w_ox,
    mid_ref, normed_ref, ff_ref, gs_ref, hbg_ref, gh_o, gh_x, gd_o, gd_x,
    wh, wd, acc_h, acc_d, *, rows,
):
    x = x_ref[0]

    @pl.when(pl.program_id(0) == 0)
    def _():
        fill(x, rows, (w_oo,), (w_ox,), wh, wd, acc_h, acc_d, hbg_ref)

    middle = (
        pick((s0, s1, s2, s3)).astype(F32)
        + te_ref[...].astype(F32)
        + (a0_ref[...].astype(F32) + a1_ref[...].astype(F32))
        + vec_ref[2:3, :]
    )
    mid_ref[...] = middle
    xhat, _ = normalize(middle)
    normed = (xhat * vec_ref[3:4, :] + vec_ref[4:5, :]).astype(BF)
    normed_ref[...] = normed
    ff_ref[...], gs_ref[...] = feed(normed, pick((c0, c1, c2, c3)), wh, wd, vec_ref[6:7, :], acc_h, acc_d, hbg_ref)

    @pl.when(pl.program_id(0) == pl.num_programs(0) - 1)
    def _():
        drain(x, rows, acc_h, gh_o, gh_x)
        drain(x, rows, acc_d, gd_o, gd_x)


def mlp_second_body(
    x_ref, normed_ref, c0, c1, c2, c3, vec_ref, f_ref, g_ref, w_yo, h_yx, d_yx,
    ff0_ref, ff1_ref, gs_ref, hbg_ref, gh_o, gh_x, gd_o, gd_x,
    wh, wd, acc_h, acc_d, *, rows,
):
    x = x_ref[0]

    @pl.when(pl.program_id(0) == 0)
    def _():
        fill(x, rows, (w_yo,), (h_yx, d_yx), wh, wd, acc_h, acc_d, hbg_ref)

    ff, gs = feed(normed_ref[...], pick((c0, c1, c2, c3)), wh, wd, vec_ref[6:7, :], acc_h, acc_d, hbg_ref)
    gs_ref[...] = (g_ref[...] + gs).astype(BF)
    ff = (f_ref[...] + ff).astype(BF)
    half = pl.num_programs(0) // 2

    @pl.when(pl.program_id(0) < half)
    def _():
        ff0_ref[...] = ff

    @pl.when(pl.program_id(0) >= half)
    def _():
        ff1_ref[...] = ff

    @pl.when(pl.program_id(0) == pl.num_programs(0) - 1)
    def _():
        drain(x, rows, acc_h, gh_o, gh_x)
        drain(x, rows, acc_d, gd_o, gd_x)


def second_back_body(mid_ref, g0_ref, g1_ref, c0, c1, c2, c3, vec_ref, w0_ref, w1_ref, m0_ref, m1_ref, gm_ref, x0_ref, x1_ref, wo0_ref, wo1_ref, sum_ref, wo_ref, acc):
    step, last = pl.program_id(0), pl.num_programs(0) - 1

    @pl.when(step == 0)
    def _():
        wo_ref[...] = jnp.concatenate([w0_ref[:, 576:], w1_ref[:, 576:]], axis=1)
        acc[...] = jnp.zeros_like(acc)
        sum_ref[...] = jnp.zeros_like(sum_ref)

    xhat, rate = normalize(mid_ref[...])
    second = g0_ref[...].astype(F32) + g1_ref[...].astype(F32)
    cot = pick((c0, c1, c2, c3)).astype(F32)
    scaled = second * vec_ref[3:4, :]
    inner = jnp.mean(scaled * xhat, axis=-1, keepdims=True)
    grad = cot + rate * (scaled - jnp.mean(scaled, axis=-1, keepdims=True) - xhat * inner)
    gm_ref[...] = grad
    sum_ref[0:1, :] += jnp.sum(second * xhat, axis=0, keepdims=True)
    sum_ref[1:2, :] += jnp.sum(second, axis=0, keepdims=True)
    sum_ref[2:3, :] += jnp.sum(grad, axis=0, keepdims=True)
    sum_ref[3:4, :] += jnp.sum(cot, axis=0, keepdims=True)
    low = grad.astype(BF)
    back = dot(low, wo_ref[...]).astype(BF).T
    x0_ref[...] = back[:192]
    x1_ref[...] = back[192:]
    mixed = jnp.concatenate([m0_ref[...], m1_ref[...]], axis=0)
    acc[...] += dot(low.T, mixed, NT)

    @pl.when(step == last)
    def _():
        wo0_ref[...] = acc[:, :192].astype(BF)
        wo1_ref[...] = acc[:, 192:].astype(BF)


def project_back_body(x_ref, q_ref, k_ref, v_ref, nt_ref, w_ref, wo_ref, *refs, rows, more):
    refs = list(refs)
    prev_ref = refs.pop(0) if more else None
    own_ref, oth_ref, first_ref, sum_ref, acc = refs
    step, last = pl.program_id(0), pl.num_programs(0) - 1
    x = x_ref[0]
    grads = jnp.concatenate([r[h] for r in (q_ref, k_ref, v_ref) for h in range(3)], axis=1)
    made = dot(nt_ref[...], grads)
    total = jnp.sum(grads.astype(F32), axis=0, keepdims=True)

    @pl.when(step == 0)
    def _():
        acc[...] = made
        sum_ref[...] = total

    @pl.when(step > 0)
    def _():
        acc[...] += made
        sum_ref[...] += total

    back = dot(grads, w_ref[:, :576], NT)
    if more:
        back = back + prev_ref[...]
    first_ref[...] = back.astype(first_ref.dtype)

    @pl.when(step == last)
    def _():
        for z in range(ZS):
            for ref, side in ((own_ref, x), (oth_ref, 1 - x)):
                at = pl.multiple_of((2 * z + side) * rows, 32)
                ref[z] = jnp.concatenate(
                    [acc[pl.ds(at, rows), :].astype(BF), wo_ref[pl.ds(at, rows), :]], axis=1
                )


def first_back_body(
    x_ref, s0, s1, s2, s3, te_ref, vec_ref, g0_ref, g1_ref, gm_ref, second_ref, ho_ref, hy_ref, qo_ref, qy_ref,
    stays_ref, sent_ref, own_ref, oth_ref, sum_ref, *, rows,
):
    @pl.when(pl.program_id(0) == 0)
    def _():
        sum_ref[...] = jnp.zeros_like(sum_ref)

    xhat, rate = normalize(pick((s0, s1, s2, s3)).astype(F32) + te_ref[...].astype(F32))
    first = g0_ref[...].astype(F32) + g1_ref[...].astype(F32)
    scaled = first * vec_ref[0:1, :]
    inner = jnp.mean(scaled * xhat, axis=-1, keepdims=True)
    grad = gm_ref[...] + rate * (scaled - jnp.mean(scaled, axis=-1, keepdims=True) - xhat * inner)

    @pl.when(pl.program_id(0) == 0)
    def _():
        half = grad.shape[0] // 2
        stays_ref[...] = grad[:half].astype(BF)
        sent_ref[...] = grad[half:].astype(BF)

    sum_ref[0:1, :] += jnp.sum(first * xhat, axis=0, keepdims=True)
    sum_ref[1:2, :] += jnp.sum(first, axis=0, keepdims=True)
    sum_ref[2:3, :] += jnp.sum(grad, axis=0, keepdims=True)

    @pl.when(pl.program_id(0) == pl.num_programs(0) - 1)
    def _():
        n = rows // 4
        sums = sum_ref[0:3, :]
        shared = [sums[0:2], second_ref[2:3, :], second_ref[0:2, :], second_ref[3:4, :]]
        blank = jnp.zeros((1, rows - 2 * n), F32)
        for hidden, bias, ref, more in ((ho_ref, qo_ref, own_ref, []), (hy_ref, qy_ref, oth_ref, [sums[2:3]])):
            made = []
            kinds = jnp.concatenate(shared + [hidden[...]], axis=0)
            extra = jnp.concatenate(more + [jnp.zeros((KINDS - 1, kinds.shape[1]), F32)], axis=0) if more else None
            for k in range(ZS * XS):
                part = slice(k * rows, k * rows + rows)
                last = [bias[0:1, k * n : k * n + n], bias[0:1, 6 * HD + k * n : 6 * HD + k * n + n], blank]
                piece = [kinds[:, part], jnp.concatenate(last, axis=1)]
                made.append(jnp.concatenate(piece + ([extra[:, part]] if more else []), axis=0))
            for z in range(ZS):
                even, odd = made[2 * z], made[2 * z + 1]
                ref[0, z] = jnp.where(x_ref[0] == 0, even, odd)
                ref[1, z] = jnp.where(x_ref[0] == 0, odd, even)


def final_body(got_ref, p0_ref, p1_ref, p2_ref, p3_ref, q_ref, k_ref, v_ref, o_ref, *small, rows):
    total = got_ref[0].astype(F32)
    for z in range(1, got_ref.shape[0]):
        total = total + got_ref[z].astype(F32)
    width = 3 * HD
    q_ref[...] = total[:, :width]
    k_ref[...] = total[:, width : 2 * width]
    v_ref[...] = total[:, 2 * width : 3 * width]
    o_ref[...] = total[:, 3 * width :].T
    sums = (p0_ref[...] + p1_ref[...]) + (p2_ref[...] + p3_ref[...])
    n = rows // 4
    for k, ref in enumerate(small[:7]):
        ref[...] = sums[k : k + 1]
    small[7][...] = sums[7:8, :n]
    small[8][...] = sums[7:8, n : 2 * n]


def output_body(mid_ref, f0_ref, f1_ref, vec_ref, stays_ref, sent_ref):
    made = (mid_ref[...] + (f0_ref[...].astype(F32) + f1_ref[...].astype(F32)) + vec_ref[5:6, :]).astype(BF)

    @pl.when(pl.program_id(0) == 0)
    def _():
        stays_ref[...] = made

    @pl.when(pl.program_id(0) == 1)
    def _():
        sent_ref[...] = made


def swap(size):
    return [(i, size - 1 - i) for i in range(size)]


def to_y(values):
    return lax.ppermute(values, "y", swap(2))


def to_x(values):
    return lax.ppermute(values, "b", swap(2))


def to_core(values):
    return lax.ppermute(values, "c", swap(2))


def gather_z(values):
    got = [lax.ppermute(values, "a", [((i + k) % ZS, i) for i in range(ZS)]) for k in range(1, ZS)]
    return jnp.stack([values] + got)


def spread_z(values):
    return lax.all_to_all(values, "a", 0, 0, tiled=True)


def body(
    fast,
    inputs,
    time_embed,
    first_gain,
    first_shift,
    query_weight,
    query_bias,
    key_weight,
    value_weight,
    value_bias,
    output_weight,
    output_bias,
    second_gain,
    second_shift,
    hidden_weight,
    hidden_bias,
    down_weight,
    down_bias,
    cotangent,
):
    _, block, width = inputs.shape
    shard = query_weight.shape[0]
    rows = width // (ZS * XS)
    seq = 4 * block
    hidden = hidden_weight.shape[1]
    yi = lax.axis_index("y")
    xi = lax.axis_index("b") if fast else jnp.int32(0)
    zi = lax.axis_index("a") if fast else jnp.int32(0)
    x_arr = jnp.stack([xi.astype(jnp.int32), zi.astype(jnp.int32)])

    n_copies = ZS if fast else 1
    attn_pack, mlp_pack = call(
        pack_body,
        (1,),
        [kept((shard, hidden // 4))] * 3
        + [kept((hidden // 4, shard)), kept((shard, hidden)), kept((shard, hidden))]
        + [kept((1, shard))] * 7
        + [kept((1, query_bias.shape[0]))] * 2,
        [
            (sds((shard + KINDS, width), BF), kept((shard + KINDS, width))),
            (sds((n_copies, 2 * shard, width), BF), kept((n_copies, 2 * shard, width))),
        ],
        flops=1e6,
        moved=2e6,
        vmem=56,
    )(
        query_weight, key_weight, value_weight, output_weight, hidden_weight, down_weight.T,
        *(v[None] for v in (first_gain, first_shift, output_bias, second_gain, second_shift, down_bias, hidden_bias, query_bias, value_bias)),
    )

    inputs, cotangent, attn_pack = lax.optimization_barrier((inputs, cotangent, attn_pack))
    both = jnp.concatenate([inputs, cotangent], axis=1)
    stays = lax.dynamic_index_in_dim(both, yi, 0, keepdims=False)
    comes = to_y(lax.dynamic_index_in_dim(both, 1 - yi, 0, keepdims=False))
    stays_mate = to_core(stays)
    te = lax.dynamic_index_in_dim(time_embed, yi, 0, keepdims=True)

    if fast:
        attn_oo = gather_z(attn_pack)
        attn_oo, mlp_pack = lax.optimization_barrier((attn_oo, mlp_pack))
        attn_oo, comes, stays_mate = lax.optimization_barrier((attn_oo, comes, stays_mate))
        comes_mate = to_core(comes)
        attn_ox, attn_yo = to_x(attn_oo), to_y(attn_oo)
        attn_ox, attn_yo = lax.optimization_barrier((attn_ox, attn_yo))
        mlp_oo = spread_z(mlp_pack)
        attn_yx = (to_y(attn_ox[:, : rows // 2]), to_x(attn_yo[:, rows // 2 :]))
    else:
        def natural(values):
            full = lax.all_gather(values, ("a", "b"), axis=0, tiled=True)
            full = full.reshape(ZS, XS, rows, width)
            return full[:, 0], full[:, 1]

        gathered = lax.all_gather(attn_pack, ("a", "b"), axis=0, tiled=False)
        matrix = gathered[:, :shard].reshape(ZS, XS, rows, width)
        small = gathered[:, shard:, :shard]
        flat = small[:, :7].transpose(1, 0, 2).reshape(7, width)
        n = shard // 4
        bias = [small[:, 7, k * n : k * n + n].reshape(ZS * XS, -1) for k in range(2)]
        bias = jnp.concatenate([*bias, jnp.zeros((ZS * XS, rows - 2 * (rows // 4)), BF)], axis=1)
        small = jnp.concatenate([flat, bias.reshape(1, width)], axis=0)
        small = small.reshape(KINDS, ZS, XS, rows).transpose(1, 2, 0, 3)
        small = jnp.pad(small, ((0, 0), (0, 0), (0, 0), (0, width - rows)))
        matrix = jnp.concatenate([matrix, small], axis=2)
        attn_oo, attn_ox = matrix[:, 0], matrix[:, 1]
        attn_yo, attn_yx = to_y(attn_oo), (to_y(attn_ox),)
        comes_mate = to_core(comes)
        h_oo, h_ox = natural(mlp_pack[0, :shard])
        d_oo, d_ox = natural(mlp_pack[0, shard:])
        mlp_oo = jnp.concatenate([h_oo, d_oo], axis=1)
        mlp_ox = jnp.concatenate([h_ox, d_ox], axis=1)

    def by(tile):
        return pl.BlockSpec((tile, width), lambda i: (i, 0))

    def by_mate(tile):
        tiles = seq // tile
        return pl.BlockSpec((tile, width), lambda i: ((i + tiles // 2) % tiles, 0))

    def low_half(tile):
        last = seq // tile // 2 - 1
        return pl.BlockSpec((tile, width), lambda i: (jnp.minimum(i, last), 0))

    def high_half(tile):
        first = seq // tile // 2
        return pl.BlockSpec((tile, width), lambda i: (jnp.maximum(i - first, 0), 0))

    tokens = tuple(far(v) for v in (stays, comes, stays_mate, comes_mate))
    start_blocks = [pl.BlockSpec((block, width), lambda *_: (0, 0), pipeline_mode=pl.Buffered(1))] * 4
    cot_blocks = [pl.BlockSpec((block, width), lambda *_: (1, 0), pipeline_mode=pl.Buffered(1))] * 4
    row = kept((1, width))
    vecs = kept((KINDS, width))
    square = whole((width, width))
    n_qkv = 9 * HD

    def project(first, source, *shards):
        tile = TILE_PROJECT
        outs = [
            (sds((width, width), BF), kept((width, width))),
            (sds((KINDS, width), F32), vecs),
            (pltpu.HBM((9, seq, HD), BF), pl.BlockSpec((9, tile, HD), lambda i: (0, i, 0))),
        ]
        if first:
            outs += [(pltpu.HBM((seq, width), BF), by(tile))]
        else:
            outs += [(pltpu.HBM((width, seq), BF), pl.BlockSpec((width, tile), lambda i: (0, i)))]
        return call(
            functools.partial(project_body, rows=rows, first=first),
            (seq // tile,),
            [scalar()] + (start_blocks + [row] if first else [by(tile)]) + [whole(v.shape) for v in shards],
            outs,
            scratch=[pltpu.VMEM((8, n_qkv), F32)],
            flops=2 * seq * width * n_qkv,
            moved=8e6,
        )(x_arr, *source, *shards)

    q_spec = pl.BlockSpec((1, seq, HD), lambda h: (h, 0, 0))
    k_spec = pl.BlockSpec((1, seq, HD), lambda h: (3 + h, 0, 0))
    v_spec = pl.BlockSpec((1, seq, HD), lambda h: (6 + h, 0, 0))
    e_spec = pl.BlockSpec((1, seq, seq), lambda h: (h, 0, 0))
    inv_spec = pl.BlockSpec((1, 1, seq), lambda h: (h, 0, 0))
    t_spec = pl.BlockSpec((1, HD, seq), lambda h: (h, 0, 0))

    def attend(qkv):
        return call(
            attend_body,
            (3,),
            [q_spec, k_spec, v_spec],
            [
                (pltpu.HBM((3, seq, seq), BF), e_spec),
                (sds((3, 1, seq), F32), inv_spec),
                (sds((3, HD, seq), BF), t_spec),
                (pltpu.HBM((3, HD, seq), F32), t_spec),
            ],
            flops=3 * 16 * seq * seq * HD,
            moved=8e6,
            trans=3 * seq * seq,
        )(*[far(qkv)] * 3)

    def attend_back(qkv, expon, inverse, mixed, grad_mixed, keep):
        made = keep((3, seq, HD), BF)
        return call(
            attend_back_body,
            (3,),
            [q_spec, k_spec, v_spec, e_spec, inv_spec, t_spec, t_spec],
            [(made, q_spec)] * 3,
            flops=3 * 40 * seq * seq * HD,
            moved=9e6,
        )(*[far(qkv)] * 3, far(expon), inverse, far(mixed), grad_mixed)

    w_o, vec, qkv_o, normed = project(True, (*tokens, te), attn_oo, attn_ox)
    qkv_o, attn_yx, mlp_oo = lax.optimization_barrier((qkv_o, attn_yx, mlp_oo))
    mlp_yo = to_y(mlp_oo)
    if fast:
        mlp_ox = to_x(mlp_oo)
    exp_o, inv_o, mixed_o, wide_o = attend(qkv_o)
    normed, exp_o = lax.optimization_barrier((normed, exp_o))
    w_y, vec_y, qkv_y, normed_t = project(False, (far(normed),), attn_yo, *attn_yx)
    exp_y, inv_y, mixed_y, wide_y = attend(qkv_y)

    tile = TILE_OUT
    half_t = pl.BlockSpec((3 * HD, tile), lambda i: (0, i))
    flat_o, flat_y = mixed_o.reshape(3 * HD, seq), mixed_y.reshape(3 * HD, seq)
    (attended,) = call(
        outproj_body,
        (seq // tile,),
        [half_t, half_t, square, square],
        [(sds((seq, width), BF), by(tile))],
        scratch=[pltpu.VMEM((width, 6 * HD), BF)],
        flops=2 * seq * width * 384,
        moved=6e6,
    )(flat_o, flat_y, w_o, w_y)
    attended, mlp_ox, mlp_yo = lax.optimization_barrier((attended, mlp_ox, mlp_yo))
    attended_mate = to_core(attended)
    h_yx = to_y(mlp_ox[:, :rows])
    d_yx = to_x(mlp_yo[:, rows:]) if fast else to_y(mlp_ox[:, rows:])

    tile = TILE_MLP
    part = (ZS, rows, hidden)
    grad_parts = [(sds((1, hidden), F32), kept((1, hidden)))] + [(sds(part, BF), kept(part))] * 4
    mlp_scratch = [pltpu.VMEM((width, hidden), t) for t in (BF, BF, F32, F32)]
    mlp_cost = dict(flops=12 * seq * width * hidden, moved=16e6, trans=seq * hidden * 2, vmem=24)
    middle, normed_second, ff_part, gs_part, hb_o, gh_oo, gh_ox, gd_oo, gd_ox = call(
        functools.partial(mlp_first_body, rows=rows),
        (seq // tile,),
        [scalar(), *start_blocks, row, by(tile), by_mate(tile), *cot_blocks, vecs]
        + [whole((ZS, 2 * rows, hidden))] * 2,
        [
            (sds((seq, width), F32), by(tile)),
            (sds((seq, width), BF), by(tile)),
            (sds((seq, width), F32), by(tile)),
            (sds((seq, width), F32), by(tile)),
        ]
        + grad_parts,
        scratch=mlp_scratch,
        **mlp_cost,
    )(x_arr, *tokens, te, attended, attended_mate, *tokens, vec, mlp_oo, mlp_ox)
    if fast:
        got_ho = to_x(gh_ox)
        normed_second, h_yx, d_yx = lax.optimization_barrier((normed_second, h_yx, d_yx))
    ff, ff_sent, gs, hb_y, gh_yo, gh_yx, gd_yo, gd_yx = call(
        functools.partial(mlp_second_body, rows=rows),
        (seq // tile,),
        [scalar(), by(tile), *cot_blocks, vecs, by(tile), by(tile)]
        + [whole((ZS, 2 * rows, hidden)), whole(part), whole(part)],
        [
            (sds((seq // 2, width), BF), low_half(tile)),
            (sds((seq // 2, width), BF), high_half(tile)),
            (sds((seq, width), BF), by(tile)),
        ]
        + grad_parts,
        scratch=mlp_scratch,
        **mlp_cost,
    )(x_arr, normed_second, *tokens, vec_y, ff_part, gs_part, mlp_yo, h_yx, d_yx)
    if fast:
        gs, got_ho = lax.optimization_barrier((gs, got_ho))
    gs_mate = to_core(gs)
    ff_mate = to_core(ff_sent)

    tile = TILE_SECOND
    half_t = pl.BlockSpec((3 * HD, tile), lambda i: (0, i))
    grad_middle, gx_o, gx_y, wo_o, wo_y, second_sums = call(
        second_back_body,
        (seq // tile,),
        [by(tile), by(tile), by_mate(tile), *cot_blocks, vecs, square, square, half_t, half_t],
        [
            (pltpu.HBM((seq, width), F32), by(tile)),
            (sds((3 * HD, seq), BF), half_t),
            (sds((3 * HD, seq), BF), half_t),
            (pltpu.HBM((width, 3 * HD), BF), kept((width, 3 * HD))),
            (pltpu.HBM((width, 3 * HD), BF), kept((width, 3 * HD))),
            (sds((KINDS, width), F32), vecs),
        ],
        scratch=[pltpu.VMEM((width, 6 * HD), BF), pltpu.VMEM((width, 6 * HD), F32)],
        flops=4 * seq * width * 384,
        moved=16e6,
    )(middle, gs, gs_mate, *tokens, vec, w_o, w_y, flat_o, flat_y)
    if fast:
        got_h, got_d = to_x(gh_yx), to_y(gd_yx)
        gx_y, got_h, got_d = lax.optimization_barrier((gx_y, got_h, got_d))
        got_hs, got_ds = to_y(gh_yo + got_h), to_x(gd_ox + got_d)

    def project_back(grads, weights, wo, prev):
        tile = TILE_BACK
        more = prev is not None
        heads = pl.BlockSpec((3, tile, HD), lambda i: (0, i, 0))
        attn_part = (ZS, rows, width)
        return call(
            functools.partial(project_back_body, rows=rows, more=more),
            (seq // tile,),
            [scalar(), heads, heads, heads, pl.BlockSpec((width, tile), lambda i: (0, i)), square, whole((width, 3 * HD))]
            + ([by(tile)] if more else []),
            [
                (pltpu.HBM(attn_part, BF), kept(attn_part)),
                (pltpu.HBM(attn_part, BF), kept(attn_part)),
                ((sds((seq, width), BF) if more else pltpu.HBM((seq, width), F32)), by(tile)),
                (sds((1, n_qkv), F32), kept((1, n_qkv))),
            ],
            scratch=[pltpu.VMEM((width, n_qkv), F32)],
            flops=4 * seq * width * n_qkv,
            moved=10e6,
        )(x_arr, *(far(v) if more else v for v in grads), far(normed_t), weights, far(wo), *((far(prev),) if more else ()))

    grads_y = attend_back(qkv_y, exp_y, inv_y, wide_y, gx_y.reshape(3, HD, seq), sds)
    ga_yo, ga_yx, first_part, qkv_sum_y = project_back(grads_y, w_y, wo_y, None)
    tile = block
    out_stays, out_tokens = call(
        output_body,
        (2,),
        [by(tile), by(tile), by(tile), vecs],
        [(sds((block, width), BF), kept((block, width)))] * 2,
        flops=1e6,
        moved=5e6,
    )(middle, ff, ff_mate, vec)
    gx_o, first_part, out_tokens = lax.optimization_barrier((gx_o, first_part, out_tokens))
    if fast:
        gx_o, ga_yx, got_hs, got_ds, gd_yo = lax.optimization_barrier((gx_o, ga_yx, got_hs, got_ds, gd_yo))
        got_do = to_y(gd_yo)
        ga_d = to_x(ga_yx)
    grads_o = attend_back(qkv_o, exp_o, inv_o, wide_o, gx_o.reshape(3, HD, seq), pltpu.HBM)
    if fast:
        *grads_o, got_do, ga_d, out_tokens = lax.optimization_barrier((*grads_o, got_do, ga_d, out_tokens))
        out_got = to_y(out_tokens)
        mlp_all = spread_z(jnp.concatenate([gh_oo + got_ho + got_hs, gd_oo + got_do + got_ds], axis=1))
        ga_s = to_y(ga_yo + ga_d)
    ga_oo, ga_ox, first, qkv_sum_o = project_back(grads_o, w_o, wo_o, first_part)
    if fast:
        ga_x = to_x(ga_ox)
        first, out_got = lax.optimization_barrier((first, out_got))
    first_mate = to_core(first)

    tile = TILE_FIRST
    hb_spec, qkv_spec = kept((1, hidden)), kept((1, n_qkv))
    small_o_shape, small_y_shape = (XS, ZS, KINDS, rows), (XS, ZS, 2 * KINDS, rows)
    in_stays, input_grad, small_o, small_y, first_sums = call(
        functools.partial(first_back_body, rows=rows),
        (seq // tile,),
        [scalar(), *start_blocks, row, vecs, by(tile), by_mate(tile), by(tile), vecs, hb_spec, hb_spec, qkv_spec, qkv_spec],
        [(sds((seq // 4, width), BF), kept((seq // 4, width)))] * 2
        + [
            (sds(small_o_shape, F32), kept(small_o_shape)),
            (sds(small_y_shape, F32), kept(small_y_shape)),
            (sds((KINDS, width), F32), vecs),
        ],
        flops=0,
        moved=0,
    )(x_arr, *tokens, te, vec, first, first_mate, far(grad_middle), second_sums, hb_o, hb_y, qkv_sum_o, qkv_sum_y)

    small_got = to_y(small_y)
    if fast:
        small_got, input_grad, ga_x, ga_s, mlp_all = lax.optimization_barrier(
            (small_got, input_grad, ga_x, ga_s, mlp_all)
        )
        ga_all = spread_z(ga_oo + ga_s + ga_x)
    small_sum = small_o + small_got[:, :, :KINDS]
    embed = first_sums[2]
    embed_got = jnp.where(xi == 0, small_got, small_got[::-1])[:, :, KINDS].transpose(1, 0, 2).reshape(width)
    embed_gradient = jnp.where(yi == 0, jnp.stack([embed, embed_got]), jnp.stack([embed_got, embed]))
    n_bias = query_bias.shape[0]
    n_head = query_weight.shape[1]
    if fast:
        small_sum = small_sum[0] + to_x(small_sum[1])
        zi = lax.axis_index("a")
        pieces = [lax.dynamic_index_in_dim(small_sum, (zi + k) % ZS, 0, keepdims=False) for k in range(ZS)]
        pieces = [lax.ppermute(v, "a", [(i, (i + k) % ZS) for i in range(ZS)]) if k else v for k, v in enumerate(pieces)]
        *weights, fg, fs, ob, sg, ss, db, hb, qb, vb = call(
            functools.partial(final_body, rows=rows),
            (1,),
            [kept(ga_all.shape)] + [kept((KINDS, rows))] * ZS,
            [(sds((shard, n_head), F32), kept((shard, n_head)))] * 3
            + [(sds((n_head, shard), F32), kept((n_head, shard)))]
            + [(sds((1, shard), F32), kept((1, shard)))] * 7
            + [(sds((1, n_bias), F32), kept((1, n_bias)))] * 2,
            flops=1e6,
            moved=2e6,
        )(ga_all, *pieces)
        vectors = [v[0] for v in (fg, fs, ob, sg, ss, db, hb, qb, vb)]
        mlp_sum = jnp.sum(mlp_all.astype(F32), axis=0)
        gh, gd = mlp_sum[:shard], mlp_sum[shard:].T
    else:

        def scatter(values):
            return lax.psum_scatter(values, ("a", "b"), scatter_dimension=0, tiled=True)

        def scatter_slow(oo, ox, yo, yx):
            own, oth = oo + to_y(yo), ox + to_y(yx)
            return scatter(jnp.stack([own, oth], axis=1).reshape(width, -1).astype(F32))

        kinds = small_sum.transpose(2, 1, 0, 3)
        bias = kinds[7].reshape(ZS * XS, rows)
        split = rows // 4
        vectors = [scatter(v) for v in kinds[:7].reshape(7, width)]
        vectors += [scatter(bias[:, k * split : k * split + split].reshape(-1)) for k in range(2)]
        gh = scatter_slow(gh_oo, gh_ox, gh_yo, gh_yx)
        gd = scatter_slow(gd_oo, gd_ox, gd_yo, gd_yx).T
        ga = scatter_slow(ga_oo, ga_ox, ga_yo, ga_yx)
        weights = [ga[:, k * n_head : k * n_head + n_head] for k in range(4)]
        weights[3] = weights[3].T

    def placed(stays, got):
        return jnp.where(yi == 0, jnp.stack([stays, got]), jnp.stack([got, stays]))

    if not fast:
        out_got = to_y(out_tokens)
    block_output = placed(out_stays, out_got)
    input_gradient = placed(in_stays, to_y(input_grad))

    fg, fs, ob, sg, ss, db, hb, qb, vb = vectors
    return (
        block_output, input_gradient, embed_gradient, fg, fs, weights[0], qb, weights[1], weights[2], vb,
        weights[3], ob, sg, ss, gh, hb, gd, db,
    )


def solution(mesh):
    dp, tensor = mesh.shape["dp"], mesh.shape["tensor"]
    fine = Mesh(mesh.devices.reshape(dp // 2, 2, tensor // 2, 2), ("a", "b", "y", "c"))
    by_dp, by_tensor = ("a", "b"), ("y", "c")
    both = by_tensor + by_dp
    column, matrix, turned = P(by_dp), P(by_dp, by_tensor), P(by_tensor, by_dp)
    seqs = P(by_dp, by_tensor, None)
    return jax.shard_map(
        functools.partial(body, dp == ZS * XS),
        mesh=fine,
        in_specs=(
            seqs, P(by_dp, None), column, column, matrix, P(both), matrix, matrix, P(both), turned,
            column, column, column, matrix, P(both), turned, column, seqs,
        ),
        out_specs=(
            seqs, seqs, P(by_dp, None), column, column, matrix, P(both), matrix, matrix, P(both), turned,
            column, column, column, matrix, P(both), turned, column,
        ),
        check_vma=False,
    )
```

```python
import functools

import jax
import jax.numpy as jnp
from jax import lax
from jax.experimental import pallas as pl
from jax.experimental.pallas import tpu as pltpu
from jax.sharding import Mesh
from jax.sharding import PartitionSpec as P

HD = 64
EPSILON = 1e-05
SCALE = 0.125
BF = jnp.bfloat16
F32 = jnp.float32
ZS, XS = 4, 2
KINDS = 8
HINT = 2.0
TILE_PROJECT = 512
TILE_OUT = 512
TILE_MLP = 512
TILE_SECOND = 512
TILE_BACK = 1024
TILE_FIRST = 512

NN = (((1,), (0,)), ((), ()))
NT = (((1,), (1,)), ((), ()))


def dot(left, right, dims=NN):
    return lax.dot_general(left, right, dims, preferred_element_type=F32)


def call(body, grid, ins, outs, scratch=(), flops=0, moved=0, trans=0, vmem=16):
    return pl.pallas_call(
        body,
        grid=grid,
        in_specs=[s for s in ins],
        out_specs=[s for _, s in outs],
        out_shape=[o for o, _ in outs],
        scratch_shapes=list(scratch),
        compiler_params=pltpu.CompilerParams(vmem_limit_bytes=vmem << 20),
        cost_estimate=pl.CostEstimate(flops=int(flops * HINT), bytes_accessed=int(moved * HINT), transcendentals=int(trans * HINT)),
    )


def whole(shape, n=1):
    zeros = (0,) * len(shape)
    return pl.BlockSpec(shape, lambda *_: zeros, pipeline_mode=pl.Buffered(1))


def kept(shape):
    zeros = (0,) * len(shape)
    return pl.BlockSpec(shape, lambda *_: zeros)


def far(values):
    return pltpu.with_memory_space_constraint(values, pltpu.HBM)


def scalar():
    return pl.BlockSpec(memory_space=pltpu.SMEM)


def sds(shape, dtype):
    return jax.ShapeDtypeStruct(shape, dtype)


def place(x_ref, k, side, rows):
    x = x_ref[0] if side == 0 else 1 - x_ref[0]
    return pl.multiple_of((2 * lax.rem(x_ref[1] + k, ZS) + x) * rows, 32)


def shard_of(refs, z, rows):
    parts = [r[z] for r in refs]
    value = parts[0] if len(parts) == 1 else jnp.concatenate(parts, axis=0)
    return value[:rows], value[rows:]


def normalize(values):
    center = values - jnp.mean(values, axis=-1, keepdims=True)
    spread = jnp.mean(center * center, axis=-1, keepdims=True)
    rate = lax.rsqrt(spread + EPSILON)
    return center * rate, rate


def pack_body(q_ref, k_ref, v_ref, o_ref, h_ref, d_ref, fg, fs, ob, sg, ss, db, hb, qb, vb, attn_ref, mlp_ref):
    shard = q_ref.shape[0]
    low = jnp.concatenate([q_ref[...], k_ref[...], v_ref[...], o_ref[...].T], axis=1)
    n = qb.shape[1]
    bias = jnp.concatenate([qb[...], vb[...], jnp.zeros((1, shard - 2 * n), BF)], axis=1)
    small = jnp.concatenate([r[...].astype(F32) for r in (fg, fs, ob, sg, ss, db, hb)] + [bias.astype(F32)], axis=0)
    small = jnp.concatenate([small, jnp.zeros((KINDS, low.shape[1] - shard), F32)], axis=1).astype(BF)
    high, down = h_ref[...], d_ref[...]
    attn_ref[:shard, :] = low
    attn_ref[shard:, :] = small
    for z in range(mlp_ref.shape[0]):
        mlp_ref[z, :shard, :] = high
        mlp_ref[z, shard:, :] = down


def pick(refs):
    step, each = pl.program_id(0), len(refs) // pl.num_programs(0)
    blocks = [r[...] for r in refs]
    tiles = [blocks[k : k + each] for k in range(0, len(blocks), each)]
    tiles = [t[0] if each == 1 else jnp.concatenate(t, axis=0) for t in tiles]
    value = tiles[0]
    for k in range(1, len(tiles)):
        value = jnp.where(step == k, tiles[k], value)
    return value


def project_body(x_ref, *refs, rows, first):
    refs = list(refs)
    if first:
        *tokens, te_ref, own_ref, oth_ref, w_ref, vec_ref, qkv_ref, normed_ref, bias_ref = refs
        oth_refs = (oth_ref,)
    else:
        source_ref, own_ref, *oth_refs, w_ref, vec_ref, qkv_ref, normed_t_ref, bias_ref = refs

    @pl.when(pl.program_id(0) == 0)
    def _():
        own, oth = [], []
        for k in range(ZS):
            weight, small = shard_of((own_ref,), k, rows)
            w_ref[pl.ds(place(x_ref, k, 0, rows), rows), :] = weight
            own.append(small[:, :rows].astype(F32))
            weight, small = shard_of(oth_refs, k, rows)
            w_ref[pl.ds(place(x_ref, k, 1, rows), rows), :] = weight
            oth.append(small[:, :rows].astype(F32))
        even = jnp.concatenate([v for pair in zip(own, oth) for v in pair], axis=1)
        odd = jnp.concatenate([v for pair in zip(oth, own) for v in pair], axis=1)
        vec = jnp.where(x_ref[0] == 0, even, odd)
        vec = pltpu.roll(vec, x_ref[1] * (2 * rows), 1)
        vec_ref[...] = vec
        n = rows // 4
        last = vec[7:8, :]
        parts = [last[:, rows * k : rows * k + n] for k in range(ZS * XS)]
        parts += [jnp.zeros((1, 3 * HD), F32)]
        parts += [last[:, rows * k + n : rows * k + 2 * n] for k in range(ZS * XS)]
        bias_ref[0:1, :] = jnp.concatenate(parts, axis=1)

    if first:
        xhat, _ = normalize(pick(tokens).astype(F32) + te_ref[...].astype(F32))
        normed = (xhat * vec_ref[0:1, :] + vec_ref[1:2, :]).astype(BF)
        normed_ref[...] = normed
    else:
        normed = source_ref[...]
        normed_t_ref[...] = normed.T
    made = dot(normed, w_ref[:, :640])[:, :576] + bias_ref[0:1, :]
    made = made.astype(BF)
    for j in range(9):
        piece = made[:, 64 * j : 64 * j + 64]
        qkv_ref[j] = piece * BF(SCALE) if j < 3 else piece


def attend_body(q_ref, k_ref, v_ref, e_ref, inv_ref, mixed_ref, wide_ref):
    scores = dot(k_ref[0], q_ref[0], NT)
    expon = jnp.exp(scores - jnp.max(scores, axis=0, keepdims=True))
    inverse = 1.0 / jnp.sum(expon, axis=0, keepdims=True)
    low = expon.astype(BF)
    e_ref[0] = low
    inv_ref[0] = inverse
    wide = dot(v_ref[0].T, low) * inverse
    mixed_ref[0] = wide.astype(BF)
    wide_ref[0] = wide


def attend_back_body(q_ref, k_ref, v_ref, e_ref, inv_ref, mixed_ref, gm_ref, dq_ref, dk_ref, dv_ref):
    low = (gm_ref[0].astype(F32) * inv_ref[0]).astype(BF)
    inner = jnp.sum(low.astype(F32) * mixed_ref[0], axis=0, keepdims=True)
    expon = e_ref[0]
    grad_scores = (expon.astype(F32) * (dot(v_ref[0], low) - inner)).astype(BF)
    dv_ref[0] = dot(expon, low, NT).astype(BF)
    dk_ref[0] = dot(grad_scores, q_ref[0]).astype(BF)
    dq_ref[0] = (dot(k_ref[0].T, grad_scores) * SCALE).T.astype(BF)


def outproj_body(m0_ref, m1_ref, w0_ref, w1_ref, out_ref, wo_ref):
    @pl.when(pl.program_id(0) == 0)
    def _():
        wo_ref[...] = jnp.concatenate([w0_ref[:, 576:], w1_ref[:, 576:]], axis=1)

    mixed = jnp.concatenate([m0_ref[...], m1_ref[...]], axis=0).T
    out_ref[...] = dot(mixed, wo_ref[...], NT).astype(BF)


def feed(normed, cot, wh, wd, bias, acc_h, acc_d, hbg_ref):
    pre = dot(normed, wh[...]) + bias
    below = 0.5 + 0.5 * lax.erf(pre * 0.7071067811865476)
    act = (pre * below).astype(BF)
    slope = below + pre * (jnp.exp(-0.5 * pre * pre) * 0.3989422804014327)
    grad = (dot(cot, wd[...]) * slope).astype(BF)
    acc_h[...] += dot(normed.T, grad)
    acc_d[...] += dot(cot.T, act)
    hbg_ref[...] += jnp.sum(grad.astype(F32), axis=0, keepdims=True)
    return dot(act, wd[...], NT), dot(grad, wh[...], NT)


def fill(x, rows, own, oth, wh, wd, acc_h, acc_d, hbg_ref):
    for z in range(ZS):
        for refs, side in ((own, x), (oth, 1 - x)):
            at = pl.multiple_of((2 * z + side) * rows, 32)
            wh[pl.ds(at, rows), :], wd[pl.ds(at, rows), :] = shard_of(refs, z, rows)
    for ref in (acc_h, acc_d, hbg_ref):
        ref[...] = jnp.zeros_like(ref)


def drain(x, rows, acc, own, oth):
    for z in range(ZS):
        own[z] = acc[pl.ds(pl.multiple_of((2 * z + x) * rows, 32), rows), :].astype(BF)
        oth[z] = acc[pl.ds(pl.multiple_of((2 * z + 1 - x) * rows, 32), rows), :].astype(BF)


def mlp_first_body(
    x_ref, s0, s1, s2, s3, te_ref, a0_ref, a1_ref, c0, c1, c2, c3, vec_ref, w_oo, w_ox,
    mid_ref, normed_ref, ff_ref, gs_ref, hbg_ref, gh_o, gh_x, gd_o, gd_x,
    wh, wd, acc_h, acc_d, *, rows,
):
    x = x_ref[0]

    @pl.when(pl.program_id(0) == 0)
    def _():
        fill(x, rows, (w_oo,), (w_ox,), wh, wd, acc_h, acc_d, hbg_ref)

    middle = (
        pick((s0, s1, s2, s3)).astype(F32)
        + te_ref[...].astype(F32)
        + (a0_ref[...].astype(F32) + a1_ref[...].astype(F32))
        + vec_ref[2:3, :]
    )
    mid_ref[...] = middle
    xhat, _ = normalize(middle)
    normed = (xhat * vec_ref[3:4, :] + vec_ref[4:5, :]).astype(BF)
    normed_ref[...] = normed
    ff_ref[...], gs_ref[...] = feed(normed, pick((c0, c1, c2, c3)), wh, wd, vec_ref[6:7, :], acc_h, acc_d, hbg_ref)

    @pl.when(pl.program_id(0) == pl.num_programs(0) - 1)
    def _():
        drain(x, rows, acc_h, gh_o, gh_x)
        drain(x, rows, acc_d, gd_o, gd_x)


def mlp_second_body(
    x_ref, normed_ref, c0, c1, c2, c3, vec_ref, f_ref, g_ref, w_yo, h_yx, d_yx,
    ff0_ref, ff1_ref, gs_ref, hbg_ref, gh_o, gh_x, gd_o, gd_x,
    wh, wd, acc_h, acc_d, *, rows,
):
    x = x_ref[0]

    @pl.when(pl.program_id(0) == 0)
    def _():
        fill(x, rows, (w_yo,), (h_yx, d_yx), wh, wd, acc_h, acc_d, hbg_ref)

    ff, gs = feed(normed_ref[...], pick((c0, c1, c2, c3)), wh, wd, vec_ref[6:7, :], acc_h, acc_d, hbg_ref)
    gs_ref[...] = (g_ref[...] + gs).astype(BF)
    ff = (f_ref[...] + ff).astype(BF)
    half = pl.num_programs(0) // 2

    @pl.when(pl.program_id(0) < half)
    def _():
        ff0_ref[...] = ff

    @pl.when(pl.program_id(0) >= half)
    def _():
        ff1_ref[...] = ff

    @pl.when(pl.program_id(0) == pl.num_programs(0) - 1)
    def _():
        drain(x, rows, acc_h, gh_o, gh_x)
        drain(x, rows, acc_d, gd_o, gd_x)


def second_back_body(mid_ref, g0_ref, g1_ref, c0, c1, c2, c3, vec_ref, w0_ref, w1_ref, m0_ref, m1_ref, gm_ref, x0_ref, x1_ref, wo0_ref, wo1_ref, sum_ref, wo_ref, acc):
    step, last = pl.program_id(0), pl.num_programs(0) - 1

    @pl.when(step == 0)
    def _():
        wo_ref[...] = jnp.concatenate([w0_ref[:, 576:], w1_ref[:, 576:]], axis=1)
        acc[...] = jnp.zeros_like(acc)
        sum_ref[...] = jnp.zeros_like(sum_ref)

    xhat, rate = normalize(mid_ref[...])
    second = g0_ref[...].astype(F32) + g1_ref[...].astype(F32)
    cot = pick((c0, c1, c2, c3)).astype(F32)
    scaled = second * vec_ref[3:4, :]
    inner = jnp.mean(scaled * xhat, axis=-1, keepdims=True)
    grad = cot + rate * (scaled - jnp.mean(scaled, axis=-1, keepdims=True) - xhat * inner)
    gm_ref[...] = grad
    sum_ref[0:1, :] += jnp.sum(second * xhat, axis=0, keepdims=True)
    sum_ref[1:2, :] += jnp.sum(second, axis=0, keepdims=True)
    sum_ref[2:3, :] += jnp.sum(grad, axis=0, keepdims=True)
    sum_ref[3:4, :] += jnp.sum(cot, axis=0, keepdims=True)
    low = grad.astype(BF)
    back = dot(low, wo_ref[...]).astype(BF).T
    x0_ref[...] = back[:192]
    x1_ref[...] = back[192:]
    mixed = jnp.concatenate([m0_ref[...], m1_ref[...]], axis=0)
    acc[...] += dot(low.T, mixed, NT)

    @pl.when(step == last)
    def _():
        wo0_ref[...] = acc[:, :192].astype(BF)
        wo1_ref[...] = acc[:, 192:].astype(BF)


def project_back_body(x_ref, q_ref, k_ref, v_ref, nt_ref, w_ref, wo_ref, *refs, rows, more):
    refs = list(refs)
    prev_ref = refs.pop(0) if more else None
    own_ref, oth_ref, first_ref, sum_ref, acc = refs
    step, last = pl.program_id(0), pl.num_programs(0) - 1
    x = x_ref[0]
    grads = jnp.concatenate([r[h] for r in (q_ref, k_ref, v_ref) for h in range(3)], axis=1)
    made = dot(nt_ref[...], grads)
    total = jnp.sum(grads.astype(F32), axis=0, keepdims=True)

    @pl.when(step == 0)
    def _():
        acc[...] = made
        sum_ref[...] = total

    @pl.when(step > 0)
    def _():
        acc[...] += made
        sum_ref[...] += total

    back = dot(grads, w_ref[:, :576], NT)
    if more:
        back = back + prev_ref[...]
    first_ref[...] = back.astype(first_ref.dtype)

    @pl.when(step == last)
    def _():
        for z in range(ZS):
            for ref, side in ((own_ref, x), (oth_ref, 1 - x)):
                at = pl.multiple_of((2 * z + side) * rows, 32)
                ref[z] = jnp.concatenate(
                    [acc[pl.ds(at, rows), :].astype(BF), wo_ref[pl.ds(at, rows), :]], axis=1
                )


def first_back_body(
    x_ref, s0, s1, s2, s3, te_ref, vec_ref, g0_ref, g1_ref, gm_ref, second_ref, ho_ref, hy_ref, qo_ref, qy_ref,
    stays_ref, sent_ref, own_ref, oth_ref, sum_ref, *, rows,
):
    @pl.when(pl.program_id(0) == 0)
    def _():
        sum_ref[...] = jnp.zeros_like(sum_ref)

    xhat, rate = normalize(pick((s0, s1, s2, s3)).astype(F32) + te_ref[...].astype(F32))
    first = g0_ref[...].astype(F32) + g1_ref[...].astype(F32)
    scaled = first * vec_ref[0:1, :]
    inner = jnp.mean(scaled * xhat, axis=-1, keepdims=True)
    grad = gm_ref[...] + rate * (scaled - jnp.mean(scaled, axis=-1, keepdims=True) - xhat * inner)

    @pl.when(pl.program_id(0) == 0)
    def _():
        half = grad.shape[0] // 2
        stays_ref[...] = grad[:half].astype(BF)
        sent_ref[...] = grad[half:].astype(BF)

    sum_ref[0:1, :] += jnp.sum(first * xhat, axis=0, keepdims=True)
    sum_ref[1:2, :] += jnp.sum(first, axis=0, keepdims=True)
    sum_ref[2:3, :] += jnp.sum(grad, axis=0, keepdims=True)

    @pl.when(pl.program_id(0) == pl.num_programs(0) - 1)
    def _():
        n = rows // 4
        sums = sum_ref[0:3, :]
        shared = [sums[0:2], second_ref[2:3, :], second_ref[0:2, :], second_ref[3:4, :]]
        blank = jnp.zeros((1, rows - 2 * n), F32)
        for hidden, bias, ref, more in ((ho_ref, qo_ref, own_ref, []), (hy_ref, qy_ref, oth_ref, [sums[2:3]])):
            made = []
            kinds = jnp.concatenate(shared + [hidden[...]], axis=0)
            extra = jnp.concatenate(more + [jnp.zeros((KINDS - 1, kinds.shape[1]), F32)], axis=0) if more else None
            for k in range(ZS * XS):
                part = slice(k * rows, k * rows + rows)
                last = [bias[0:1, k * n : k * n + n], bias[0:1, 6 * HD + k * n : 6 * HD + k * n + n], blank]
                piece = [kinds[:, part], jnp.concatenate(last, axis=1)]
                made.append(jnp.concatenate(piece + ([extra[:, part]] if more else []), axis=0))
            for z in range(ZS):
                even, odd = made[2 * z], made[2 * z + 1]
                ref[0, z] = jnp.where(x_ref[0] == 0, even, odd)
                ref[1, z] = jnp.where(x_ref[0] == 0, odd, even)


def final_body(got_ref, p0_ref, p1_ref, p2_ref, p3_ref, q_ref, k_ref, v_ref, o_ref, *small, rows):
    total = got_ref[0].astype(F32)
    for z in range(1, got_ref.shape[0]):
        total = total + got_ref[z].astype(F32)
    width = 3 * HD
    q_ref[...] = total[:, :width]
    k_ref[...] = total[:, width : 2 * width]
    v_ref[...] = total[:, 2 * width : 3 * width]
    o_ref[...] = total[:, 3 * width :].T
    sums = (p0_ref[...] + p1_ref[...]) + (p2_ref[...] + p3_ref[...])
    n = rows // 4
    for k, ref in enumerate(small[:7]):
        ref[...] = sums[k : k + 1]
    small[7][...] = sums[7:8, :n]
    small[8][...] = sums[7:8, n : 2 * n]


def output_body(mid_ref, f0_ref, f1_ref, vec_ref, stays_ref, sent_ref):
    made = (mid_ref[...] + (f0_ref[...].astype(F32) + f1_ref[...].astype(F32)) + vec_ref[5:6, :]).astype(BF)

    @pl.when(pl.program_id(0) == 0)
    def _():
        stays_ref[...] = made

    @pl.when(pl.program_id(0) == 1)
    def _():
        sent_ref[...] = made


def swap(size):
    return [(i, size - 1 - i) for i in range(size)]


def to_y(values):
    return lax.ppermute(values, "y", swap(2))


def to_x(values):
    return lax.ppermute(values, "b", swap(2))


def to_core(values):
    return lax.ppermute(values, "c", swap(2))


def gather_z(values):
    got = [lax.ppermute(values, "a", [((i + k) % ZS, i) for i in range(ZS)]) for k in range(1, ZS)]
    return jnp.stack([values] + got)


def spread_z(values):
    return lax.all_to_all(values, "a", 0, 0, tiled=True)


def body(
    fast,
    inputs,
    time_embed,
    first_gain,
    first_shift,
    query_weight,
    query_bias,
    key_weight,
    value_weight,
    value_bias,
    output_weight,
    output_bias,
    second_gain,
    second_shift,
    hidden_weight,
    hidden_bias,
    down_weight,
    down_bias,
    cotangent,
):
    _, block, width = inputs.shape
    shard = query_weight.shape[0]
    rows = width // (ZS * XS)
    seq = 4 * block
    hidden = hidden_weight.shape[1]
    yi = lax.axis_index("y")
    xi = lax.axis_index("b") if fast else jnp.int32(0)
    zi = lax.axis_index("a") if fast else jnp.int32(0)
    x_arr = jnp.stack([xi.astype(jnp.int32), zi.astype(jnp.int32)])

    n_copies = ZS if fast else 1
    attn_pack, mlp_pack = call(
        pack_body,
        (1,),
        [kept((shard, hidden // 4))] * 3
        + [kept((hidden // 4, shard)), kept((shard, hidden)), kept((shard, hidden))]
        + [kept((1, shard))] * 7
        + [kept((1, query_bias.shape[0]))] * 2,
        [
            (sds((shard + KINDS, width), BF), kept((shard + KINDS, width))),
            (sds((n_copies, 2 * shard, width), BF), kept((n_copies, 2 * shard, width))),
        ],
        flops=1e6,
        moved=2e6,
        vmem=56,
    )(
        query_weight, key_weight, value_weight, output_weight, hidden_weight, down_weight.T,
        *(v[None] for v in (first_gain, first_shift, output_bias, second_gain, second_shift, down_bias, hidden_bias, query_bias, value_bias)),
    )

    inputs, cotangent, attn_pack = lax.optimization_barrier((inputs, cotangent, attn_pack))
    both = jnp.concatenate([inputs, cotangent], axis=1)
    stays = lax.dynamic_index_in_dim(both, yi, 0, keepdims=False)
    comes = to_y(lax.dynamic_index_in_dim(both, 1 - yi, 0, keepdims=False))
    stays_mate = to_core(stays)
    te = lax.dynamic_index_in_dim(time_embed, yi, 0, keepdims=True)

    if fast:
        attn_oo = gather_z(attn_pack)
        attn_oo, mlp_pack = lax.optimization_barrier((attn_oo, mlp_pack))
        attn_oo, comes, stays_mate = lax.optimization_barrier((attn_oo, comes, stays_mate))
        comes_mate = to_core(comes)
        attn_ox, attn_yo = to_x(attn_oo), to_y(attn_oo)
        attn_ox, attn_yo = lax.optimization_barrier((attn_ox, attn_yo))
        mlp_oo = spread_z(mlp_pack)
        attn_yx = (to_y(attn_ox[:, : rows // 2]), to_x(attn_yo[:, rows // 2 :]))
    else:
        def natural(values):
            full = lax.all_gather(values, ("a", "b"), axis=0, tiled=True)
            full = full.reshape(ZS, XS, rows, width)
            return full[:, 0], full[:, 1]

        gathered = lax.all_gather(attn_pack, ("a", "b"), axis=0, tiled=False)
        matrix = gathered[:, :shard].reshape(ZS, XS, rows, width)
        small = gathered[:, shard:, :shard]
        flat = small[:, :7].transpose(1, 0, 2).reshape(7, width)
        n = shard // 4
        bias = [small[:, 7, k * n : k * n + n].reshape(ZS * XS, -1) for k in range(2)]
        bias = jnp.concatenate([*bias, jnp.zeros((ZS * XS, rows - 2 * (rows // 4)), BF)], axis=1)
        small = jnp.concatenate([flat, bias.reshape(1, width)], axis=0)
        small = small.reshape(KINDS, ZS, XS, rows).transpose(1, 2, 0, 3)
        small = jnp.pad(small, ((0, 0), (0, 0), (0, 0), (0, width - rows)))
        matrix = jnp.concatenate([matrix, small], axis=2)
        attn_oo, attn_ox = matrix[:, 0], matrix[:, 1]
        attn_yo, attn_yx = to_y(attn_oo), (to_y(attn_ox),)
        comes_mate = to_core(comes)
        h_oo, h_ox = natural(mlp_pack[0, :shard])
        d_oo, d_ox = natural(mlp_pack[0, shard:])
        mlp_oo = jnp.concatenate([h_oo, d_oo], axis=1)
        mlp_ox = jnp.concatenate([h_ox, d_ox], axis=1)

    def by(tile):
        return pl.BlockSpec((tile, width), lambda i: (i, 0))

    def by_mate(tile):
        tiles = seq // tile
        return pl.BlockSpec((tile, width), lambda i: ((i + tiles // 2) % tiles, 0))

    def low_half(tile):
        last = seq // tile // 2 - 1
        return pl.BlockSpec((tile, width), lambda i: (jnp.minimum(i, last), 0))

    def high_half(tile):
        first = seq // tile // 2
        return pl.BlockSpec((tile, width), lambda i: (jnp.maximum(i - first, 0), 0))

    tokens = tuple(far(v) for v in (stays, comes, stays_mate, comes_mate))
    start_blocks = [pl.BlockSpec((block, width), lambda *_: (0, 0), pipeline_mode=pl.Buffered(1))] * 4
    cot_blocks = [pl.BlockSpec((block, width), lambda *_: (1, 0), pipeline_mode=pl.Buffered(1))] * 4
    row = kept((1, width))
    vecs = kept((KINDS, width))
    square = whole((width, width))
    n_qkv = 9 * HD

    def project(first, source, *shards):
        tile = TILE_PROJECT
        outs = [
            (sds((width, width), BF), kept((width, width))),
            (sds((KINDS, width), F32), vecs),
            (pltpu.HBM((9, seq, HD), BF), pl.BlockSpec((9, tile, HD), lambda i: (0, i, 0))),
        ]
        if first:
            outs += [(pltpu.HBM((seq, width), BF), by(tile))]
        else:
            outs += [(pltpu.HBM((width, seq), BF), pl.BlockSpec((width, tile), lambda i: (0, i)))]
        return call(
            functools.partial(project_body, rows=rows, first=first),
            (seq // tile,),
            [scalar()] + (start_blocks + [row] if first else [by(tile)]) + [whole(v.shape) for v in shards],
            outs,
            scratch=[pltpu.VMEM((8, n_qkv), F32)],
            flops=2 * seq * width * n_qkv,
            moved=8e6,
        )(x_arr, *source, *shards)

    q_spec = pl.BlockSpec((1, seq, HD), lambda h: (h, 0, 0))
    k_spec = pl.BlockSpec((1, seq, HD), lambda h: (3 + h, 0, 0))
    v_spec = pl.BlockSpec((1, seq, HD), lambda h: (6 + h, 0, 0))
    e_spec = pl.BlockSpec((1, seq, seq), lambda h: (h, 0, 0))
    inv_spec = pl.BlockSpec((1, 1, seq), lambda h: (h, 0, 0))
    t_spec = pl.BlockSpec((1, HD, seq), lambda h: (h, 0, 0))

    def attend(qkv):
        return call(
            attend_body,
            (3,),
            [q_spec, k_spec, v_spec],
            [
                (pltpu.HBM((3, seq, seq), BF), e_spec),
                (sds((3, 1, seq), F32), inv_spec),
                (sds((3, HD, seq), BF), t_spec),
                (pltpu.HBM((3, HD, seq), F32), t_spec),
            ],
            flops=3 * 16 * seq * seq * HD,
            moved=8e6,
            trans=3 * seq * seq,
        )(*[far(qkv)] * 3)

    def attend_back(qkv, expon, inverse, mixed, grad_mixed, keep):
        made = keep((3, seq, HD), BF)
        return call(
            attend_back_body,
            (3,),
            [q_spec, k_spec, v_spec, e_spec, inv_spec, t_spec, t_spec],
            [(made, q_spec)] * 3,
            flops=3 * 40 * seq * seq * HD,
            moved=9e6,
        )(*[far(qkv)] * 3, far(expon), inverse, far(mixed), grad_mixed)

    w_o, vec, qkv_o, normed = project(True, (*tokens, te), attn_oo, attn_ox)
    qkv_o, attn_yx, mlp_oo = lax.optimization_barrier((qkv_o, attn_yx, mlp_oo))
    mlp_yo = to_y(mlp_oo)
    if fast:
        mlp_ox = to_x(mlp_oo)
    exp_o, inv_o, mixed_o, wide_o = attend(qkv_o)
    normed, exp_o = lax.optimization_barrier((normed, exp_o))
    w_y, vec_y, qkv_y, normed_t = project(False, (far(normed),), attn_yo, *attn_yx)
    exp_y, inv_y, mixed_y, wide_y = attend(qkv_y)

    tile = TILE_OUT
    half_t = pl.BlockSpec((3 * HD, tile), lambda i: (0, i))
    flat_o, flat_y = mixed_o.reshape(3 * HD, seq), mixed_y.reshape(3 * HD, seq)
    (attended,) = call(
        outproj_body,
        (seq // tile,),
        [half_t, half_t, square, square],
        [(sds((seq, width), BF), by(tile))],
        scratch=[pltpu.VMEM((width, 6 * HD), BF)],
        flops=2 * seq * width * 384,
        moved=6e6,
    )(flat_o, flat_y, w_o, w_y)
    attended, mlp_ox, mlp_yo = lax.optimization_barrier((attended, mlp_ox, mlp_yo))
    attended_mate = to_core(attended)
    h_yx = to_y(mlp_ox[:, :rows])
    d_yx = to_x(mlp_yo[:, rows:]) if fast else to_y(mlp_ox[:, rows:])

    tile = TILE_MLP
    part = (ZS, rows, hidden)
    grad_parts = [(sds((1, hidden), F32), kept((1, hidden)))] + [(sds(part, BF), kept(part))] * 4
    mlp_scratch = [pltpu.VMEM((width, hidden), t) for t in (BF, BF, F32, F32)]
    mlp_cost = dict(flops=12 * seq * width * hidden, moved=16e6, trans=seq * hidden * 2, vmem=24)
    middle, normed_second, ff_part, gs_part, hb_o, gh_oo, gh_ox, gd_oo, gd_ox = call(
        functools.partial(mlp_first_body, rows=rows),
        (seq // tile,),
        [scalar(), *start_blocks, row, by(tile), by_mate(tile), *cot_blocks, vecs]
        + [whole((ZS, 2 * rows, hidden))] * 2,
        [
            (sds((seq, width), F32), by(tile)),
            (sds((seq, width), BF), by(tile)),
            (sds((seq, width), F32), by(tile)),
            (sds((seq, width), F32), by(tile)),
        ]
        + grad_parts,
        scratch=mlp_scratch,
        **mlp_cost,
    )(x_arr, *tokens, te, attended, attended_mate, *tokens, vec, mlp_oo, mlp_ox)
    if fast:
        got_ho = to_x(gh_ox)
        normed_second, h_yx, d_yx = lax.optimization_barrier((normed_second, h_yx, d_yx))
    ff, ff_sent, gs, hb_y, gh_yo, gh_yx, gd_yo, gd_yx = call(
        functools.partial(mlp_second_body, rows=rows),
        (seq // tile,),
        [scalar(), by(tile), *cot_blocks, vecs, by(tile), by(tile)]
        + [whole((ZS, 2 * rows, hidden)), whole(part), whole(part)],
        [
            (sds((seq // 2, width), BF), low_half(tile)),
            (sds((seq // 2, width), BF), high_half(tile)),
            (sds((seq, width), BF), by(tile)),
        ]
        + grad_parts,
        scratch=mlp_scratch,
        **mlp_cost,
    )(x_arr, normed_second, *tokens, vec_y, ff_part, gs_part, mlp_yo, h_yx, d_yx)
    if fast:
        gs, got_ho = lax.optimization_barrier((gs, got_ho))
    gs_mate = to_core(gs)
    ff_mate = to_core(ff_sent)

    tile = TILE_SECOND
    half_t = pl.BlockSpec((3 * HD, tile), lambda i: (0, i))
    grad_middle, gx_o, gx_y, wo_o, wo_y, second_sums = call(
        second_back_body,
        (seq // tile,),
        [by(tile), by(tile), by_mate(tile), *cot_blocks, vecs, square, square, half_t, half_t],
        [
            (pltpu.HBM((seq, width), F32), by(tile)),
            (sds((3 * HD, seq), BF), half_t),
            (sds((3 * HD, seq), BF), half_t),
            (pltpu.HBM((width, 3 * HD), BF), kept((width, 3 * HD))),
            (pltpu.HBM((width, 3 * HD), BF), kept((width, 3 * HD))),
            (sds((KINDS, width), F32), vecs),
        ],
        scratch=[pltpu.VMEM((width, 6 * HD), BF), pltpu.VMEM((width, 6 * HD), F32)],
        flops=4 * seq * width * 384,
        moved=16e6,
    )(middle, gs, gs_mate, *tokens, vec, w_o, w_y, flat_o, flat_y)
    if fast:
        got_h, got_d = to_x(gh_yx), to_y(gd_yx)
        gx_y, got_h, got_d = lax.optimization_barrier((gx_y, got_h, got_d))
        got_hs, got_ds = to_y(gh_yo + got_h), to_x(gd_ox + got_d)

    def project_back(grads, weights, wo, prev):
        tile = TILE_BACK
        more = prev is not None
        heads = pl.BlockSpec((3, tile, HD), lambda i: (0, i, 0))
        attn_part = (ZS, rows, width)
        return call(
            functools.partial(project_back_body, rows=rows, more=more),
            (seq // tile,),
            [scalar(), heads, heads, heads, pl.BlockSpec((width, tile), lambda i: (0, i)), square, whole((width, 3 * HD))]
            + ([by(tile)] if more else []),
            [
                (pltpu.HBM(attn_part, BF), kept(attn_part)),
                (pltpu.HBM(attn_part, BF), kept(attn_part)),
                ((sds((seq, width), BF) if more else pltpu.HBM((seq, width), F32)), by(tile)),
                (sds((1, n_qkv), F32), kept((1, n_qkv))),
            ],
            scratch=[pltpu.VMEM((width, n_qkv), F32)],
            flops=4 * seq * width * n_qkv,
            moved=10e6,
        )(x_arr, *(far(v) if more else v for v in grads), far(normed_t), weights, far(wo), *((far(prev),) if more else ()))

    grads_y = attend_back(qkv_y, exp_y, inv_y, wide_y, gx_y.reshape(3, HD, seq), sds)
    ga_yo, ga_yx, first_part, qkv_sum_y = project_back(grads_y, w_y, wo_y, None)
    tile = block
    out_stays, out_tokens = call(
        output_body,
        (2,),
        [by(tile), by(tile), by(tile), vecs],
        [(sds((block, width), BF), kept((block, width)))] * 2,
        flops=1e6,
        moved=5e6,
    )(middle, ff, ff_mate, vec)
    gx_o, first_part, out_tokens = lax.optimization_barrier((gx_o, first_part, out_tokens))
    if fast:
        gx_o, ga_yx, got_hs, got_ds, gd_yo = lax.optimization_barrier((gx_o, ga_yx, got_hs, got_ds, gd_yo))
        got_do = to_y(gd_yo)
        ga_d = to_x(ga_yx)
    grads_o = attend_back(qkv_o, exp_o, inv_o, wide_o, gx_o.reshape(3, HD, seq), pltpu.HBM)
    if fast:
        *grads_o, got_do, ga_d, out_tokens = lax.optimization_barrier((*grads_o, got_do, ga_d, out_tokens))
        out_got = to_y(out_tokens)
        mlp_all = spread_z(jnp.concatenate([gh_oo + got_ho + got_hs, gd_oo + got_do + got_ds], axis=1))
        ga_s = to_y(ga_yo + ga_d)
    ga_oo, ga_ox, first, qkv_sum_o = project_back(grads_o, w_o, wo_o, first_part)
    if fast:
        ga_x = to_x(ga_ox)
        first, out_got = lax.optimization_barrier((first, out_got))
    first_mate = to_core(first)

    tile = TILE_FIRST
    hb_spec, qkv_spec = kept((1, hidden)), kept((1, n_qkv))
    small_o_shape, small_y_shape = (XS, ZS, KINDS, rows), (XS, ZS, 2 * KINDS, rows)
    in_stays, input_grad, small_o, small_y, first_sums = call(
        functools.partial(first_back_body, rows=rows),
        (seq // tile,),
        [scalar(), *start_blocks, row, vecs, by(tile), by_mate(tile), by(tile), vecs, hb_spec, hb_spec, qkv_spec, qkv_spec],
        [(sds((seq // 4, width), BF), kept((seq // 4, width)))] * 2
        + [
            (sds(small_o_shape, F32), kept(small_o_shape)),
            (sds(small_y_shape, F32), kept(small_y_shape)),
            (sds((KINDS, width), F32), vecs),
        ],
        flops=0,
        moved=0,
    )(x_arr, *tokens, te, vec, first, first_mate, far(grad_middle), second_sums, hb_o, hb_y, qkv_sum_o, qkv_sum_y)

    small_got = to_y(small_y)
    if fast:
        small_got, input_grad, ga_x, ga_s, mlp_all = lax.optimization_barrier(
            (small_got, input_grad, ga_x, ga_s, mlp_all)
        )
        ga_all = spread_z(ga_oo + ga_s + ga_x)
    small_sum = small_o + small_got[:, :, :KINDS]
    embed = first_sums[2]
    embed_got = jnp.where(xi == 0, small_got, small_got[::-1])[:, :, KINDS].transpose(1, 0, 2).reshape(width)
    embed_gradient = jnp.where(yi == 0, jnp.stack([embed, embed_got]), jnp.stack([embed_got, embed]))
    n_bias = query_bias.shape[0]
    n_head = query_weight.shape[1]
    if fast:
        small_sum = small_sum[0] + to_x(small_sum[1])
        zi = lax.axis_index("a")
        pieces = [lax.dynamic_index_in_dim(small_sum, (zi + k) % ZS, 0, keepdims=False) for k in range(ZS)]
        pieces = [lax.ppermute(v, "a", [(i, (i + k) % ZS) for i in range(ZS)]) if k else v for k, v in enumerate(pieces)]
        *weights, fg, fs, ob, sg, ss, db, hb, qb, vb = call(
            functools.partial(final_body, rows=rows),
            (1,),
            [kept(ga_all.shape)] + [kept((KINDS, rows))] * ZS,
            [(sds((shard, n_head), F32), kept((shard, n_head)))] * 3
            + [(sds((n_head, shard), F32), kept((n_head, shard)))]
            + [(sds((1, shard), F32), kept((1, shard)))] * 7
            + [(sds((1, n_bias), F32), kept((1, n_bias)))] * 2,
            flops=1e6,
            moved=2e6,
        )(ga_all, *pieces)
        vectors = [v[0] for v in (fg, fs, ob, sg, ss, db, hb, qb, vb)]
        mlp_sum = jnp.sum(mlp_all.astype(F32), axis=0)
        gh, gd = mlp_sum[:shard], mlp_sum[shard:].T
    else:

        def scatter(values):
            return lax.psum_scatter(values, ("a", "b"), scatter_dimension=0, tiled=True)

        def scatter_slow(oo, ox, yo, yx):
            own, oth = oo + to_y(yo), ox + to_y(yx)
            return scatter(jnp.stack([own, oth], axis=1).reshape(width, -1).astype(F32))

        kinds = small_sum.transpose(2, 1, 0, 3)
        bias = kinds[7].reshape(ZS * XS, rows)
        split = rows // 4
        vectors = [scatter(v) for v in kinds[:7].reshape(7, width)]
        vectors += [scatter(bias[:, k * split : k * split + split].reshape(-1)) for k in range(2)]
        gh = scatter_slow(gh_oo, gh_ox, gh_yo, gh_yx)
        gd = scatter_slow(gd_oo, gd_ox, gd_yo, gd_yx).T
        ga = scatter_slow(ga_oo, ga_ox, ga_yo, ga_yx)
        weights = [ga[:, k * n_head : k * n_head + n_head] for k in range(4)]
        weights[3] = weights[3].T

    def placed(stays, got):
        return jnp.where(yi == 0, jnp.stack([stays, got]), jnp.stack([got, stays]))

    if not fast:
        out_got = to_y(out_tokens)
    block_output = placed(out_stays, out_got)
    input_gradient = placed(in_stays, to_y(input_grad))

    fg, fs, ob, sg, ss, db, hb, qb, vb = vectors
    return (
        block_output, input_gradient, embed_gradient, fg, fs, weights[0], qb, weights[1], weights[2], vb,
        weights[3], ob, sg, ss, gh, hb, gd, db,
    )


def solution(mesh):
    dp, tensor = mesh.shape["dp"], mesh.shape["tensor"]
    fine = Mesh(mesh.devices.reshape(dp // 2, 2, tensor // 2, 2), ("a", "b", "y", "c"))
    by_dp, by_tensor = ("a", "b"), ("y", "c")
    both = by_tensor + by_dp
    column, matrix, turned = P(by_dp), P(by_dp, by_tensor), P(by_tensor, by_dp)
    seqs = P(by_dp, by_tensor, None)
    return jax.shard_map(
        functools.partial(body, dp == ZS * XS),
        mesh=fine,
        in_specs=(
            seqs, P(by_dp, None), column, column, matrix, P(both), matrix, matrix, P(both), turned,
            column, column, column, matrix, P(both), turned, column, seqs,
        ),
        out_specs=(
            seqs, seqs, P(by_dp, None), column, column, matrix, P(both), matrix, matrix, P(both), turned,
            column, column, column, matrix, P(both), turned, column,
        ),
        check_vma=False,
    )
```
